32 devices in a mesh: tract: 2 (over x), sky: 8 (over z, y), visit: 2 (over core).
Axes of the slice: x: 2, y: 2, z: 4, core: 2. Of those that a mesh axis runs over, the one named last changes fastest.
Arguments:
- warps: bfloat16 [16, 256, 4096], P(('tract', 'visit'), 'sky'), parts along dimension 0, may hold values from -6 to 6
- badbits: int32 [16, 256, 4096], P(('tract', 'visit'), 'sky'), parts along dimension 0, may hold values from 0 to 15
- coverage: int32 [16, 8], P(('tract', 'visit'), 'sky'), parts along dimension 0, may hold values from 0 to 1, as said below
- variance: float32 [16, 8], P(('tract', 'visit'), 'sky'), parts along dimension 0, may hold values from 0.05 to 5
- psf_index: int32 [16], P(('tract', 'visit')), parts along dimension 0, may hold values from 0 to 15
- psf_table: float32 [16, 8], replicated, may hold values from -2 to 2
- row_basis: bfloat16 [8, 21], replicated, may hold values from -1.25 to 1.25
- col_basis: bfloat16 [8, 21], replicated, may hold values from -1.25 to 1.25
Outputs:
- coadd: float32 [512, 4096], P(('tract', 'sky'), 'visit'), parts along dimension 0
- visit_chi: float32 [16], P(('tract', 'visit')), parts along dimension 0
The draws below stay inside these ranges and needn't reach their ends.
There are 2 independent parts, one for each index of `tract`. The reference program is written for one: setup_inputs(seed, part) draws one part's arguments, and reference() takes and returns one part's arrays. A program takes and returns all parts, laid end to end along the dimension named above; an argument that names none is the same for every part. Nothing has to cross between parts.
Inputs may be any that keep to these rules, and one draw needn't show every extreme that they name: `coverage`: each visit covers one run of 2 or more consecutive bands and no other; every band is covered by some visit.
All inputs are finite; a program needn't handle non-finite values.
Results may differ from the reference program's by a relative error of at most 0.0038.
Values may be sent and summed in bfloat16 or wider, within the bound.
No kernel may reach another device: no remote copies, remote signals or barrier semaphores. Data moves between devices by JAX's collectives and lax.ppermute only.
A program may use at most 64 MiB of HBM per device.

```python
import jax
import jax.numpy as jnp
from jax import lax

COLS = 4096
KW = 21
NB = 8
NTAB = 16
BAND_ROWS = 32
VISITS = 8
ROWS = 256
BANDS = 8


def draw_coverage(key, part):
    first_key, second_key, third_key = jax.random.split(jax.random.fold_in(key, 11), 3)
    shortest = BANDS // 4
    longer = (BANDS + 1) // 2
    start = jax.random.randint(first_key, (VISITS, 1), 0, BANDS - shortest + 1)
    extent = jax.random.randint(second_key, (VISITS, 1), shortest, BANDS - start + 1)
    edge_extent = jax.random.randint(third_key, (VISITS, 1), longer, BANDS + 1)
    visit_number = jnp.arange(VISITS)[:, None]
    first_visit = visit_number == 0
    last_visit = visit_number == VISITS - 1
    start = jnp.where(first_visit, 0, jnp.where(last_visit, BANDS - edge_extent, start))
    extent = jnp.where(first_visit | last_visit, edge_extent, extent)
    band = jnp.arange(BANDS)[None, :]
    return ((band >= start) & (band < start + extent)).astype(jnp.int32)


def draw_variance(key, part):
    first_key = jax.random.fold_in(jax.random.fold_in(key, 23), 0)
    band = jnp.arange(BANDS).astype(jnp.float32)[None, :]
    base = jnp.exp(jax.random.uniform(first_key, (VISITS, BANDS), jnp.float32, jnp.log(0.5), jnp.log(5.0)))
    tilt = 3.0 ** (-band / (BANDS - 1))
    return (base * tilt).astype(jnp.float32)


def plant(result, rng, low, high):
    longest = result.shape.index(max(result.shape))
    spots = []
    for shift in (0, 1):
        where = [jax.random.randint(jax.random.fold_in(rng, axis), (), 0, length) for axis, length in enumerate(result.shape)]
        where[longest] = (where[longest] + shift) % result.shape[longest]
        spots.append(tuple(where))
    return result.at[spots[0]].set(low).at[spots[1]].set(high)


def level_of(own_key, dims, shards, smallest, top_value):
    def one(axis_at, shards_of):
        heights = jax.random.uniform(jax.random.fold_in(jax.random.fold_in(own_key, 6), axis_at), (shards_of,), jnp.float32, smallest / len(shards), top_value / len(shards))
        return jnp.repeat(jnp.exp(heights), dims[axis_at] // shards_of).reshape((-1,) + (1,) * (len(dims) - axis_at - 1))

    gain = one(*shards[0])
    for cut in shards[1:]:
        gain = gain * one(*cut)
    return gain


def gaussian(stream_key, shape, deviation, limit, shards=(), held_as=jnp.bfloat16):
    values = jax.random.normal(stream_key, shape, jnp.float32) * deviation
    if len(shards) > 0:
        values = level_of(stream_key, shape, shards, -0.22, 0.18) * values
    return jnp.clip(values, min=-limit, max=limit).astype(held_as)


def setup_inputs(seed: int = 0, part: int = 0) -> dict:
    arg_keys = jax.random.split(jax.random.key(seed), 9)
    part_splits = jax.random.split(jax.random.fold_in(arg_keys[8], part), 9)
    warps = gaussian(part_splits[0], (VISITS, ROWS, COLS), 1.0, 6.0, ((0, 2), (1, 8)))
    badbits = plant(jax.random.randint(part_splits[1], (VISITS, ROWS, COLS), 0, 16), jax.random.fold_in(part_splits[1], 1), 0, 15).astype(jnp.int32)
    coverage = draw_coverage(jax.random.fold_in(jax.random.fold_in(arg_keys[8], part), 71), part)
    variance = draw_variance(jax.random.fold_in(jax.random.fold_in(arg_keys[8], part), 71), part)
    psf_index = plant(jax.random.randint(part_splits[4], (VISITS,), 0, NTAB), jax.random.fold_in(part_splits[4], 1), 0, NTAB - 1).astype(jnp.int32)
    psf_table = gaussian(arg_keys[5], (NTAB, NB), NB ** -0.5, 2.0, (), jnp.float32)
    row_basis = gaussian(arg_keys[6], (NB, KW), KW ** -0.5, 1.25)
    col_basis = gaussian(arg_keys[7], (NB, KW), KW ** -0.5, 1.25)
    return dict(warps=warps, badbits=badbits, coverage=coverage, variance=variance, psf_index=psf_index, psf_table=psf_table, row_basis=row_basis, col_basis=col_basis)


PRIOR_WEIGHT = 1.0
CLIP_LEVEL = 9.0
CHI_OFFSET = 0.5


def reference(warps, badbits, coverage, variance, psf_index, psf_table, row_basis, col_basis):
    half_width = KW // 2
    coefficients = psf_table[psf_index]
    column_profile = col_basis.astype(jnp.float32)
    row_profile = row_basis.astype(jnp.float32)

    def convolve(member):
        image, coefficient = member
        source = jnp.pad(image.astype(jnp.float32), ((0, 0), (half_width, half_width)))
        layers = jnp.zeros((NB, ROWS, COLS), jnp.float32)
        for tap in range(KW):
            layers = layers + column_profile[:, tap, None, None] * source[None, :, tap:tap + COLS]
        layers = lax.optimization_barrier(layers.astype(jnp.bfloat16)).astype(jnp.float32)
        padded = jnp.pad(layers, ((0, 0), (half_width, half_width), (0, 0)))
        rows_sum = jnp.zeros((NB, ROWS, COLS), jnp.float32)
        for tap in range(KW):
            rows_sum = rows_sum + row_profile[:, tap, None, None] * padded[:, tap:tap + ROWS, :]
        return jnp.sum(coefficient[:, None, None] * rows_sum, axis=0).astype(jnp.bfloat16)

    matched = lax.map(convolve, (warps, coefficients))
    values = matched.astype(jnp.float32)
    covered = jnp.repeat(coverage, BAND_ROWS, axis=1).astype(jnp.float32)
    spread_variance = jnp.repeat(variance, BAND_ROWS, axis=1)
    usable = covered[:, :, None] * (jnp.bitwise_and(badbits, 7) != 7).astype(jnp.float32)
    weight = usable / spread_variance[:, :, None]
    first = jnp.sum(weight * values, axis=0) / (jnp.sum(weight, axis=0) + PRIOR_WEIGHT)
    residual = values - first[None]
    squared = residual * residual
    visit_chi = jnp.sum(weight * squared, axis=(1, 2)) / jnp.sum(usable, axis=(1, 2))
    revised = weight / ((CHI_OFFSET + visit_chi)[:, None, None] * (1.0 + weight * squared / CLIP_LEVEL))
    coadd = jnp.sum(revised * values, axis=0) / (jnp.sum(revised, axis=0) + PRIOR_WEIGHT)
    return coadd, visit_chi
```

```python
import functools

import jax
import jax.numpy as jnp
import numpy as np
from jax import lax
from jax.experimental import pallas as pl
from jax.experimental.pallas import tpu as pltpu
from jax.sharding import PartitionSpec as P

PRIOR_WEIGHT = 1.0
CLIP_LEVEL = 9.0
CHI_OFFSET = 0.5
LANES = 128
SHIFT = LANES // 2
F32 = jnp.float32
BF16 = jnp.bfloat16


def whole(space=pltpu.VMEM):
    return pl.BlockSpec(memory_space=space)


def lane_index(shape):
    return lax.broadcasted_iota(jnp.int32, shape, len(shape) - 1)


def rotated(groups):
    turned = [pltpu.roll(group, SHIFT, 1) for group in groups]
    low = lane_index(groups[0].shape) < SHIFT
    return [jnp.where(low, turned[g - 1], turned[g]) for g in range(len(groups))]


def pack_kernel(half, select_ref, x_ref, up_ref, down_ref):
    columns = x_ref.shape[1]
    edge = up_ref.shape[0]
    step = 2 * LANES
    groups = []
    for start in range(0, columns, step):
        rows = jnp.dot(
            select_ref[...], x_ref[:, start : start + step], preferred_element_type=F32
        )
        groups += [rows[:, :LANES], rows[:, LANES:]]
    for g, group in enumerate(rotated(groups)):
        lanes = slice(g * LANES, (g + 1) * LANES)
        up_ref[:, lanes] = group[:edge].astype(BF16)
        down_ref[:, lanes] = group[edge:].astype(BF16)


def pack_rows(warps, half):
    visits, rows, columns = warps.shape
    edge = visits * half
    select = np.zeros((2 * edge, visits * rows), np.float32)
    for v in range(visits):
        for i in range(half):
            select[v * half + i, v * rows + rows - half + i] = 1
            select[edge + v * half + i, v * rows + i] = 1
    shape = jax.ShapeDtypeStruct((edge, columns), BF16)
    return pl.pallas_call(
        functools.partial(pack_kernel, half),
        out_shape=(shape, shape),
        in_specs=[whole(), whole()],
        out_specs=(whole(), whole()),
        name="pack",
    )(jnp.asarray(select, BF16), warps.reshape(visits * rows, columns))


def weight_kernel(visits, bands, side_ref, cover_ref, var_ref, send_bits, keep_bits, send_ref, keep_ref):
    rows = send_bits.shape[0] // visits
    high = rows // bands
    tile = (high, send_bits.shape[1])
    for v in range(visits):
        for b in range(bands):
            at = slice(v * rows + b * high, v * rows + (b + 1) * high)
            cover = jnp.full((8, LANES), cover_ref[v, b].astype(F32), F32)
            level = (cover / jnp.full((8, LANES), var_ref[v, b], F32))[:1, :1]
            level = jnp.broadcast_to(level, tile)
            for bits_ref, out_ref in ((send_bits, send_ref), (keep_bits, keep_ref)):
                usable = jnp.bitwise_and(bits_ref[at, :], 7) != 7
                out_ref[at, :] = jnp.where(usable, level, 0.0)


def pixel_weights(badbits, coverage, variance, side):
    visits, rows, columns = badbits.shape
    bits = badbits.reshape(visits * rows, columns)
    width = columns // 2
    tile = min(512, width)
    count = width // tile
    block = (visits * rows, tile)
    shape = jax.ShapeDtypeStruct((visits * rows, width), F32)
    spec = pl.BlockSpec(block, lambda i, s: (0, i))
    return pl.pallas_call(
        functools.partial(weight_kernel, visits, coverage.shape[1]),
        out_shape=(shape, shape),
        grid_spec=pltpu.PrefetchScalarGridSpec(
            num_scalar_prefetch=1,
            grid=(count,),
            in_specs=[
                whole(pltpu.SMEM),
                whole(pltpu.SMEM),
                pl.BlockSpec(block, lambda i, s: (0, (1 - s[0]) * count + i)),
                pl.BlockSpec(block, lambda i, s: (0, s[0] * count + i)),
            ],
            out_specs=(spec, spec),
        ),
        name="weights",
    )(side, coverage, variance, bits, bits)


def split(value):
    high = value.astype(BF16)
    return high, (value - high.astype(F32)).astype(BF16)


def table_kernel(visits, rows, half, index_ref, table_ref, row_ref, col_ref, column_out, own_out, edge_out):
    bases, taps = row_ref.shape
    outputs = visits * rows
    window = 2 * LANES
    k = lax.broadcasted_iota(jnp.int32, (window, LANES), 0)
    gap = k - lane_index((window, LANES)) - (SHIFT - half)
    for b in range(bases):
        band = jnp.zeros((window, LANES), F32)
        for t in range(taps):
            band = jnp.where(gap == t, col_ref[b, t], band)
        column_out[:, b * LANES : (b + 1) * LANES] = band.astype(BF16)
    out_row = lax.broadcasted_iota(jnp.int32, (rows, outputs), 0)
    lane = lane_index((rows, outputs))
    own_gap = lax.rem(lane, rows) - out_row + half
    member = lax.div(lane, rows)
    edge = visits * half
    source = lax.broadcasted_iota(jnp.int32, (2 * edge, outputs), 0)
    target = lane_index((2 * edge, outputs))
    i = lax.rem(source, half)
    line = lax.rem(target, rows)
    above = source < edge
    edge_gap = jnp.where(above, i - line, i + rows + half - line)
    same = lax.div(lax.rem(source, edge), half) == lax.div(target, rows)
    edge_gap = jnp.where(same, edge_gap, -1)
    owner = lax.div(target, rows)
    for b in range(bases):
        band = jnp.zeros((rows, outputs), F32)
        rim = jnp.zeros((2 * edge, outputs), F32)
        for t in range(taps):
            band = jnp.where(own_gap == t, row_ref[b, t], band)
            rim = jnp.where(edge_gap == t, row_ref[b, t], rim)
        scale = jnp.zeros((2 * edge, outputs), F32)
        for v in range(visits):
            factor = table_ref[index_ref[v], b]
            high, low = split(jnp.where(member == v, band * factor, 0.0))
            lanes = slice(b * outputs, (b + 1) * outputs)
            own_out[v * rows : (v + 1) * rows, lanes] = high
            own_out[outputs + v * rows : outputs + (v + 1) * rows, lanes] = low
            scale = jnp.where(owner == v, factor, scale)
        rim = rim * scale
        edge_out[b * 2 * edge : (b + 1) * 2 * edge, :] = rim


def turn_kernel(rim_ref, out_ref):
    count = rim_ref.shape[1]
    for start in range(0, rim_ref.shape[0], LANES):
        high, low = split(rim_ref[start : start + LANES, :].T)
        out_ref[:count, start : start + LANES] = high
        out_ref[count:, start : start + LANES] = low


def tables(psf_index, psf_table, row_basis, col_basis, visits, rows):
    bases, taps = row_basis.shape
    half = taps // 2
    outputs = visits * rows
    column, own, rim = pl.pallas_call(
        functools.partial(table_kernel, visits, rows, half),
        out_shape=(
            jax.ShapeDtypeStruct((2 * LANES, bases * LANES), BF16),
            jax.ShapeDtypeStruct((2 * outputs, bases * outputs), BF16),
            jax.ShapeDtypeStruct((bases * 2 * visits * half, outputs), F32),
        ),
        in_specs=[whole(pltpu.SMEM)] * 4,
        out_specs=(whole(),) * 3,
        name="tables",
    )(psf_index, psf_table, row_basis.astype(F32), col_basis.astype(F32))
    edge = pl.pallas_call(
        turn_kernel,
        out_shape=jax.ShapeDtypeStruct((2 * outputs, rim.shape[0]), BF16),
        in_specs=[whole()],
        out_specs=whole(),
        name="turn",
    )(rim)
    return column, own, edge


def convolve(window, column_ref, row_ref, step):
    bases = column_ref.shape[1] // LANES
    sides = []
    for n in range(2):
        layers = jnp.dot(window(2 * step + n), column_ref[...], preferred_element_type=F32)
        layers = layers.astype(BF16)
        sides.append(
            jnp.concatenate([layers[:, b * LANES : (b + 1) * LANES] for b in range(bases)], axis=0)
        )
    total = jnp.dot(row_ref[...], jnp.concatenate(sides, axis=1), preferred_element_type=F32)
    count = total.shape[0] // 2
    return total[:count] + total[count:]


def own_kernel(x_ref, column_ref, row_ref, out_ref, shifted):
    rows, columns = x_ref.shape
    groups = columns // LANES
    low = lane_index((rows, LANES)) < SHIFT

    def turn(g):
        return pltpu.roll(x_ref[:, g * LANES : (g + 1) * LANES].astype(F32), SHIFT, 1)

    before = jnp.zeros((rows, LANES), F32)
    for g in range(groups + 1):
        here = turn(g) if g < groups else jnp.zeros((rows, LANES), F32)
        shifted[:, g * LANES : (g + 1) * LANES] = jnp.where(low, before, here).astype(BF16)
        before = here

    def window(n):
        return shifted[:, pl.ds(pl.multiple_of(n * LANES, LANES), 2 * LANES)]

    def body(step, carry):
        at = pl.ds(pl.multiple_of(step * 2 * LANES, 2 * LANES), 2 * LANES)
        out_ref[:, at] = convolve(window, column_ref, row_ref, step)
        return carry

    lax.fori_loop(0, columns // (2 * LANES), body, 0)


def own_part(warps, column, own):
    visits, rows, columns = warps.shape
    count = visits * rows
    return pl.pallas_call(
        own_kernel,
        out_shape=jax.ShapeDtypeStruct((count, columns), F32),
        in_specs=[whole()] * 3,
        out_specs=whole(),
        scratch_shapes=[pltpu.VMEM((count, columns + LANES), BF16)],
        name="own_rows",
    )(warps.reshape(count, columns), column, own)


def edge_kernel(side_ref, up_ref, down_ref, column_ref, row_ref, part_ref, out_ref, shifted):
    edge, columns = up_ref.shape
    width = shifted.shape[1] - LANES
    groups = columns // LANES

    @pl.when(pl.program_id(0) == 0)
    def _():
        first = side_ref[0] * (width // LANES)
        lane = lane_index((2 * edge, LANES))
        for g in range(width // LANES + 1):
            at = first + g
            lanes = pl.ds(pl.multiple_of(lax.rem(at, groups) * LANES, LANES), LANES)
            value = jnp.concatenate(
                [up_ref[:, lanes].astype(F32), down_ref[:, lanes].astype(F32)], axis=0
            )
            bottom = jnp.where(at == 0, SHIFT, 0)
            top = jnp.where(at == groups, SHIFT, LANES)
            value = jnp.where((lane >= bottom) & (lane < top), value, 0.0)
            shifted[:, g * LANES : (g + 1) * LANES] = value.astype(BF16)

    start = pl.program_id(0) * (out_ref.shape[1] // LANES)

    def window(n):
        return shifted[:, pl.ds(pl.multiple_of((start + n) * LANES, LANES), 2 * LANES)]

    for step in range(out_ref.shape[1] // (2 * LANES)):
        at = slice(step * 2 * LANES, (step + 1) * 2 * LANES)
        total = convolve(window, column_ref, row_ref, step) + part_ref[:, at]
        out_ref[:, at] = total.astype(BF16)


def edge_part(side, up, down, column, edge, part):
    count, columns = part.shape
    width = columns // 2
    tile = min(512, width)
    steps = width // tile
    return pl.pallas_call(
        edge_kernel,
        out_shape=jax.ShapeDtypeStruct((count, width), BF16),
        grid_spec=pltpu.PrefetchScalarGridSpec(
            num_scalar_prefetch=1,
            grid=(steps,),
            in_specs=[whole()] * 4
            + [pl.BlockSpec((count, tile), lambda i, s: (0, s[0] * steps + i))],
            out_specs=pl.BlockSpec((count, tile), lambda i, s: (0, i)),
            scratch_shapes=[pltpu.VMEM((2 * up.shape[0], width + LANES), BF16)],
        ),
        name="edge_rows",
    )(side, up, down, column, edge, part)


def residual_kernel(visits, *refs):
    value_refs, weight_refs = refs[0:2], refs[2:4]
    factor_ref, sums_ref, chi_ref, count_ref = refs[4:]
    rows = value_refs[0].shape[0] // visits
    width = value_refs[0].shape[1]
    high = min(16, rows)

    @pl.when(pl.program_id(0) == 0)
    def _():
        chi_ref[...] = jnp.zeros_like(chi_ref)
        count_ref[...] = jnp.zeros_like(count_ref)

    def folded(value):
        total = value[:8]
        for start in range(8, high, 8):
            total = total + value[start : start + 8]
        return total

    members = [(side, v) for side in range(2) for v in range(visits)]
    for lane in range(0, width, LANES):
        for row in range(0, rows, high):
            lanes = slice(lane, lane + LANES)
            values, weights = [], []
            numer = denom = None
            for side, v in members:
                at = slice(v * rows + row, v * rows + row + high)
                value = value_refs[side][at, lanes].astype(F32)
                weight = weight_refs[side][at, lanes]
                values.append(value)
                weights.append(weight)
                numer = weight * value if numer is None else numer + weight * value
                denom = weight if denom is None else denom + weight
            first = numer / (denom + PRIOR_WEIGHT)
            for m, (side, v) in enumerate(members):
                residual = values[m] - first
                term = weights[m] * (residual * residual)
                at = slice(m * 8, (m + 1) * 8)
                chi_ref[at, :] += folded(term)
                count_ref[at, :] += folded(jnp.where(weights[m] > 0.0, 1.0, 0.0))
                target = slice(m * rows + row, m * rows + row + high)
                factor_ref[target, lanes] = weights[m] / (1.0 + term / CLIP_LEVEL)

    @pl.when(pl.program_id(0) == pl.num_programs(0) - 1)
    def _():
        count = len(members)
        for m in range(count):
            at = slice(m * 8, (m + 1) * 8)
            sums_ref[0, m : m + 1, :] = jnp.sum(chi_ref[at, :], axis=0, keepdims=True)
            sums_ref[1, m : m + 1, :] = jnp.sum(count_ref[at, :], axis=0, keepdims=True)


def residual_pass(values, weights, visits):
    count, width = values[0].shape
    tile = min(512, width)
    spec = pl.BlockSpec((count, tile), lambda i: (0, i))
    members = 2 * visits
    return pl.pallas_call(
        functools.partial(residual_kernel, visits),
        out_shape=(
            jax.ShapeDtypeStruct((2 * count, width), F32),
            jax.ShapeDtypeStruct((2, members, LANES), F32),
        ),
        grid=(width // tile,),
        in_specs=[spec] * 4,
        out_specs=(
            pl.BlockSpec((2 * count, tile), lambda i: (0, i)),
            pl.BlockSpec((2, members, LANES), lambda i: (0, 0, 0)),
        ),
        scratch_shapes=[pltpu.VMEM((members * 8, LANES), F32)] * 2,
        name="residual",
    )(*values, *weights)


def final_kernel(visits, sums_ref, own_ref, other_ref, factor_ref, out_ref, chi_ref):
    rows = own_ref.shape[0] // visits
    width = own_ref.shape[1]
    high = min(16, rows)
    chi = jnp.sum(sums_ref[0], axis=1, keepdims=True) / jnp.sum(
        sums_ref[1], axis=1, keepdims=True
    )
    scale = 1.0 / (CHI_OFFSET + chi)

    @pl.when(pl.program_id(0) == 0)
    def _():
        chi_ref[...] = jnp.broadcast_to(chi, chi_ref.shape)

    scales = [jnp.broadcast_to(scale[m : m + 1], (high, LANES)) for m in range(2 * visits)]
    for lane in range(0, width, LANES):
        for row in range(0, rows, high):
            lanes = slice(lane, lane + LANES)
            numer = denom = None
            for m in range(2 * visits):
                source = own_ref if m < visits else other_ref
                v = m % visits
                value = source[v * rows + row : v * rows + row + high, lanes].astype(F32)
                revised = factor_ref[m * rows + row : m * rows + row + high, lanes] * scales[m]
                numer = revised * value if numer is None else numer + revised * value
                denom = revised if denom is None else denom + revised
            out_ref[row : row + high, lanes] = numer / (denom + PRIOR_WEIGHT)


def final_pass(sums, values, factors, visits):
    count, width = values[0].shape
    rows = count // visits
    tile = min(512, width)
    spec = pl.BlockSpec((count, tile), lambda i: (0, i))
    members = 2 * visits
    return pl.pallas_call(
        functools.partial(final_kernel, visits),
        out_shape=(
            jax.ShapeDtypeStruct((rows, width), F32),
            jax.ShapeDtypeStruct((members, LANES), F32),
        ),
        grid=(width // tile,),
        in_specs=[
            pl.BlockSpec((2, members, LANES), lambda i: (0, 0, 0)),
            spec,
            spec,
            pl.BlockSpec((2 * count, tile), lambda i: (0, i)),
        ],
        out_specs=(
            pl.BlockSpec((rows, tile), lambda i: (0, i)),
            pl.BlockSpec((members, LANES), lambda i: (0, 0)),
        ),
        name="final",
    )(sums, *values, factors)


def per_device(warps, badbits, coverage, variance, psf_index, psf_table, row_basis, col_basis):
    visits, rows, columns = warps.shape
    half = row_basis.shape[1] // 2
    strips = lax.axis_size("sky")
    up = [(i, i + 1) for i in range(strips - 1)]
    down = [(j, i) for i, j in up]
    swap = [(0, 1), (1, 0)]
    side = lax.axis_index("visit").astype(jnp.int32).reshape(1)

    last, leading = pack_rows(warps, half)
    before = lax.ppermute(last, "sky", up)
    after = lax.ppermute(leading, "sky", down)
    send_weight, own_weight = pixel_weights(badbits, coverage, variance, side)
    other_weight = lax.ppermute(send_weight, "visit", swap)
    column, own, edge = tables(psf_index, psf_table, row_basis, col_basis, visits, rows)
    part = own_part(warps, column, own)
    send_value = edge_part(1 - side, before, after, column, edge, part)
    other_value = lax.ppermute(send_value, "visit", swap)
    own_value = edge_part(side, before, after, column, edge, part)
    values = (own_value, other_value)
    factors, sums = residual_pass(values, (own_weight, other_weight), visits)
    theirs = lax.ppermute(sums, "visit", swap)
    sums = sums + jnp.concatenate([theirs[:, visits:], theirs[:, :visits]], axis=1)
    step = 1
    while step < strips:
        sums = sums + lax.ppermute(sums, "sky", [(i, i ^ step) for i in range(strips)])
        step *= 2
    coadd, chi = final_pass(sums, values, factors, visits)
    return coadd, chi[:visits, 0]


def solution(mesh):
    placed = (
        P(("tract", "visit"), "sky", None),
        P(("tract", "visit"), "sky", None),
        P(("tract", "visit"), "sky"),
        P(("tract", "visit"), "sky"),
        P(("tract", "visit")),
        P(),
        P(),
        P(),
    )
    return jax.shard_map(
        per_device,
        mesh=mesh,
        in_specs=placed,
        out_specs=(P(("tract", "sky"), "visit"), P(("tract", "visit"))),
        check_vma=False,
    )
```

```python
import functools

import jax
import jax.numpy as jnp
import numpy as np
from jax import lax
from jax.experimental import pallas as pl
from jax.experimental.pallas import tpu as pltpu
from jax.sharding import PartitionSpec as P

PRIOR_WEIGHT = 1.0
CLIP_LEVEL = 9.0
CHI_OFFSET = 0.5
LANES = 128
SHIFT = LANES // 2
F32 = jnp.float32
BF16 = jnp.bfloat16


def whole(space=pltpu.VMEM):
    return pl.BlockSpec(memory_space=space)


def kept(*arrays):
    return [pltpu.with_memory_space_constraint(array, pltpu.VMEM) for array in arrays]


def held(shape, dtype):
    return pltpu.VMEM(shape, dtype)


LIMIT = pltpu.CompilerParams(vmem_limit_bytes=20 * 1024 * 1024)


def lane_index(shape):
    return lax.broadcasted_iota(jnp.int32, shape, len(shape) - 1)


def rotated(groups):
    turned = [pltpu.roll(group, SHIFT, 1) for group in groups]
    low = lane_index(groups[0].shape) < SHIFT
    return [jnp.where(low, turned[g - 1], turned[g]) for g in range(len(groups))]


def pack_kernel(select_ref, x_ref, up_ref, down_ref):
    columns = x_ref.shape[1]
    edge = up_ref.shape[0]
    step = 2 * LANES
    groups = []
    for start in range(0, columns, step):
        rows = jnp.dot(
            select_ref[...], x_ref[:, start : start + step], preferred_element_type=F32
        )
        groups += [rows[:, :LANES], rows[:, LANES:]]
    for g, group in enumerate(rotated(groups)):
        lanes = slice(g * LANES, (g + 1) * LANES)
        up_ref[:, lanes] = group[:edge].astype(BF16)
        down_ref[:, lanes] = group[edge:].astype(BF16)


def pack_rows(warps, half):
    visits, rows, columns = warps.shape
    edge = visits * half
    select = np.zeros((2 * edge, visits * rows), np.float32)
    for v in range(visits):
        for i in range(half):
            select[v * half + i, v * rows + rows - half + i] = 1
            select[edge + v * half + i, v * rows + i] = 1
    shape = held((edge, columns), BF16)
    return pl.pallas_call(
        pack_kernel,
        out_shape=(shape, shape),
        in_specs=[whole(), whole()],
        out_specs=(whole(), whole()),
        compiler_params=LIMIT,
        name="pack",
    )(jnp.asarray(select, BF16), *kept(warps.reshape(visits * rows, columns)))


def weight_kernel(visits, bands, side_ref, cover_ref, var_ref, bits_ref, send_ref, keep_ref):
    rows = bits_ref.shape[0] // visits
    high = rows // bands
    width = bits_ref.shape[1]
    tile = (high, width)
    count = send_ref.shape[1] // width
    step = pl.program_id(0)
    half = lax.div(step, count)
    lanes = pl.ds(pl.multiple_of(lax.rem(step, count) * width, width), width)

    def fill(out_ref):
        for v in range(visits):
            for b in range(bands):
                at = slice(v * rows + b * high, v * rows + (b + 1) * high)
                cover = jnp.full((8, LANES), cover_ref[b, v].astype(F32), F32)
                level = (cover / jnp.full((8, LANES), var_ref[b, v], F32))[:1, :1]
                usable = jnp.bitwise_and(bits_ref[at, :], 7) != 7
                out_ref[at, lanes] = jnp.where(usable, jnp.broadcast_to(level, tile), 0.0)

    pl.when(half == 0)(lambda: fill(send_ref))
    pl.when(half == 1)(lambda: fill(keep_ref))


def pixel_weights(badbits, coverage, variance, side):
    visits, rows, columns = badbits.shape
    bits = badbits.reshape(visits * rows, columns)
    width = columns // 2
    tile = min(512, width)
    count = width // tile
    shape = held((visits * rows, width), F32)

    def block(i, s):
        first = i < count
        return 0, jnp.where(first, (1 - s[0]) * count + i, s[0] * count + i - count)

    return pl.pallas_call(
        functools.partial(weight_kernel, visits, coverage.shape[1]),
        out_shape=(shape, shape),
        grid_spec=pltpu.PrefetchScalarGridSpec(
            num_scalar_prefetch=1,
            grid=(2 * count,),
            in_specs=[
                whole(pltpu.SMEM),
                whole(pltpu.SMEM),
                pl.BlockSpec((visits * rows, tile), block),
            ],
            out_specs=(whole(), whole()),
        ),
        compiler_params=LIMIT,
        name="weights",
    )(side, coverage.T, variance.T, bits)


def split(value):
    high = value.astype(BF16)
    return high, (value - high.astype(F32)).astype(BF16)


def padded_rows(half):
    return -(-2 * half // 8) * 8


def table_kernel(visits, rows, half, index_ref, table_ref, profile_ref, column_out, own_out, edge_out):
    bases = table_ref.shape[0]
    taps = 2 * half + 1
    window = 2 * LANES
    padded = padded_rows(half)

    def spread(line, shift, count):
        line = jnp.broadcast_to(line, (8, LANES))
        block = pltpu.roll(line, 0, 1, stride=1, stride_axis=0)
        blocks = [pltpu.roll(block, (shift + i) % LANES, 1) for i in range(0, count, 8)]
        return jnp.concatenate(blocks, axis=0)

    k = lax.broadcasted_iota(jnp.int32, (window, LANES), 0)
    gap = k - lane_index((window, LANES))
    inside = (gap >= 0) & (gap < LANES)
    for b in range(bases):
        line = profile_ref[bases + b : bases + b + 1, :]
        band = jnp.where(inside, spread(line, SHIFT - half, window), 0.0)
        column_out[:, b * LANES : (b + 1) * LANES] = band.astype(BF16)

    r = lax.broadcasted_iota(jnp.int32, (rows, LANES), 0)
    lane = lane_index((rows, LANES))
    tap = lane_index((1, LANES))

    def assemble(out_ref, high, valid, lines):
        groups = -(-bases * high // LANES)
        for g in range(groups):
            total = jnp.zeros((rows, LANES), F32)
            factors = [jnp.zeros((rows, LANES), F32) for _ in range(visits)]
            for b in range(bases):
                start = b * high - g * LANES
                if start >= LANES or start + high <= 0:
                    continue
                here = lane - start
                mask = (here >= 0) & (here < high)
                total = jnp.where(mask & valid(here), spread(lines(b), b * high, rows), total)
                for v in range(visits):
                    factors[v] = jnp.where(mask, table_ref[b, index_ref[v]], factors[v])
            wide = min(LANES, bases * high - g * LANES)
            lanes = slice(g * LANES, g * LANES + wide)
            for v in range(visits):
                top, low = split(total * factors[v])
                at = 2 * v * rows
                out_ref[at : at + rows, lanes] = top[:, :wide]
                out_ref[at + rows : at + 2 * rows, lanes] = low[:, :wide]

    def profile(b):
        return profile_ref[b : b + 1, :]

    def own_line(b):
        return pltpu.roll(profile(b), LANES - half, 1)

    def own_valid(e):
        return (e - r >= -half) & (e - r <= half)

    def edge_line(b):
        above = jnp.where(tap < half, profile(b), 0.0)
        below = jnp.where((tap > half) & (tap < taps), profile(b), 0.0)
        return above + pltpu.roll(below, LANES - rows, 1)

    def edge_valid(p):
        above = (p < half) & (p >= r)
        below = (p >= half) & (p < 2 * half) & (p - r <= 2 * half - rows)
        return above | below

    assemble(own_out, rows, own_valid, own_line)
    assemble(edge_out, padded, edge_valid, edge_line)


def tables(psf_index, psf_table, row_basis, col_basis, visits, rows):
    bases, taps = row_basis.shape
    half = taps // 2
    profile = jnp.concatenate([row_basis, col_basis[:, ::-1]], axis=0).astype(F32)
    profile = jnp.pad(profile, ((0, 0), (0, LANES - taps)))
    return pl.pallas_call(
        functools.partial(table_kernel, visits, rows, half),
        out_shape=(
            held((2 * LANES, bases * LANES), BF16),
            held((2 * visits * rows, bases * rows), BF16),
            held((2 * visits * rows, bases * padded_rows(half)), BF16),
        ),
        in_specs=[whole(pltpu.SMEM), whole(pltpu.SMEM), whole()],
        out_specs=(whole(),) * 3,
        compiler_params=LIMIT,
        name="tables",
    )(psf_index, psf_table.T, profile)


def convolve(windows, column_ref, row_ref, visits):
    bases = column_ref.shape[1] // LANES
    count = windows[0].shape[0]
    rows = count // visits
    layers = jnp.dot(
        jnp.concatenate(windows, axis=0), column_ref[...], preferred_element_type=F32
    )
    high = row_ref.shape[0] // (2 * visits)
    totals = []
    for v in range(visits):
        sides = []
        for n in range(len(windows)):
            at = n * count + v * rows
            part = [layers[at : at + rows, b * LANES : (b + 1) * LANES] for b in range(bases)]
            sides.append(jnp.concatenate(part, axis=0).astype(BF16))
        total = jnp.dot(
            row_ref[2 * v * high : 2 * (v + 1) * high, :],
            jnp.concatenate(sides, axis=1),
            preferred_element_type=F32,
        )
        totals.append(total[:high] + total[high:])
    return totals


def own_kernel(visits, x_ref, column_ref, row_ref, out_ref, shifted):
    count, columns = x_ref.shape
    rows = count // visits
    groups = columns // LANES
    low = lane_index((count, LANES)) < SHIFT

    def turn(g):
        return pltpu.roll(x_ref[:, g * LANES : (g + 1) * LANES].astype(F32), SHIFT, 1)

    before = jnp.zeros((count, LANES), F32)
    for g in range(groups + 1):
        here = turn(g) if g < groups else jnp.zeros((count, LANES), F32)
        shifted[:, g * LANES : (g + 1) * LANES] = jnp.where(low, before, here).astype(BF16)
        before = here

    def window(n):
        return shifted[:, pl.ds(pl.multiple_of(n * LANES, LANES), 2 * LANES)]

    def body(step, carry):
        at = pl.ds(pl.multiple_of(step * 2 * LANES, 2 * LANES), 2 * LANES)
        windows = [window(2 * step), window(2 * step + 1)]
        for v, total in enumerate(convolve(windows, column_ref, row_ref, visits)):
            out_ref[v * rows : (v + 1) * rows, at] = total
        return carry

    lax.fori_loop(0, columns // (2 * LANES), body, 0)


def own_part(warps, column, own):
    visits, rows, columns = warps.shape
    count = visits * rows
    return pl.pallas_call(
        functools.partial(own_kernel, visits),
        out_shape=held((count, columns), F32),
        in_specs=[whole()] * 3,
        out_specs=whole(),
        scratch_shapes=[pltpu.VMEM((count, columns + LANES), BF16)],
        compiler_params=LIMIT,
        cost_estimate=pl.CostEstimate(flops=10**9, bytes_accessed=10**7, transcendentals=0),
        name="own_rows",
    )(*kept(warps.reshape(count, columns), column, own))


def edge_kernel(visits, side_ref, select_ref, up_ref, down_ref, column_ref, row_ref, part_ref, out_ref, shifted):
    columns = up_ref.shape[1]
    rows = out_ref.shape[0] // visits
    width = out_ref.shape[1]
    groups = columns // LANES
    base = side_ref[0] * (width // LANES)
    count = shifted.shape[0]
    lane = lane_index((count, LANES))
    for g in range(width // LANES + 1):
        at = base + g
        lanes = pl.ds(pl.multiple_of(lax.rem(at, groups) * LANES, LANES), LANES)
        value = jnp.dot(select_ref[0], up_ref[:, lanes], preferred_element_type=F32)
        value += jnp.dot(select_ref[1], down_ref[:, lanes], preferred_element_type=F32)
        if g == 0:
            value = jnp.where(lane >= jnp.where(at == 0, SHIFT, 0), value, 0.0)
        if g == width // LANES:
            value = jnp.where(lane < jnp.where(at == groups, SHIFT, LANES), value, 0.0)
        shifted[:, g * LANES : (g + 1) * LANES] = value.astype(BF16)

    def window(n):
        return shifted[:, pl.ds(pl.multiple_of(n * LANES, LANES), 2 * LANES)]

    def body(step, carry):
        start = pl.multiple_of(step * 2 * LANES, 2 * LANES)
        at = pl.ds(start, 2 * LANES)
        source = pl.ds(pl.multiple_of(side_ref[0] * width + start, 2 * LANES), 2 * LANES)
        windows = [window(2 * step), window(2 * step + 1)]
        for v, total in enumerate(convolve(windows, column_ref, row_ref, visits)):
            lines = slice(v * rows, (v + 1) * rows)
            out_ref[lines, at] = (total + part_ref[lines, source]).astype(BF16)
        return carry

    lax.fori_loop(0, width // (2 * LANES), body, 0)


def edge_part(side, up, down, column, edge, part, visits, half):
    count, columns = part.shape
    width = columns // 2
    padded = padded_rows(half)
    select = np.zeros((2, visits * padded, visits * half), np.float32)
    for v in range(visits):
        for i in range(half):
            select[0, v * padded + i, v * half + i] = 1
            select[1, v * padded + half + i, v * half + i] = 1
    return pl.pallas_call(
        functools.partial(edge_kernel, visits),
        out_shape=held((count, width), BF16),
        in_specs=[whole(pltpu.SMEM)] + [whole()] * 6,
        out_specs=whole(),
        scratch_shapes=[pltpu.VMEM((visits * padded, width + LANES), BF16)],
        compiler_params=LIMIT,
        name="edge_rows",
    )(side, jnp.asarray(select, BF16), *kept(up, down, column, edge, part))


def residual_kernel(visits, *refs):
    value_refs, weight_refs = refs[0:2], refs[2:4]
    factor_ref, sums_ref, chi_ref, count_ref = refs[4:]
    rows = value_refs[0].shape[0] // visits
    width = value_refs[0].shape[1]
    high = min(16, rows)
    chi_ref[...] = jnp.zeros_like(chi_ref)
    count_ref[...] = jnp.zeros_like(count_ref)

    def folded(value):
        total = value[:8]
        for start in range(8, high, 8):
            total = total + value[start : start + 8]
        return total

    members = [(side, v) for side in range(2) for v in range(visits)]

    def body(step, carry):
        lanes = pl.ds(pl.multiple_of(step * LANES, LANES), LANES)
        for row in range(0, rows, high):
            values, weights = [], []
            numer = denom = None
            for side, v in members:
                at = slice(v * rows + row, v * rows + row + high)
                value = value_refs[side][at, lanes].astype(F32)
                weight = weight_refs[side][at, lanes]
                values.append(value)
                weights.append(weight)
                numer = weight * value if numer is None else numer + weight * value
                denom = weight if denom is None else denom + weight
            first = numer / (denom + PRIOR_WEIGHT)
            for m, (side, v) in enumerate(members):
                residual = values[m] - first
                term = weights[m] * (residual * residual)
                at = slice(m * 8, (m + 1) * 8)
                chi_ref[at, :] += folded(term)
                count_ref[at, :] += folded(jnp.where(weights[m] > 0.0, 1.0, 0.0))
                target = slice(m * rows + row, m * rows + row + high)
                factor_ref[target, lanes] = weights[m] / (1.0 + term / CLIP_LEVEL)
        return carry

    lax.fori_loop(0, width // LANES, body, 0)
    for m in range(len(members)):
        at = slice(m * 8, (m + 1) * 8)
        sums_ref[0, m : m + 1, :] = jnp.sum(chi_ref[at, :], axis=0, keepdims=True)
        sums_ref[1, m : m + 1, :] = jnp.sum(count_ref[at, :], axis=0, keepdims=True)


def residual_pass(values, weights, visits):
    count, width = values[0].shape
    members = 2 * visits
    return pl.pallas_call(
        functools.partial(residual_kernel, visits),
        out_shape=(held((2 * count, width), F32), held((2, members, LANES), F32)),
        in_specs=[whole()] * 4,
        out_specs=(whole(), whole()),
        scratch_shapes=[pltpu.VMEM((members * 8, LANES), F32)] * 2,
        compiler_params=LIMIT,
        name="residual",
    )(*kept(*values, *weights))


def final_kernel(visits, sums_ref, own_ref, other_ref, factor_ref, out_ref, chi_ref):
    rows = own_ref.shape[0] // visits
    width = out_ref.shape[1]
    high = min(16, rows)
    start = pl.program_id(0) * width
    chi = jnp.sum(sums_ref[0], axis=1, keepdims=True) / jnp.sum(
        sums_ref[1], axis=1, keepdims=True
    )
    scale = 1.0 / (CHI_OFFSET + chi)

    @pl.when(pl.program_id(0) == 0)
    def _():
        for v in range(visits):
            chi_ref[v] = chi[v, 0]

    scales = [jnp.broadcast_to(scale[m : m + 1], (high, LANES)) for m in range(2 * visits)]
    for lane in range(0, width, LANES):
        lanes = pl.ds(pl.multiple_of(start + lane, LANES), LANES)
        for row in range(0, rows, high):
            numer = denom = None
            for m in range(2 * visits):
                source = own_ref if m < visits else other_ref
                v = m % visits
                value = source[v * rows + row : v * rows + row + high, lanes].astype(F32)
                revised = factor_ref[m * rows + row : m * rows + row + high, lanes] * scales[m]
                numer = revised * value if numer is None else numer + revised * value
                denom = revised if denom is None else denom + revised
            out_ref[row : row + high, lane : lane + LANES] = numer / (denom + PRIOR_WEIGHT)


def final_pass(sums, values, factors, visits):
    count, width = values[0].shape
    rows = count // visits
    tile = min(512, width)
    return pl.pallas_call(
        functools.partial(final_kernel, visits),
        out_shape=(
            jax.ShapeDtypeStruct((rows, width), F32),
            jax.ShapeDtypeStruct((visits,), F32),
        ),
        grid=(width // tile,),
        in_specs=[whole()] * 4,
        out_specs=(pl.BlockSpec((rows, tile), lambda i: (0, i)), whole(pltpu.SMEM)),
        compiler_params=LIMIT,
        name="final",
    )(*kept(sums, *values, factors))


def per_device(warps, badbits, coverage, variance, psf_index, psf_table, row_basis, col_basis):
    visits, rows, _ = warps.shape
    half = row_basis.shape[1] // 2
    strips = lax.axis_size("sky")
    up = [(i, i + 1) for i in range(strips - 1)]
    down = [(j, i) for i, j in up]
    swap = [(0, 1), (1, 0)]
    side = lax.axis_index("visit").astype(jnp.int32).reshape(1)

    last, leading = pack_rows(warps, half)
    before = lax.ppermute(last, "sky", up)
    after = lax.ppermute(leading, "sky", down)
    send_weight, own_weight = pixel_weights(badbits, coverage, variance, side)
    other_weight = lax.ppermute(send_weight, "visit", swap)
    column, own, edge = tables(psf_index, psf_table, row_basis, col_basis, visits, rows)
    part = own_part(warps, column, own)
    send_value = edge_part(
        1 - side, before, after, column, edge, part, visits, half
    )
    other_value = lax.ppermute(send_value, "visit", swap)
    own_value = edge_part(side, before, after, column, edge, part, visits, half)
    values = (own_value, other_value)
    factors, sums = residual_pass(values, (own_weight, other_weight), visits)
    theirs = lax.ppermute(sums, "visit", swap)
    sums = sums + jnp.concatenate([theirs[:, visits:], theirs[:, :visits]], axis=1)
    step = 1
    while step < strips:
        sums = sums + lax.ppermute(sums, "sky", [(i, i ^ step) for i in range(strips)])
        step *= 2
    return final_pass(sums, values, factors, visits)


def solution(mesh):
    placed = (
        P(("tract", "visit"), "sky", None),
        P(("tract", "visit"), "sky", None),
        P(("tract", "visit"), "sky"),
        P(("tract", "visit"), "sky"),
        P(("tract", "visit")),
        P(),
        P(),
        P(),
    )
    return jax.shard_map(
        per_device,
        mesh=mesh,
        in_specs=placed,
        out_specs=(P(("tract", "sky"), "visit"), P(("tract", "visit"))),
        check_vma=False,
    )
```

```python
import functools

import jax
import jax.numpy as jnp
import numpy as np
from jax import lax
from jax.experimental import pallas as pl
from jax.experimental.pallas import tpu as pltpu
from jax.sharding import PartitionSpec as P

PRIOR_WEIGHT = 1.0
CLIP_LEVEL = 9.0
CHI_OFFSET = 0.5
LANES = 128
SHIFT = LANES // 2
F32 = jnp.float32
BF16 = jnp.bfloat16


def whole(space=pltpu.VMEM):
    return pl.BlockSpec(memory_space=space)


def kept(*arrays):
    return [pltpu.with_memory_space_constraint(array, pltpu.VMEM) for array in arrays]


def away(*arrays):
    return [pltpu.with_memory_space_constraint(array, pltpu.HBM) for array in arrays]


def held(shape, dtype):
    return pltpu.VMEM(shape, dtype)


LIMIT = pltpu.CompilerParams(vmem_limit_bytes=20 * 1024 * 1024)


def lane_index(shape):
    return lax.broadcasted_iota(jnp.int32, shape, len(shape) - 1)


def pack_kernel(visits, half, x_ref, up_ref, down_ref, rows_ref, arrived):
    count, columns = x_ref.shape
    rows = count // visits
    edge = up_ref.shape[0]
    chunks = arrived.shape[0]
    width = columns // chunks
    copies = []
    for c in range(chunks):
        lanes = slice(c * width, (c + 1) * width)
        copies.append(
            pltpu.make_async_copy(x_ref.at[:, lanes], rows_ref.at[:, lanes], arrived.at[c])
        )
        copies[c].start()
    target = lax.broadcasted_iota(jnp.int32, (2 * edge, count), 0)
    source = lane_index((2 * edge, count))
    within = lax.rem(target, edge)
    line = lax.div(within, half) * rows + lax.rem(within, half)
    line = line + jnp.where(target < edge, rows - half, 0)
    select = jnp.where(source == line, 1.0, 0.0).astype(BF16)
    low = lane_index((2 * edge, LANES)) < SHIFT
    step = 2 * LANES

    def put(g, value):
        lanes = slice(g * LANES, (g + 1) * LANES)
        up_ref[:, lanes] = value[:edge].astype(BF16)
        down_ref[:, lanes] = value[edge:].astype(BF16)

    before = opening = None
    for start in range(0, columns, step):
        if start % width == 0:
            copies[start // width].wait()
        found = jnp.dot(select, rows_ref[:, start : start + step], preferred_element_type=F32)
        for part in range(2):
            here = pltpu.roll(found[:, part * LANES : (part + 1) * LANES], SHIFT, 1)
            if before is None:
                opening = here
            else:
                put(start // LANES + part, jnp.where(low, before, here))
            before = here
    put(0, jnp.where(low, before, opening))


def pack_rows(warps, half):
    visits, rows, columns = warps.shape
    count = visits * rows
    shape = held((visits * half, columns), BF16)
    chunks = max(1, columns // 1024)
    (image,) = away(warps.reshape(count, columns))
    return pl.pallas_call(
        functools.partial(pack_kernel, visits, half),
        out_shape=(shape, shape, held((count, columns), BF16)),
        in_specs=[pl.BlockSpec(memory_space=pl.ANY)],
        out_specs=(whole(),) * 3,
        scratch_shapes=[pltpu.SemaphoreType.DMA((chunks,))],
        compiler_params=LIMIT,
        name="pack",
    )(image)


def weight_kernel(visits, bands, side_ref, cover_ref, var_ref, bits_ref, send_ref, keep_ref):
    rows = bits_ref.shape[0] // visits
    high = rows // bands
    width = bits_ref.shape[1]
    tile = (high, width)
    count = send_ref.shape[1] // width
    step = pl.program_id(0)
    half = lax.div(step, count)
    lanes = pl.ds(pl.multiple_of(lax.rem(step, count) * width, width), width)

    def fill(out_ref):
        for v in range(visits):
            for b in range(bands):
                at = slice(v * rows + b * high, v * rows + (b + 1) * high)
                cover = jnp.full((8, LANES), cover_ref[b, v].astype(F32), F32)
                level = (cover / jnp.full((8, LANES), var_ref[b, v], F32))[:1, :1]
                usable = jnp.bitwise_and(bits_ref[at, :], 7) != 7
                out_ref[at, lanes] = jnp.where(usable, jnp.broadcast_to(level, tile), 0.0)

    pl.when(half == 0)(lambda: fill(send_ref))
    pl.when(half == 1)(lambda: fill(keep_ref))


def pixel_weights(badbits, coverage, variance, side):
    visits, rows, columns = badbits.shape
    (bits,) = away(badbits.reshape(visits * rows, columns))
    width = columns // 2
    tile = min(512, width)
    count = width // tile
    shape = held((visits * rows, width), F32)

    def block(i, s):
        first = i < count
        return 0, jnp.where(first, (1 - s[0]) * count + i, s[0] * count + i - count)

    return pl.pallas_call(
        functools.partial(weight_kernel, visits, coverage.shape[1]),
        out_shape=(shape, shape),
        grid_spec=pltpu.PrefetchScalarGridSpec(
            num_scalar_prefetch=1,
            grid=(2 * count,),
            in_specs=[
                whole(pltpu.SMEM),
                whole(pltpu.SMEM),
                pl.BlockSpec((visits * rows, tile), block),
            ],
            out_specs=(whole(), whole()),
        ),
        compiler_params=LIMIT,
        name="weights",
    )(side, *away(coverage.T, variance.T), bits)


def split(value):
    high = value.astype(BF16)
    return high, (value - high.astype(F32)).astype(BF16)


def padded_rows(half):
    return -(-2 * half // 8) * 8


def table_kernel(visits, rows, half, index_ref, table_ref, profile_ref, column_out, own_out, edge_out):
    bases = table_ref.shape[0]
    taps = 2 * half + 1
    window = 2 * LANES
    padded = padded_rows(half)

    def spread(line, shift, count):
        line = jnp.broadcast_to(line, (8, LANES))
        block = pltpu.roll(line, 0, 1, stride=1, stride_axis=0)
        blocks = [pltpu.roll(block, (shift + i) % LANES, 1) for i in range(0, count, 8)]
        return jnp.concatenate(blocks, axis=0)

    k = lax.broadcasted_iota(jnp.int32, (window, LANES), 0)
    gap = k - lane_index((window, LANES))
    inside = (gap >= 0) & (gap < LANES)
    for b in range(bases):
        line = profile_ref[bases + b : bases + b + 1, :]
        band = jnp.where(inside, spread(line, SHIFT - half, window), 0.0)
        column_out[:, b * LANES : (b + 1) * LANES] = band.astype(BF16)

    r = lax.broadcasted_iota(jnp.int32, (rows, LANES), 0)
    lane = lane_index((rows, LANES))
    tap = lane_index((1, LANES))

    def assemble(out_ref, high, valid, lines):
        groups = -(-bases * high // LANES)
        for g in range(groups):
            total = jnp.zeros((rows, LANES), F32)
            factors = [jnp.zeros((rows, LANES), F32) for _ in range(visits)]
            for b in range(bases):
                start = b * high - g * LANES
                if start >= LANES or start + high <= 0:
                    continue
                here = lane - start
                mask = (here >= 0) & (here < high)
                total = jnp.where(mask & valid(here), spread(lines(b), b * high, rows), total)
                for v in range(visits):
                    factors[v] = jnp.where(mask, table_ref[b, index_ref[v]], factors[v])
            wide = min(LANES, bases * high - g * LANES)
            lanes = slice(g * LANES, g * LANES + wide)
            for v in range(visits):
                top, low = split(total * factors[v])
                at = 2 * v * rows
                out_ref[at : at + rows, lanes] = top[:, :wide]
                out_ref[at + rows : at + 2 * rows, lanes] = low[:, :wide]

    def profile(b):
        return profile_ref[b : b + 1, :]

    def own_line(b):
        return pltpu.roll(profile(b), LANES - half, 1)

    def own_valid(e):
        return (e - r >= -half) & (e - r <= half)

    def edge_line(b):
        above = jnp.where(tap < half, profile(b), 0.0)
        below = jnp.where((tap > half) & (tap < taps), profile(b), 0.0)
        return above + pltpu.roll(below, LANES - rows, 1)

    def edge_valid(p):
        above = (p < half) & (p >= r)
        below = (p >= half) & (p < 2 * half) & (p - r <= 2 * half - rows)
        return above | below

    assemble(own_out, rows, own_valid, own_line)
    assemble(edge_out, padded, edge_valid, edge_line)


def tables(psf_index, psf_table, row_basis, col_basis, visits, rows):
    bases, taps = row_basis.shape
    half = taps // 2
    profile = jnp.concatenate([row_basis, col_basis[:, ::-1]], axis=0).astype(F32)
    profile = jnp.pad(profile, ((0, 0), (0, LANES - taps)))
    return pl.pallas_call(
        functools.partial(table_kernel, visits, rows, half),
        out_shape=(
            held((2 * LANES, bases * LANES), BF16),
            held((2 * visits * rows, bases * rows), BF16),
            held((2 * visits * rows, bases * padded_rows(half)), BF16),
        ),
        in_specs=[whole(pltpu.SMEM), whole(pltpu.SMEM), whole()],
        out_specs=(whole(),) * 3,
        compiler_params=LIMIT,
        name="tables",
    )(psf_index, psf_table.T, profile)


def convolve(windows, column_ref, row_ref, visits):
    bases = column_ref.shape[1] // LANES
    count = windows[0].shape[0]
    rows = count // visits
    layers = jnp.dot(
        jnp.concatenate(windows, axis=0), column_ref[...], preferred_element_type=F32
    )
    high = row_ref.shape[0] // (2 * visits)
    totals = []
    for v in range(visits):
        sides = []
        for n in range(len(windows)):
            at = n * count + v * rows
            part = [layers[at : at + rows, b * LANES : (b + 1) * LANES] for b in range(bases)]
            sides.append(jnp.concatenate(part, axis=0).astype(BF16))
        total = jnp.dot(
            row_ref[2 * v * high : 2 * (v + 1) * high, :],
            jnp.concatenate(sides, axis=1),
            preferred_element_type=F32,
        )
        totals.append(total[:high] + total[high:])
    return totals


def own_kernel(visits, x_ref, column_ref, row_ref, out_ref, shifted):
    count, columns = x_ref.shape
    rows = count // visits
    groups = columns // LANES
    low = lane_index((count, LANES)) < SHIFT

    def turn(g):
        return pltpu.roll(x_ref[:, g * LANES : (g + 1) * LANES].astype(F32), SHIFT, 1)

    before = jnp.zeros((count, LANES), F32)
    for g in range(groups + 1):
        here = turn(g) if g < groups else jnp.zeros((count, LANES), F32)
        shifted[:, g * LANES : (g + 1) * LANES] = jnp.where(low, before, here).astype(BF16)
        before = here

    def window(n):
        return shifted[:, pl.ds(pl.multiple_of(n * LANES, LANES), 2 * LANES)]

    def body(step, carry):
        at = pl.ds(pl.multiple_of(step * 2 * LANES, 2 * LANES), 2 * LANES)
        windows = [window(2 * step), window(2 * step + 1)]
        for v, total in enumerate(convolve(windows, column_ref, row_ref, visits)):
            out_ref[v * rows : (v + 1) * rows, at] = total
        return carry

    lax.fori_loop(0, columns // (2 * LANES), body, 0, unroll=8)


def own_part(image, column, own, visits):
    count, columns = image.shape
    return pl.pallas_call(
        functools.partial(own_kernel, visits),
        out_shape=held((count, columns), F32),
        in_specs=[whole()] * 3,
        out_specs=whole(),
        scratch_shapes=[pltpu.VMEM((count, columns + LANES), BF16)],
        compiler_params=LIMIT,
        cost_estimate=pl.CostEstimate(flops=10**9, bytes_accessed=10**7, transcendentals=0),
        name="own_rows",
    )(*kept(image, column, own))


def edge_kernel(visits, side_ref, select_ref, up_ref, down_ref, column_ref, row_ref, part_ref, *refs):
    if len(refs) > 2:
        far_ref, out_ref, near_ref, shifted, arrived = refs
        fetch = pltpu.make_async_copy(far_ref, near_ref, arrived)
        fetch.start()
    else:
        fetch = None
        out_ref, shifted = refs
    columns = up_ref.shape[1]
    rows = out_ref.shape[0] // visits
    width = out_ref.shape[1]
    groups = columns // LANES
    base = side_ref[0] * (width // LANES)
    count = shifted.shape[0]
    lane = lane_index((count, LANES))
    for g in range(width // LANES + 1):
        at = base + g
        lanes = pl.ds(pl.multiple_of(lax.rem(at, groups) * LANES, LANES), LANES)
        value = jnp.dot(select_ref[0], up_ref[:, lanes], preferred_element_type=F32)
        value += jnp.dot(select_ref[1], down_ref[:, lanes], preferred_element_type=F32)
        if g == 0:
            value = jnp.where(lane >= jnp.where(at == 0, SHIFT, 0), value, 0.0)
        if g == width // LANES:
            value = jnp.where(lane < jnp.where(at == groups, SHIFT, LANES), value, 0.0)
        shifted[:, g * LANES : (g + 1) * LANES] = value.astype(BF16)

    def window(n):
        return shifted[:, pl.ds(pl.multiple_of(n * LANES, LANES), 2 * LANES)]

    def body(step, carry):
        start = pl.multiple_of(step * 2 * LANES, 2 * LANES)
        at = pl.ds(start, 2 * LANES)
        source = pl.ds(pl.multiple_of(side_ref[0] * width + start, 2 * LANES), 2 * LANES)
        windows = [window(2 * step), window(2 * step + 1)]
        for v, total in enumerate(convolve(windows, column_ref, row_ref, visits)):
            lines = slice(v * rows, (v + 1) * rows)
            out_ref[lines, at] = (total + part_ref[lines, source]).astype(BF16)
        return carry

    lax.fori_loop(0, width // (2 * LANES), body, 0, unroll=8)
    if fetch is not None:
        fetch.wait()


def edge_part(side, up, down, column, edge, part, visits, half, *far):
    count, columns = part.shape
    width = columns // 2
    padded = padded_rows(half)
    select = np.zeros((2, visits * padded, visits * half), np.float32)
    for v in range(visits):
        for i in range(half):
            select[0, v * padded + i, v * half + i] = 1
            select[1, v * padded + half + i, v * half + i] = 1
    return pl.pallas_call(
        functools.partial(edge_kernel, visits),
        out_shape=[held((count, width), BF16)] + [held(a.shape, a.dtype) for a in far],
        in_specs=[whole(pltpu.SMEM)]
        + [whole()] * 6
        + [pl.BlockSpec(memory_space=pl.ANY)] * len(far),
        out_specs=[whole()] * (1 + len(far)),
        scratch_shapes=[pltpu.VMEM((visits * padded, width + LANES), BF16)]
        + [pltpu.SemaphoreType.DMA(())] * len(far),
        compiler_params=LIMIT,
        name="edge_rows",
    )(side, jnp.asarray(select, BF16), *kept(up, down, column, edge, part), *away(*far))


def residual_kernel(visits, *refs):
    value_refs, weight_refs = refs[0:2], refs[2:4]
    factor_ref, sums_ref, chi_ref, count_ref = refs[4:]
    rows = value_refs[0].shape[0] // visits
    width = value_refs[0].shape[1]
    high = min(16, rows)
    chi_ref[...] = jnp.zeros_like(chi_ref)
    count_ref[...] = jnp.zeros_like(count_ref)

    def folded(value):
        total = value[:8]
        for start in range(8, high, 8):
            total = total + value[start : start + 8]
        return total

    members = [(side, v) for side in range(2) for v in range(visits)]

    def body(step, carry):
        lanes = pl.ds(pl.multiple_of(step * LANES, LANES), LANES)
        for row in range(0, rows, high):
            values, weights = [], []
            numer = denom = None
            for side, v in members:
                at = slice(v * rows + row, v * rows + row + high)
                value = value_refs[side][at, lanes].astype(F32)
                weight = weight_refs[side][at, lanes]
                values.append(value)
                weights.append(weight)
                numer = weight * value if numer is None else numer + weight * value
                denom = weight if denom is None else denom + weight
            first = numer / (denom + PRIOR_WEIGHT)
            for m, (side, v) in enumerate(members):
                residual = values[m] - first
                term = weights[m] * (residual * residual)
                at = slice(m * 8, (m + 1) * 8)
                chi_ref[at, :] += folded(term)
                count_ref[at, :] += folded(jnp.where(weights[m] > 0.0, 1.0, 0.0))
                target = slice(m * rows + row, m * rows + row + high)
                factor_ref[target, lanes] = weights[m] / (1.0 + term / CLIP_LEVEL)
        return carry

    lax.fori_loop(0, width // LANES, body, 0, unroll=2)
    for m in range(len(members)):
        at = slice(m * 8, (m + 1) * 8)
        sums_ref[0, m : m + 1, :] = jnp.sum(chi_ref[at, :], axis=0, keepdims=True)
        sums_ref[1, m : m + 1, :] = jnp.sum(count_ref[at, :], axis=0, keepdims=True)


def residual_pass(values, weights, visits):
    count, width = values[0].shape
    members = 2 * visits
    return pl.pallas_call(
        functools.partial(residual_kernel, visits),
        out_shape=(held((2 * count, width), F32), held((2, members, LANES), F32)),
        in_specs=[whole()] * 4,
        out_specs=(whole(), whole()),
        scratch_shapes=[pltpu.VMEM((members * 8, LANES), F32)] * 2,
        compiler_params=LIMIT,
        name="residual",
    )(*kept(*values, *weights))


def final_kernel(visits, sums_ref, own_ref, other_ref, factor_ref, out_ref, chi_ref):
    rows = own_ref.shape[0] // visits
    width = out_ref.shape[1]
    high = min(16, rows)
    start = pl.program_id(0) * width
    chi = jnp.sum(sums_ref[0], axis=1, keepdims=True) / jnp.sum(
        sums_ref[1], axis=1, keepdims=True
    )
    scale = 1.0 / (CHI_OFFSET + chi)

    @pl.when(pl.program_id(0) == 0)
    def _():
        for v in range(visits):
            chi_ref[v] = chi[v, 0]

    scales = [jnp.broadcast_to(scale[m : m + 1], (high, LANES)) for m in range(2 * visits)]
    for lane in range(0, width, LANES):
        lanes = pl.ds(pl.multiple_of(start + lane, LANES), LANES)
        for row in range(0, rows, high):
            numer = denom = None
            for m in range(2 * visits):
                source = own_ref if m < visits else other_ref
                v = m % visits
                value = source[v * rows + row : v * rows + row + high, lanes].astype(F32)
                revised = factor_ref[m * rows + row : m * rows + row + high, lanes] * scales[m]
                numer = revised * value if numer is None else numer + revised * value
                denom = revised if denom is None else denom + revised
            out_ref[row : row + high, lane : lane + LANES] = numer / (denom + PRIOR_WEIGHT)


def final_pass(sums, values, factors, visits):
    count, width = values[0].shape
    rows = count // visits
    tile = min(512, width)
    return pl.pallas_call(
        functools.partial(final_kernel, visits),
        out_shape=(
            jax.ShapeDtypeStruct((rows, width), F32),
            jax.ShapeDtypeStruct((visits,), F32),
        ),
        grid=(width // tile,),
        in_specs=[whole()] * 4,
        out_specs=(pl.BlockSpec((rows, tile), lambda i: (0, i)), whole(pltpu.SMEM)),
        compiler_params=LIMIT,
        name="final",
    )(*kept(sums, *values, factors))


def per_device(warps, badbits, coverage, variance, psf_index, psf_table, row_basis, col_basis):
    visits, rows, _ = warps.shape
    half = row_basis.shape[1] // 2
    strips = lax.axis_size("sky")
    up = [(i, i + 1) for i in range(strips - 1)]
    down = [(j, i) for i, j in up]
    swap = [(0, 1), (1, 0)]
    side = lax.axis_index("visit").astype(jnp.int32).reshape(1)

    last, leading, image = pack_rows(warps, half)
    before = lax.ppermute(last, "sky", up)
    after = lax.ppermute(leading, "sky", down)
    send_weight, own_weight = pixel_weights(badbits, coverage, variance, side)
    other_weight = lax.ppermute(send_weight, "visit", swap)
    column, own, edge = tables(psf_index, psf_table, row_basis, col_basis, visits, rows)
    part = own_part(image, column, own, visits)
    (send_value,) = edge_part(
        1 - side, before, after, column, edge, part, visits, half
    )
    other_value = lax.ppermute(send_value, "visit", swap)
    own_value, other_weight = edge_part(
        side, before, after, column, edge, part, visits, half, other_weight
    )
    values = (own_value, other_value)
    factors, sums = residual_pass(values, (own_weight, other_weight), visits)
    theirs = lax.ppermute(sums, "visit", swap)
    sums = sums + jnp.concatenate([theirs[:, visits:], theirs[:, :visits]], axis=1)
    step = 1
    while step < strips:
        sums = sums + lax.ppermute(sums, "sky", [(i, i ^ step) for i in range(strips)])
        step *= 2
    return final_pass(sums, values, factors, visits)


def solution(mesh):
    placed = (
        P(("tract", "visit"), "sky", None),
        P(("tract", "visit"), "sky", None),
        P(("tract", "visit"), "sky"),
        P(("tract", "visit"), "sky"),
        P(("tract", "visit")),
        P(),
        P(),
        P(),
    )
    return jax.shard_map(
        per_device,
        mesh=mesh,
        in_specs=placed,
        out_specs=(P(("tract", "sky"), "visit"), P(("tract", "visit"))),
        check_vma=False,
    )
```

```python
import functools

import jax
import jax.numpy as jnp
from jax import lax
from jax.experimental import pallas as pl
from jax.experimental.pallas import tpu as pltpu
from jax.sharding import PartitionSpec as P

PRIOR_WEIGHT = 1.0
CLIP_LEVEL = 9.0
CHI_OFFSET = 0.5
LANES = 128
SHIFT = LANES // 2
F32 = jnp.float32
BF16 = jnp.bfloat16


def whole(space=pltpu.VMEM):
    return pl.BlockSpec(memory_space=space)


def kept(*arrays):
    return [pltpu.with_memory_space_constraint(array, pltpu.VMEM) for array in arrays]


def away(*arrays):
    return [pltpu.with_memory_space_constraint(array, pltpu.HBM) for array in arrays]


def held(shape, dtype):
    return pltpu.VMEM(shape, dtype)


LIMIT = pltpu.CompilerParams(vmem_limit_bytes=20 * 1024 * 1024)


def lane_index(shape):
    return lax.broadcasted_iota(jnp.int32, shape, len(shape) - 1)


def pack_kernel(half, first, skip, x_ref, edge_ref, rows_ref, arrived):
    visits, depth, columns = rows_ref.shape
    chunks = arrived.shape[0]
    width = columns // chunks
    copies = []
    for c in range(chunks):
        lanes = slice(c * width, (c + 1) * width)
        copies.append(
            pltpu.make_async_copy(
                x_ref.at[:, first : first + depth, lanes], rows_ref.at[:, :, lanes], arrived.at[c]
            )
        )
        copies[c].start()
    main = half // 8 * 8
    rest = half - main
    shape = (visits * half, visits * depth)
    target = lax.broadcasted_iota(jnp.int32, shape, 0)
    source_row = lane_index(shape)
    line = jnp.where(
        target < visits * main,
        lax.div(target, max(main, 1)) * depth + lax.rem(target, max(main, 1)),
        lax.div(target - visits * main, max(rest, 1)) * depth
        + main
        + lax.rem(target - visits * main, max(rest, 1)),
    )
    select = jnp.where(source_row == line + skip, 1.0, 0.0).astype(BF16)
    low = lane_index((edge_ref.shape[0], LANES)) < SHIFT
    step = 2 * LANES

    def put(g, value):
        edge_ref[:, g * LANES : (g + 1) * LANES] = value.astype(BF16)

    before = opening = None
    for start in range(0, columns, step):
        if start % width == 0:
            copies[start // width].wait()
        source = rows_ref[:, :, start : start + step].reshape(visits * depth, step)
        found = jnp.dot(select, source, preferred_element_type=F32)
        for part in range(2):
            here = pltpu.roll(found[:, part * LANES : (part + 1) * LANES], SHIFT, 1)
            if before is None:
                opening = here
            else:
                put(start // LANES + part, jnp.where(low, before, here))
            before = here
    put(0, jnp.where(low, before, opening))


def pack_rows(warps, half, upper):
    visits, rows, columns = warps.shape
    depth = rows // 2
    assert depth >= half and rows % 2 == 0
    first = 0 if upper else depth
    skip = 0 if upper else depth - half
    chunks = max(1, columns // 1024)
    return pl.pallas_call(
        functools.partial(pack_kernel, half, first, skip),
        out_shape=(held((visits * half, columns), BF16), held((visits, depth, columns), BF16)),
        in_specs=[pl.BlockSpec(memory_space=pl.ANY)],
        out_specs=(whole(),) * 2,
        scratch_shapes=[pltpu.SemaphoreType.DMA((chunks,))],
        compiler_params=LIMIT,
        name="pack_upper" if upper else "pack_lower",
    )(*away(warps))


def level_rows(visits, bands):
    return -(-3 * visits * bands // 16) * 16


def weight_kernel(visits, bands, side_ref, cover_ref, var_ref, bits_ref, send_ref, keep_ref):
    count = bits_ref.shape[0]
    rows = count // visits
    high = rows // bands
    width = bits_ref.shape[1]
    steps = send_ref.shape[1] // width
    step = pl.program_id(0)
    half = lax.div(step, steps)
    lanes = pl.ds(pl.multiple_of(lax.rem(step, steps) * width, width), width)
    extra = level_rows(visits, bands)

    def fill(out_ref):
        line = lax.broadcasted_iota(jnp.int32, (extra, LANES), 0)
        levels = jnp.zeros((extra, LANES), F32)
        for v in range(visits):
            for b in range(bands):
                at = slice(v * rows + b * high, v * rows + (b + 1) * high)
                covers = jnp.where(cover_ref[b, v] != 0, 7, 0)
                usable = jnp.bitwise_and(bits_ref[at, :], 7) < covers
                out_ref[at, lanes] = jnp.where(usable, 1.0, 0.0).astype(BF16)
                left = 1.0 / jnp.full((8, LANES), var_ref[b, v], F32)
                for k in range(3):
                    part = left.astype(BF16).astype(F32)
                    left = left - part
                    spot = (k * bands + b) * visits + v
                    levels = jnp.where(line == spot, part[:1], levels)
        wide = jnp.concatenate([levels.astype(BF16)] * (width // LANES), axis=1)
        out_ref[count:, lanes] = wide

    pl.when(half == 0)(lambda: fill(send_ref))
    pl.when(half == 1)(lambda: fill(keep_ref))


def pixel_weights(badbits, coverage, variance, side):
    visits, rows, columns = badbits.shape
    bands = coverage.shape[1]
    (bits,) = away(badbits.reshape(visits * rows, columns))
    width = columns // 2
    tile = min(1024, width)
    count = width // tile
    shape = held((visits * rows + level_rows(visits, bands), width), BF16)

    def block(i, s):
        first = i < count
        return 0, jnp.where(first, (1 - s[0]) * count + i, s[0] * count + i - count)

    return pl.pallas_call(
        functools.partial(weight_kernel, visits, bands),
        out_shape=(shape, shape),
        grid_spec=pltpu.PrefetchScalarGridSpec(
            num_scalar_prefetch=1,
            grid=(2 * count,),
            in_specs=[
                whole(pltpu.SMEM),
                whole(pltpu.SMEM),
                pl.BlockSpec((visits * rows, tile), block),
            ],
            out_specs=(whole(), whole()),
        ),
        compiler_params=LIMIT,
        name="weights",
    )(side, *away(coverage.T, variance.T), bits)


def split(value):
    high = value.astype(BF16)
    return high, (value - high.astype(F32)).astype(BF16)


def edge_segments(visits, rows, half):
    main = half // 8 * 8
    rest = half - main
    segments = []
    for v in range(visits):
        here, start = [], 0
        for below in (0, 1):
            here.append((start, start + main, (half + rows if below else 0) - start))
            start += main
        for below in (0, 1):
            first = start + v * rest
            offset = (half + rows if below else 0) + main - first
            here.append((first, first + rest, offset))
            start += visits * rest
        segments.append(here)
    return segments, start


def table_kernel(visits, rows, half, index_ref, table_ref, profile_ref, column_out, own_out, edge_out):
    bases = table_ref.shape[0]
    window = 2 * LANES

    def spread(line, shift, count):
        line = jnp.broadcast_to(line, (8, LANES))
        block = pltpu.roll(line, 0, 1, stride=1, stride_axis=0)
        blocks = [pltpu.roll(block, (shift + i) % LANES, 1) for i in range(0, count, 8)]
        return jnp.concatenate(blocks, axis=0)

    k = lax.broadcasted_iota(jnp.int32, (window, LANES), 0)
    gap = k - lane_index((window, LANES))
    inside = (gap >= 0) & (gap < LANES)
    for b in range(bases):
        line = profile_ref[bases + b : bases + b + 1, :]
        band = jnp.where(inside, spread(line, SHIFT - half, window), 0.0)
        column_out[:, b * LANES : (b + 1) * LANES] = band.astype(BF16)

    lane = lane_index((rows, LANES))

    def assemble(out_ref, high, segments):
        for b in range(bases):
            start = b * high % LANES
            group = b * high // LANES * LANES
            line = profile_ref[b : b + 1, :]
            found = {}
            for v in range(visits):
                total = jnp.zeros((rows, LANES), F32)
                for first, last, offset in segments[v]:
                    if first == last:
                        continue
                    key = (first, last, offset)
                    if key not in found:
                        mask = (lane >= start + first) & (lane < start + last)
                        found[key] = jnp.where(mask, spread(line, start - offset, rows), 0.0)
                    total = total + found[key]
                top, low = split(total * table_ref[b, index_ref[v]])
                at = 2 * v * rows
                lanes = slice(group, group + LANES)
                if start == 0:
                    out_ref[at : at + rows, lanes] = top
                    out_ref[at + rows : at + 2 * rows, lanes] = low
                else:
                    out_ref[at : at + rows, lanes] += top
                    out_ref[at + rows : at + 2 * rows, lanes] += low

    assemble(own_out, rows, [[(0, rows, half)]] * visits)
    segments, high = edge_segments(visits, rows, half)
    assemble(edge_out, high, segments)


def tables(psf_index, psf_table, row_basis, col_basis, visits, rows):
    bases, taps = row_basis.shape
    half = taps // 2
    profile = jnp.concatenate([row_basis, col_basis[:, ::-1]], axis=0).astype(F32)
    profile = jnp.pad(profile, ((0, 0), (0, LANES - taps)))
    return pl.pallas_call(
        functools.partial(table_kernel, visits, rows, half),
        out_shape=(
            held((2 * LANES, bases * LANES), BF16),
            held((2 * visits * rows, bases * rows), BF16),
            held((2 * visits * rows, bases * edge_segments(visits, rows, half)[1]), BF16),
        ),
        in_specs=[whole(pltpu.SMEM), whole(pltpu.SMEM), whole()],
        out_specs=(whole(),) * 3,
        compiler_params=LIMIT,
        name="tables",
    )(psf_index, psf_table.T, profile)


BLOCKS = 4


def convolve(windows, column_ref, row_ref, pieces):
    bases = column_ref.shape[1] // LANES
    count = windows[0].shape[0]
    layers = jnp.dot(
        jnp.concatenate(windows, axis=0), column_ref[...], preferred_element_type=F32
    )
    high = row_ref.shape[0] // (2 * len(pieces))
    for first in range(0, len(windows), 2):
        totals = []
        for v, parts in enumerate(pieces):
            sides = []
            for n in (first, first + 1):
                taken = [
                    layers[n * count + top : n * count + last, b * LANES : (b + 1) * LANES]
                    for b in range(bases)
                    for top, last in parts
                ]
                sides.append(jnp.concatenate(taken, axis=0).astype(BF16))
            total = jnp.dot(
                row_ref[2 * v * high : 2 * (v + 1) * high, :],
                jnp.concatenate(sides, axis=1),
                preferred_element_type=F32,
            )
            totals.append(total[:high] + total[high:])
        yield first, totals


def own_kernel(visits, upper_ref, lower_ref, column_ref, row_ref, out_ref, shifted):
    half_count, columns = upper_ref.shape
    depth = half_count // visits
    rows = 2 * depth
    groups = columns // LANES
    low = lane_index((half_count, LANES)) < SHIFT
    for place, ref in enumerate((upper_ref, lower_ref)):
        lines = slice(place * half_count, (place + 1) * half_count)
        before = jnp.zeros((half_count, LANES), F32)
        for g in range(groups + 1):
            here = jnp.zeros((half_count, LANES), F32)
            if g < groups:
                here = pltpu.roll(ref[:, g * LANES : (g + 1) * LANES].astype(F32), SHIFT, 1)
            value = jnp.where(low, before, here).astype(BF16)
            shifted[lines, g * LANES : (g + 1) * LANES] = value
            before = here
    pieces = [
        [(place * half_count + v * depth, place * half_count + (v + 1) * depth) for place in (0, 1)]
        for v in range(visits)
    ]
    blocks = min(BLOCKS, groups)

    def body(step, carry):
        windows = [
            shifted[:, pl.ds(pl.multiple_of((blocks * step + n) * LANES, LANES), 2 * LANES)]
            for n in range(blocks)
        ]
        for first, totals in convolve(windows, column_ref, row_ref, pieces):
            start = (blocks * step + first) * LANES
            at = pl.ds(pl.multiple_of(start, 2 * LANES), 2 * LANES)
            for v, total in enumerate(totals):
                out_ref[v * rows : (v + 1) * rows, at] = total
        return carry

    lax.fori_loop(0, groups // blocks, body, 0, unroll=4)


def own_part(upper, lower, column, own, visits):
    half_count, columns = upper.shape
    return pl.pallas_call(
        functools.partial(own_kernel, visits),
        out_shape=held((2 * half_count, columns), F32),
        in_specs=[whole()] * 4,
        out_specs=whole(),
        scratch_shapes=[pltpu.VMEM((2 * half_count, columns + LANES), BF16)],
        compiler_params=LIMIT,
        cost_estimate=pl.CostEstimate(flops=10**9, bytes_accessed=10**7, transcendentals=0),
        name="own_rows",
    )(*kept(upper, lower, column, own))


def edge_kernel(visits, half, side_ref, up_ref, down_ref, column_ref, row_ref, part_ref, *refs):
    out_ref, shifted = refs
    edge, columns = up_ref.shape
    rows = out_ref.shape[0] // visits
    width = out_ref.shape[1]
    groups = columns // LANES
    inner = width // LANES
    base = side_ref[0] * inner
    lane = lane_index((2 * edge, LANES))
    for g in range(inner + 1):
        at = base + g
        lanes = pl.ds(pl.multiple_of(lax.rem(at, groups) * LANES, LANES), LANES)
        value = jnp.concatenate(
            [up_ref[:, lanes].astype(F32), down_ref[:, lanes].astype(F32)], axis=0
        )
        if g == 0:
            value = jnp.where(lane >= jnp.where(at == 0, SHIFT, 0), value, 0.0)
        if g == inner:
            value = jnp.where(lane < jnp.where(at == groups, SHIFT, LANES), value, 0.0)
        shifted[:, g * LANES : (g + 1) * LANES] = value.astype(BF16)
    main = half // 8 * 8
    pieces = [
        [(top + v * main, top + (v + 1) * main) for top in (0, edge)]
        + [(top + visits * main, top + edge) for top in (0, edge)]
        for v in range(visits)
    ]
    pieces = [[(top, last) for top, last in parts if last > top] for parts in pieces]
    blocks = min(BLOCKS, inner)

    def body(step, carry):
        windows = [
            shifted[:, pl.ds(pl.multiple_of((blocks * step + n) * LANES, LANES), 2 * LANES)]
            for n in range(blocks)
        ]
        for first, totals in convolve(windows, column_ref, row_ref, pieces):
            start = (blocks * step + first) * LANES
            at = pl.ds(pl.multiple_of(start, 2 * LANES), 2 * LANES)
            source = pl.ds(pl.multiple_of(base * LANES + start, 2 * LANES), 2 * LANES)
            for v, total in enumerate(totals):
                lines = slice(v * rows, (v + 1) * rows)
                out_ref[lines, at] = (total + part_ref[lines, source]).astype(BF16)
        return carry

    lax.fori_loop(0, inner // blocks, body, 0, unroll=4)


def edge_part(side, up, down, column, edge, part, visits, half):
    count, columns = part.shape
    width = columns // 2
    return pl.pallas_call(
        functools.partial(edge_kernel, visits, half),
        out_shape=held((count, width), BF16),
        in_specs=[whole(pltpu.SMEM)] + [whole()] * 5,
        out_specs=whole(),
        scratch_shapes=[pltpu.VMEM((2 * up.shape[0], width + LANES), BF16)],
        compiler_params=LIMIT,
        name="edge_rows",
    )(side, *kept(up, down, column, edge, part))


def residual_kernel(visits, bands, *refs):
    value_refs, weight_refs = refs[0:2], refs[2:4]
    factor_ref, sums_ref, chi_ref, count_ref = refs[4:]
    rows = value_refs[0].shape[0] // visits
    width = value_refs[0].shape[1]
    high = min(16, rows // bands)
    chi_ref[...] = jnp.zeros_like(chi_ref)
    count_ref[...] = jnp.zeros_like(count_ref)

    def folded(value):
        total = value[:8]
        for start in range(8, high, 8):
            total = total + value[start : start + 8]
        return total

    members = [(side, v) for side in range(2) for v in range(visits)]
    count = value_refs[0].shape[0]
    levels = {}
    for side in range(2):
        found = weight_refs[side][count:, :LANES].astype(F32)
        for v in range(visits):
            for b in range(bands):
                spots = [(k * bands + b) * visits + v for k in range(3)]
                parts = [found[spot : spot + 1] for spot in spots]
                level = (parts[0] + parts[1]) + parts[2]
                levels[side, v, b] = jnp.broadcast_to(level, (high, LANES))

    def body(step, carry):
        lanes = pl.ds(pl.multiple_of(step * LANES, LANES), LANES)
        for row in range(0, rows, high):
            band = row // (rows // bands)
            values, weights, flags = [], [], []
            numer = denom = None
            for side, v in members:
                at = slice(v * rows + row, v * rows + row + high)
                value = value_refs[side][at, lanes].astype(F32)
                flag = weight_refs[side][at, lanes].astype(F32)
                weight = flag * levels[side, v, band]
                flags.append(flag)
                values.append(value)
                weights.append(weight)
                numer = weight * value if numer is None else numer + weight * value
                denom = weight if denom is None else denom + weight
            first = numer / (denom + PRIOR_WEIGHT)
            for m, (side, v) in enumerate(members):
                residual = values[m] - first
                term = weights[m] * (residual * residual)
                at = slice(m * 8, (m + 1) * 8)
                chi_ref[at, :] += folded(term)
                count_ref[at, :] += folded(flags[m])
                target = slice(m * rows + row, m * rows + row + high)
                factor_ref[target, lanes] = weights[m] / (1.0 + term / CLIP_LEVEL)
        return carry

    lax.fori_loop(0, width // LANES, body, 0, unroll=2)
    for m in range(len(members)):
        at = slice(m * 8, (m + 1) * 8)
        sums_ref[0, m : m + 1, :] = jnp.sum(chi_ref[at, :], axis=0, keepdims=True)
        sums_ref[1, m : m + 1, :] = jnp.sum(count_ref[at, :], axis=0, keepdims=True)


def residual_pass(values, weights, visits, bands):
    count, width = values[0].shape
    members = 2 * visits
    return pl.pallas_call(
        functools.partial(residual_kernel, visits, bands),
        out_shape=(held((2 * count, width), F32), held((2, members, LANES), F32)),
        in_specs=[whole()] * 4,
        out_specs=(whole(), whole()),
        scratch_shapes=[pltpu.VMEM((members * 8, LANES), F32)] * 2,
        compiler_params=LIMIT,
        name="residual",
    )(*kept(*values, *weights))


def final_kernel(visits, sums_ref, own_ref, other_ref, factor_ref, out_ref, chi_ref, done, sent):
    rows, width = done.shape
    chunks = sent.shape[0]
    high = min(16, rows)
    chi = jnp.sum(sums_ref[0], axis=1, keepdims=True) / jnp.sum(
        sums_ref[1], axis=1, keepdims=True
    )
    scale = 1.0 / (CHI_OFFSET + chi)
    for v in range(visits):
        chi_ref[v] = chi[v, 0]
    scales = [jnp.broadcast_to(scale[m : m + 1], (high, LANES)) for m in range(2 * visits)]
    copies = []
    for c in range(chunks):
        for lane in range(c * width // chunks, (c + 1) * width // chunks, LANES):
            lanes = slice(lane, lane + LANES)
            for row in range(0, rows, high):
                numer = denom = None
                for m in range(2 * visits):
                    source = own_ref if m < visits else other_ref
                    at = (m % visits) * rows + row
                    value = source[at : at + high, lanes].astype(F32)
                    at = m * rows + row
                    revised = factor_ref[at : at + high, lanes] * scales[m]
                    numer = revised * value if numer is None else numer + revised * value
                    denom = revised if denom is None else denom + revised
                done[row : row + high, lanes] = numer / (denom + PRIOR_WEIGHT)
        lanes = slice(c * width // chunks, (c + 1) * width // chunks)
        copies.append(
            pltpu.make_async_copy(done.at[:, lanes], out_ref.at[:, lanes], sent.at[c])
        )
        copies[c].start()
    for copy in copies:
        copy.wait()


def final_pass(sums, values, factors, visits):
    count, width = values[0].shape
    rows = count // visits
    chunks = max(1, width // 512)
    return pl.pallas_call(
        functools.partial(final_kernel, visits),
        out_shape=(
            jax.ShapeDtypeStruct((rows, width), F32),
            jax.ShapeDtypeStruct((visits,), F32),
        ),
        in_specs=[whole()] * 4,
        out_specs=(pl.BlockSpec(memory_space=pl.ANY), whole(pltpu.SMEM)),
        scratch_shapes=[pltpu.VMEM((rows, width), F32), pltpu.SemaphoreType.DMA((chunks,))],
        compiler_params=LIMIT,
        name="final",
    )(*kept(sums, *values, factors))


def per_device(warps, badbits, coverage, variance, psf_index, psf_table, row_basis, col_basis):
    visits, rows, columns = warps.shape
    half = row_basis.shape[1] // 2
    strips = lax.axis_size("sky")
    up = [(i, i + 1) for i in range(strips - 1)]
    down = [(j, i) for i, j in up]
    swap = [(0, 1), (1, 0)]
    side = lax.axis_index("visit").astype(jnp.int32).reshape(1)

    last, lower = pack_rows(warps, half, False)
    before = lax.ppermute(last, "sky", up)
    leading, upper = pack_rows(warps, half, True)
    after = lax.ppermute(leading, "sky", down)
    send_weight, own_weight = pixel_weights(badbits, coverage, variance, side)
    other_weight = lax.ppermute(send_weight, "visit", swap)
    column, own, edge = tables(psf_index, psf_table, row_basis, col_basis, visits, rows)
    part = own_part(upper.reshape(-1, columns), lower.reshape(-1, columns), column, own, visits)
    send_value = edge_part(1 - side, before, after, column, edge, part, visits, half)
    other_value = lax.ppermute(send_value, "visit", swap)
    own_value = edge_part(side, before, after, column, edge, part, visits, half)
    values = (own_value, other_value)
    factors, sums = residual_pass(values, (own_weight, other_weight), visits, coverage.shape[1])
    theirs = lax.ppermute(sums, "visit", swap)
    sums = sums + jnp.concatenate([theirs[:, visits:], theirs[:, :visits]], axis=1)
    step = 1
    while step < strips:
        sums = sums + lax.ppermute(sums, "sky", [(i, i ^ step) for i in range(strips)])
        step *= 2
    return final_pass(sums, values, factors, visits)


def solution(mesh):
    placed = (
        P(("tract", "visit"), "sky", None),
        P(("tract", "visit"), "sky", None),
        P(("tract", "visit"), "sky"),
        P(("tract", "visit"), "sky"),
        P(("tract", "visit")),
        P(),
        P(),
        P(),
    )
    return jax.shard_map(
        per_device,
        mesh=mesh,
        in_specs=placed,
        out_specs=(P(("tract", "sky"), "visit"), P(("tract", "visit"))),
        check_vma=False,
    )
```

```python
import functools

import jax
import jax.numpy as jnp
from jax import lax
from jax.experimental import pallas as pl
from jax.experimental.pallas import tpu as pltpu
from jax.sharding import PartitionSpec as P

PRIOR_WEIGHT = 1.0
CLIP_LEVEL = 9.0
CHI_OFFSET = 0.5
LANES = 128
SHIFT = LANES // 2
F32 = jnp.float32
BF16 = jnp.bfloat16


def whole(space=pltpu.VMEM):
    return pl.BlockSpec(memory_space=space)


def kept(*arrays):
    return [pltpu.with_memory_space_constraint(array, pltpu.VMEM) for array in arrays]


def away(*arrays):
    return [pltpu.with_memory_space_constraint(array, pltpu.HBM) for array in arrays]


def held(shape, dtype):
    return pltpu.VMEM(shape, dtype)


LIMIT = pltpu.CompilerParams(vmem_limit_bytes=20 * 1024 * 1024)


def lane_index(shape):
    return lax.broadcasted_iota(jnp.int32, shape, len(shape) - 1)


def pack_kernel(half, first, skip, x_ref, edge_ref, rows_ref, arrived):
    visits, depth, columns = rows_ref.shape
    chunks = arrived.shape[0]
    width = columns // chunks
    copies = []
    for c in range(chunks):
        lanes = slice(c * width, (c + 1) * width)
        copies.append(
            pltpu.make_async_copy(
                x_ref.at[:, first : first + depth, lanes], rows_ref.at[:, :, lanes], arrived.at[c]
            )
        )
        copies[c].start()
    main = half // 8 * 8
    rest = half - main
    shape = (visits * half, visits * depth)
    target = lax.broadcasted_iota(jnp.int32, shape, 0)
    source_row = lane_index(shape)
    line = jnp.where(
        target < visits * main,
        lax.div(target, max(main, 1)) * depth + lax.rem(target, max(main, 1)),
        lax.div(target - visits * main, max(rest, 1)) * depth
        + main
        + lax.rem(target - visits * main, max(rest, 1)),
    )
    select = jnp.where(source_row == line + skip, 1.0, 0.0).astype(BF16)
    low = lane_index((edge_ref.shape[0], LANES)) < SHIFT
    step = 2 * LANES

    def put(g, value):
        edge_ref[:, g * LANES : (g + 1) * LANES] = value.astype(BF16)

    before = opening = None
    for start in range(0, columns, step):
        if start % width == 0:
            copies[start // width].wait()
        source = rows_ref[:, :, start : start + step].reshape(visits * depth, step)
        found = jnp.dot(select, source, preferred_element_type=F32)
        for part in range(2):
            here = pltpu.roll(found[:, part * LANES : (part + 1) * LANES], SHIFT, 1)
            if before is None:
                opening = here
            else:
                put(start // LANES + part, jnp.where(low, before, here))
            before = here
    put(0, jnp.where(low, before, opening))


def pack_rows(warps, half, upper):
    visits, rows, columns = warps.shape
    depth = rows // 2
    assert depth >= half and rows % 2 == 0
    first = 0 if upper else depth
    skip = 0 if upper else depth - half
    chunks = max(1, columns // 1024)
    return pl.pallas_call(
        functools.partial(pack_kernel, half, first, skip),
        out_shape=(held((visits * half, columns), BF16), held((visits, depth, columns), BF16)),
        in_specs=[pl.BlockSpec(memory_space=pl.ANY)],
        out_specs=(whole(),) * 2,
        scratch_shapes=[pltpu.SemaphoreType.DMA((chunks,))],
        compiler_params=LIMIT,
        name="pack_upper" if upper else "pack_lower",
    )(*away(warps))


def level_rows(visits, bands):
    return -(-3 * visits * bands // 16) * 16


def weight_kernel(visits, bands, side_ref, cover_ref, var_ref, bits_ref, send_ref, keep_ref):
    count = bits_ref.shape[0]
    rows = count // visits
    high = rows // bands
    width = bits_ref.shape[1]
    steps = send_ref.shape[1] // width
    step = pl.program_id(0)
    half = lax.div(step, steps)
    lanes = pl.ds(pl.multiple_of(lax.rem(step, steps) * width, width), width)
    extra = level_rows(visits, bands)

    def fill(out_ref):
        line = lax.broadcasted_iota(jnp.int32, (extra, LANES), 0)
        levels = jnp.zeros((extra, LANES), F32)
        for v in range(visits):
            for b in range(bands):
                at = slice(v * rows + b * high, v * rows + (b + 1) * high)
                covers = jnp.where(cover_ref[b, v] != 0, 7, 0)
                usable = jnp.bitwise_and(bits_ref[at, :], 7) < covers
                out_ref[at, lanes] = jnp.where(usable, 1.0, 0.0).astype(BF16)
                left = 1.0 / jnp.full((8, LANES), var_ref[b, v], F32)
                for k in range(3):
                    part = left.astype(BF16).astype(F32)
                    left = left - part
                    spot = (k * bands + b) * visits + v
                    levels = jnp.where(line == spot, part[:1], levels)
        wide = jnp.concatenate([levels.astype(BF16)] * (width // LANES), axis=1)
        out_ref[count:, lanes] = wide

    pl.when(half == 0)(lambda: fill(send_ref))
    pl.when(half == 1)(lambda: fill(keep_ref))


def pixel_weights(badbits, coverage, variance, side):
    visits, rows, columns = badbits.shape
    bands = coverage.shape[1]
    (bits,) = away(badbits.reshape(visits * rows, columns))
    width = columns // 2
    tile = min(1024, width)
    count = width // tile
    shape = held((visits * rows + level_rows(visits, bands), width), BF16)

    def block(i, s):
        first = i < count
        return 0, jnp.where(first, (1 - s[0]) * count + i, s[0] * count + i - count)

    return pl.pallas_call(
        functools.partial(weight_kernel, visits, bands),
        out_shape=(shape, shape),
        grid_spec=pltpu.PrefetchScalarGridSpec(
            num_scalar_prefetch=1,
            grid=(2 * count,),
            in_specs=[
                whole(pltpu.SMEM),
                whole(pltpu.SMEM),
                pl.BlockSpec((visits * rows, tile), block),
            ],
            out_specs=(whole(), whole()),
        ),
        compiler_params=LIMIT,
        name="weights",
    )(side, *away(coverage.T, variance.T), bits)


def split(value):
    high = value.astype(BF16)
    return high, (value - high.astype(F32)).astype(BF16)


def edge_segments(visits, rows, half):
    main = half // 8 * 8
    rest = half - main
    segments = []
    for v in range(visits):
        here, start = [], 0
        for below in (0, 1):
            here.append((start, start + main, (half + rows if below else 0) - start))
            start += main
        for below in (0, 1):
            first = start + v * rest
            offset = (half + rows if below else 0) + main - first
            here.append((first, first + rest, offset))
            start += visits * rest
        segments.append(here)
    return segments, start


def table_kernel(visits, rows, half, index_ref, table_ref, row_ref, col_ref, column_out, own_out, edge_out):
    bases, taps = row_ref.shape
    window = 2 * LANES

    def spread(line, shift, count):
        line = jnp.broadcast_to(line, (8, LANES))
        block = pltpu.roll(line, 0, 1, stride=1, stride_axis=0)
        blocks = [pltpu.roll(block, (shift + i) % LANES, 1) for i in range(0, count, 8)]
        return jnp.concatenate(blocks, axis=0)

    tap = lax.broadcasted_iota(jnp.int32, (taps, LANES), 0)
    place = lane_index((taps, LANES))
    ahead = jnp.where(place == tap, 1.0, 0.0).astype(BF16)
    back = jnp.where(place == taps - 1 - tap, 1.0, 0.0).astype(BF16)
    row_lines = jnp.dot(row_ref[...], ahead, preferred_element_type=F32)
    col_lines = jnp.dot(col_ref[...], back, preferred_element_type=F32)
    k = lax.broadcasted_iota(jnp.int32, (window, LANES), 0)
    gap = k - lane_index((window, LANES))
    inside = (gap >= 0) & (gap < LANES)
    for b in range(bases):
        line = col_lines[b : b + 1, :]
        band = jnp.where(inside, spread(line, SHIFT - half, window), 0.0)
        column_out[:, b * LANES : (b + 1) * LANES] = band.astype(BF16)

    lane = lane_index((rows, LANES))

    def assemble(out_ref, high, segments):
        for b in range(bases):
            start = b * high % LANES
            group = b * high // LANES * LANES
            line = row_lines[b : b + 1, :]
            found = {}
            for v in range(visits):
                total = jnp.zeros((rows, LANES), F32)
                for first, last, offset in segments[v]:
                    if first == last:
                        continue
                    key = (first, last, offset)
                    if key not in found:
                        mask = (lane >= start + first) & (lane < start + last)
                        found[key] = jnp.where(mask, spread(line, start - offset, rows), 0.0)
                    total = total + found[key]
                top, low = split(total * table_ref[b, index_ref[v]])
                at = 2 * v * rows
                lanes = slice(group, group + LANES)
                if start == 0:
                    out_ref[at : at + rows, lanes] = top
                    out_ref[at + rows : at + 2 * rows, lanes] = low
                else:
                    out_ref[at : at + rows, lanes] += top
                    out_ref[at + rows : at + 2 * rows, lanes] += low

    assemble(own_out, rows, [[(0, rows, half)]] * visits)
    segments, high = edge_segments(visits, rows, half)
    assemble(edge_out, high, segments)


def tables(psf_index, psf_table, row_basis, col_basis, visits, rows):
    bases, taps = row_basis.shape
    half = taps // 2
    return pl.pallas_call(
        functools.partial(table_kernel, visits, rows, half),
        out_shape=(
            held((2 * LANES, bases * LANES), BF16),
            held((2 * visits * rows, bases * rows), BF16),
            held((2 * visits * rows, bases * edge_segments(visits, rows, half)[1]), BF16),
        ),
        in_specs=[whole(pltpu.SMEM)] * 2 + [whole()] * 2,
        out_specs=(whole(),) * 3,
        compiler_params=LIMIT,
        name="tables",
    )(psf_index, psf_table.T, row_basis, col_basis)


BLOCKS = 4


def convolve(windows, column_ref, row_ref, pieces):
    bases = column_ref.shape[1] // LANES
    count = windows[0].shape[0]
    layers = jnp.dot(
        jnp.concatenate(windows, axis=0), column_ref[...], preferred_element_type=F32
    )
    high = row_ref.shape[0] // (2 * len(pieces))
    for first in range(0, len(windows), 2):
        totals = []
        for v, parts in enumerate(pieces):
            sides = []
            for n in (first, first + 1):
                taken = [
                    layers[n * count + top : n * count + last, b * LANES : (b + 1) * LANES]
                    for b in range(bases)
                    for top, last in parts
                ]
                sides.append(jnp.concatenate(taken, axis=0).astype(BF16))
            total = jnp.dot(
                row_ref[2 * v * high : 2 * (v + 1) * high, :],
                jnp.concatenate(sides, axis=1),
                preferred_element_type=F32,
            )
            totals.append(total[:high] + total[high:])
        yield first, totals


def own_kernel(visits, upper_ref, lower_ref, column_ref, row_ref, out_ref, shifted):
    half_count, columns = upper_ref.shape
    depth = half_count // visits
    rows = 2 * depth
    groups = columns // LANES
    low = lane_index((half_count, LANES)) < SHIFT
    for place, ref in enumerate((upper_ref, lower_ref)):
        lines = slice(place * half_count, (place + 1) * half_count)
        before = jnp.zeros((half_count, LANES), F32)
        for g in range(groups + 1):
            here = jnp.zeros((half_count, LANES), F32)
            if g < groups:
                here = pltpu.roll(ref[:, g * LANES : (g + 1) * LANES].astype(F32), SHIFT, 1)
            value = jnp.where(low, before, here).astype(BF16)
            shifted[lines, g * LANES : (g + 1) * LANES] = value
            before = here
    pieces = [
        [(place * half_count + v * depth, place * half_count + (v + 1) * depth) for place in (0, 1)]
        for v in range(visits)
    ]
    blocks = min(BLOCKS, groups)

    def body(step, carry):
        windows = [
            shifted[:, pl.ds(pl.multiple_of((blocks * step + n) * LANES, LANES), 2 * LANES)]
            for n in range(blocks)
        ]
        for first, totals in convolve(windows, column_ref, row_ref, pieces):
            start = (blocks * step + first) * LANES
            at = pl.ds(pl.multiple_of(start, 2 * LANES), 2 * LANES)
            for v, total in enumerate(totals):
                out_ref[v * rows : (v + 1) * rows, at] = total
        return carry

    lax.fori_loop(0, groups // blocks, body, 0, unroll=4)


def own_part(upper, lower, column, own, visits):
    half_count, columns = upper.shape
    return pl.pallas_call(
        functools.partial(own_kernel, visits),
        out_shape=held((2 * half_count, columns), F32),
        in_specs=[whole()] * 4,
        out_specs=whole(),
        scratch_shapes=[pltpu.VMEM((2 * half_count, columns + LANES), BF16)],
        compiler_params=LIMIT,
        cost_estimate=pl.CostEstimate(flops=10**9, bytes_accessed=10**7, transcendentals=0),
        name="own_rows",
    )(*kept(upper, lower, column, own))


def edge_kernel(visits, half, side_ref, up_ref, down_ref, column_ref, row_ref, part_ref, *refs):
    out_ref, shifted = refs
    edge, columns = up_ref.shape
    rows = out_ref.shape[0] // visits
    width = out_ref.shape[1]
    groups = columns // LANES
    inner = width // LANES
    base = side_ref[0] * inner
    lane = lane_index((2 * edge, LANES))
    for g in range(inner + 1):
        at = base + g
        lanes = pl.ds(pl.multiple_of(lax.rem(at, groups) * LANES, LANES), LANES)
        value = jnp.concatenate(
            [up_ref[:, lanes].astype(F32), down_ref[:, lanes].astype(F32)], axis=0
        )
        if g == 0:
            value = jnp.where(lane >= jnp.where(at == 0, SHIFT, 0), value, 0.0)
        if g == inner:
            value = jnp.where(lane < jnp.where(at == groups, SHIFT, LANES), value, 0.0)
        shifted[:, g * LANES : (g + 1) * LANES] = value.astype(BF16)
    main = half // 8 * 8
    pieces = [
        [(top + v * main, top + (v + 1) * main) for top in (0, edge)]
        + [(top + visits * main, top + edge) for top in (0, edge)]
        for v in range(visits)
    ]
    pieces = [[(top, last) for top, last in parts if last > top] for parts in pieces]
    blocks = min(BLOCKS, inner)

    def body(step, carry):
        windows = [
            shifted[:, pl.ds(pl.multiple_of((blocks * step + n) * LANES, LANES), 2 * LANES)]
            for n in range(blocks)
        ]
        for first, totals in convolve(windows, column_ref, row_ref, pieces):
            start = (blocks * step + first) * LANES
            at = pl.ds(pl.multiple_of(start, 2 * LANES), 2 * LANES)
            source = pl.ds(pl.multiple_of(base * LANES + start, 2 * LANES), 2 * LANES)
            for v, total in enumerate(totals):
                lines = slice(v * rows, (v + 1) * rows)
                out_ref[lines, at] = (total + part_ref[lines, source]).astype(BF16)
        return carry

    lax.fori_loop(0, inner // blocks, body, 0, unroll=4)


def edge_part(side, up, down, column, edge, part, visits, half):
    count, columns = part.shape
    width = columns // 2
    return pl.pallas_call(
        functools.partial(edge_kernel, visits, half),
        out_shape=held((count, width), BF16),
        in_specs=[whole(pltpu.SMEM)] + [whole()] * 5,
        out_specs=whole(),
        scratch_shapes=[pltpu.VMEM((2 * up.shape[0], width + LANES), BF16)],
        compiler_params=LIMIT,
        name="edge_rows",
    )(side, *kept(up, down, column, edge, part))


def residual_kernel(visits, bands, *refs):
    value_refs, weight_refs = refs[0:2], refs[2:4]
    factor_ref, sums_ref, chi_ref, count_ref = refs[4:]
    rows = value_refs[0].shape[0] // visits
    width = value_refs[0].shape[1]
    high = min(16, rows // bands)
    chi_ref[...] = jnp.zeros_like(chi_ref)
    count_ref[...] = jnp.zeros_like(count_ref)

    def folded(value):
        total = value[:8]
        for start in range(8, high, 8):
            total = total + value[start : start + 8]
        return total

    members = [(side, v) for side in range(2) for v in range(visits)]
    count = value_refs[0].shape[0]
    levels = {}
    for side in range(2):
        found = weight_refs[side][count:, :LANES].astype(F32)
        for v in range(visits):
            for b in range(bands):
                spots = [(k * bands + b) * visits + v for k in range(3)]
                parts = [found[spot : spot + 1] for spot in spots]
                level = (parts[0] + parts[1]) + parts[2]
                levels[side, v, b] = jnp.broadcast_to(level, (high, LANES))

    def body(step, carry):
        lanes = pl.ds(pl.multiple_of(step * LANES, LANES), LANES)
        for row in range(0, rows, high):
            band = row // (rows // bands)
            values, weights, flags = [], [], []
            numer = denom = None
            for side, v in members:
                at = slice(v * rows + row, v * rows + row + high)
                value = value_refs[side][at, lanes].astype(F32)
                flag = weight_refs[side][at, lanes].astype(F32)
                weight = flag * levels[side, v, band]
                flags.append(flag)
                values.append(value)
                weights.append(weight)
                numer = weight * value if numer is None else numer + weight * value
                denom = weight if denom is None else denom + weight
            first = numer / (denom + PRIOR_WEIGHT)
            for m, (side, v) in enumerate(members):
                residual = values[m] - first
                term = weights[m] * (residual * residual)
                at = slice(m * 8, (m + 1) * 8)
                chi_ref[at, :] += folded(term)
                count_ref[at, :] += folded(flags[m])
                target = slice(m * rows + row, m * rows + row + high)
                factor_ref[target, lanes] = weights[m] / (1.0 + term / CLIP_LEVEL)
        return carry

    lax.fori_loop(0, width // LANES, body, 0, unroll=2)
    for m in range(len(members)):
        at = slice(m * 8, (m + 1) * 8)
        sums_ref[0, m : m + 1, :] = jnp.sum(chi_ref[at, :], axis=0, keepdims=True)
        sums_ref[1, m : m + 1, :] = jnp.sum(count_ref[at, :], axis=0, keepdims=True)


def residual_pass(values, weights, visits, bands):
    count, width = values[0].shape
    members = 2 * visits
    return pl.pallas_call(
        functools.partial(residual_kernel, visits, bands),
        out_shape=(held((2 * count, width), F32), held((2, members, LANES), F32)),
        in_specs=[whole()] * 4,
        out_specs=(whole(), whole()),
        scratch_shapes=[pltpu.VMEM((members * 8, LANES), F32)] * 2,
        compiler_params=LIMIT,
        name="residual",
    )(*kept(*values, *weights))


def final_kernel(visits, sums_ref, own_ref, other_ref, factor_ref, out_ref, chi_ref, done, sent):
    rows, width = done.shape
    chunks = sent.shape[0]
    high = min(16, rows)
    chi = jnp.sum(sums_ref[0], axis=1, keepdims=True) / jnp.sum(
        sums_ref[1], axis=1, keepdims=True
    )
    scale = 1.0 / (CHI_OFFSET + chi)
    for v in range(visits):
        chi_ref[v] = chi[v, 0]
    scales = [jnp.broadcast_to(scale[m : m + 1], (high, LANES)) for m in range(2 * visits)]
    copies = []
    for c in range(chunks):
        for lane in range(c * width // chunks, (c + 1) * width // chunks, LANES):
            lanes = slice(lane, lane + LANES)
            for row in range(0, rows, high):
                numer = denom = None
                for m in range(2 * visits):
                    source = own_ref if m < visits else other_ref
                    at = (m % visits) * rows + row
                    value = source[at : at + high, lanes].astype(F32)
                    at = m * rows + row
                    revised = factor_ref[at : at + high, lanes] * scales[m]
                    numer = revised * value if numer is None else numer + revised * value
                    denom = revised if denom is None else denom + revised
                done[row : row + high, lanes] = numer / (denom + PRIOR_WEIGHT)
        lanes = slice(c * width // chunks, (c + 1) * width // chunks)
        copies.append(
            pltpu.make_async_copy(done.at[:, lanes], out_ref.at[:, lanes], sent.at[c])
        )
        copies[c].start()
    for copy in copies:
        copy.wait()


def final_pass(sums, values, factors, visits):
    count, width = values[0].shape
    rows = count // visits
    chunks = max(1, width // 512)
    return pl.pallas_call(
        functools.partial(final_kernel, visits),
        out_shape=(
            jax.ShapeDtypeStruct((rows, width), F32),
            jax.ShapeDtypeStruct((visits,), F32),
        ),
        in_specs=[whole()] * 4,
        out_specs=(pl.BlockSpec(memory_space=pl.ANY), whole(pltpu.SMEM)),
        scratch_shapes=[pltpu.VMEM((rows, width), F32), pltpu.SemaphoreType.DMA((chunks,))],
        compiler_params=LIMIT,
        name="final",
    )(*kept(sums, *values, factors))


def per_device(warps, badbits, coverage, variance, psf_index, psf_table, row_basis, col_basis):
    visits, rows, columns = warps.shape
    half = row_basis.shape[1] // 2
    strips = lax.axis_size("sky")
    up = [(i, i + 1) for i in range(strips - 1)]
    down = [(j, i) for i, j in up]
    swap = [(0, 1), (1, 0)]
    side = lax.axis_index("visit").astype(jnp.int32).reshape(1)

    last, lower = pack_rows(warps, half, False)
    before = lax.ppermute(last, "sky", up)
    leading, upper = pack_rows(warps, half, True)
    after = lax.ppermute(leading, "sky", down)
    send_weight, own_weight = pixel_weights(badbits, coverage, variance, side)
    other_weight = lax.ppermute(send_weight, "visit", swap)
    column, own, edge = tables(psf_index, psf_table, row_basis, col_basis, visits, rows)
    part = own_part(upper.reshape(-1, columns), lower.reshape(-1, columns), column, own, visits)
    send_value = edge_part(1 - side, before, after, column, edge, part, visits, half)
    other_value = lax.ppermute(send_value, "visit", swap)
    own_value = edge_part(side, before, after, column, edge, part, visits, half)
    values = (own_value, other_value)
    factors, sums = residual_pass(values, (own_weight, other_weight), visits, coverage.shape[1])
    theirs = lax.ppermute(sums, "visit", swap)
    sums = sums + jnp.concatenate([theirs[:, visits:], theirs[:, :visits]], axis=1)
    step = 1
    while step < strips:
        sums = sums + lax.ppermute(sums, "sky", [(i, i ^ step) for i in range(strips)])
        step *= 2
    return final_pass(sums, values, factors, visits)


def solution(mesh):
    placed = (
        P(("tract", "visit"), "sky", None),
        P(("tract", "visit"), "sky", None),
        P(("tract", "visit"), "sky"),
        P(("tract", "visit"), "sky"),
        P(("tract", "visit")),
        P(),
        P(),
        P(),
    )
    return jax.shard_map(
        per_device,
        mesh=mesh,
        in_specs=placed,
        out_specs=(P(("tract", "sky"), "visit"), P(("tract", "visit"))),
        check_vma=False,
    )
```

```python
import functools

import jax
import jax.numpy as jnp
from jax import lax
from jax.experimental import pallas as pl
from jax.experimental.pallas import tpu as pltpu
from jax.sharding import PartitionSpec as P

PRIOR_WEIGHT = 1.0
CLIP_LEVEL = 9.0
CHI_OFFSET = 0.5
LANES = 128
SHIFT = LANES // 2
F32 = jnp.float32
BF16 = jnp.bfloat16


def whole(space=pltpu.VMEM):
    return pl.BlockSpec(memory_space=space)


def kept(*arrays):
    return [pltpu.with_memory_space_constraint(array, pltpu.VMEM) for array in arrays]


def away(*arrays):
    return [pltpu.with_memory_space_constraint(array, pltpu.HBM) for array in arrays]


def held(shape, dtype):
    return pltpu.VMEM(shape, dtype)


LIMIT = pltpu.CompilerParams(vmem_limit_bytes=20 * 1024 * 1024)


def lane_index(shape):
    return lax.broadcasted_iota(jnp.int32, shape, len(shape) - 1)


def pack_kernel(half, first, skip, x_ref, *refs):
    edge_ref, rows_ref, arrived = refs[-3:]
    visits, depth, columns = rows_ref.shape
    chunks = arrived.shape[0]
    width = columns // chunks
    copies = []
    for c in range(chunks):
        lanes = slice(c * width, (c + 1) * width)
        copies.append(
            pltpu.make_async_copy(
                x_ref.at[:, first : first + depth, lanes], rows_ref.at[:, :, lanes], arrived.at[c]
            )
        )
        copies[c].start()
    main = half // 8 * 8
    rest = half - main
    shape = (visits * half, visits * depth)
    target = lax.broadcasted_iota(jnp.int32, shape, 0)
    source_row = lane_index(shape)
    line = jnp.where(
        target < visits * main,
        lax.div(target, max(main, 1)) * depth + lax.rem(target, max(main, 1)),
        lax.div(target - visits * main, max(rest, 1)) * depth
        + main
        + lax.rem(target - visits * main, max(rest, 1)),
    )
    select = jnp.where(source_row == line + skip, 1.0, 0.0).astype(BF16)
    low = lane_index((edge_ref.shape[0], LANES)) < SHIFT
    step = 2 * LANES

    def put(g, value):
        edge_ref[:, g * LANES : (g + 1) * LANES] = value.astype(BF16)

    before = opening = None
    for start in range(0, columns, step):
        if start % width == 0:
            copies[start // width].wait()
        source = rows_ref[:, :, start : start + step].reshape(visits * depth, step)
        found = jnp.dot(select, source, preferred_element_type=F32)
        for part in range(2):
            here = pltpu.roll(found[:, part * LANES : (part + 1) * LANES], SHIFT, 1)
            if before is None:
                opening = here
            else:
                put(start // LANES + part, jnp.where(low, before, here))
            before = here
    put(0, jnp.where(low, before, opening))


def pack_rows(warps, half, upper, *after):
    visits, rows, columns = warps.shape
    depth = rows // 2
    assert depth >= half and rows % 2 == 0
    first = 0 if upper else depth
    skip = 0 if upper else depth - half
    chunks = 1
    return pl.pallas_call(
        functools.partial(pack_kernel, half, first, skip),
        out_shape=(held((visits * half, columns), BF16), held((visits, depth, columns), BF16)),
        in_specs=[pl.BlockSpec(memory_space=pl.ANY)] * (1 + len(after)),
        out_specs=(whole(),) * 2,
        scratch_shapes=[pltpu.SemaphoreType.DMA((chunks,))],
        compiler_params=LIMIT,
        name="pack_upper" if upper else "pack_lower",
    )(*away(warps), *after)


def level_rows(visits, bands):
    return -(-3 * visits * bands // 16) * 16


def weight_kernel(visits, bands, side_ref, cover_ref, var_ref, bits_ref, send_ref, keep_ref):
    count = bits_ref.shape[0]
    rows = count // visits
    high = rows // bands
    width = bits_ref.shape[1]
    steps = send_ref.shape[1] // width
    step = pl.program_id(0)
    half = lax.div(step, steps)
    lanes = pl.ds(pl.multiple_of(lax.rem(step, steps) * width, width), width)
    extra = level_rows(visits, bands)

    def fill(out_ref):
        line = lax.broadcasted_iota(jnp.int32, (extra, LANES), 0)
        levels = jnp.zeros((extra, LANES), F32)
        for v in range(visits):
            for b in range(bands):
                at = slice(v * rows + b * high, v * rows + (b + 1) * high)
                covers = jnp.where(cover_ref[b, v] != 0, 7, 0)
                usable = jnp.bitwise_and(bits_ref[at, :], 7) < covers
                out_ref[at, lanes] = jnp.where(usable, 1.0, 0.0).astype(BF16)
                left = 1.0 / jnp.full((8, LANES), var_ref[b, v], F32)
                for k in range(3):
                    part = left.astype(BF16).astype(F32)
                    left = left - part
                    spot = (k * bands + b) * visits + v
                    levels = jnp.where(line == spot, part[:1], levels)
        wide = jnp.concatenate([levels.astype(BF16)] * (width // LANES), axis=1)
        out_ref[count:, lanes] = wide

    pl.when(half == 0)(lambda: fill(send_ref))
    pl.when(half == 1)(lambda: fill(keep_ref))


def pixel_weights(badbits, coverage, variance, side):
    visits, rows, columns = badbits.shape
    bands = coverage.shape[1]
    (bits,) = away(badbits.reshape(visits * rows, columns))
    width = columns // 2
    tile = width
    count = width // tile
    shape = held((visits * rows + level_rows(visits, bands), width), BF16)

    def block(i, s):
        first = i < count
        return 0, jnp.where(first, (1 - s[0]) * count + i, s[0] * count + i - count)

    return pl.pallas_call(
        functools.partial(weight_kernel, visits, bands),
        out_shape=(shape, shape),
        grid_spec=pltpu.PrefetchScalarGridSpec(
            num_scalar_prefetch=1,
            grid=(2 * count,),
            in_specs=[
                whole(pltpu.SMEM),
                whole(pltpu.SMEM),
                pl.BlockSpec((visits * rows, tile), block),
            ],
            out_specs=(whole(), whole()),
        ),
        compiler_params=LIMIT,
        name="weights",
    )(side, *away(coverage.T, variance.T), bits)


def split(value):
    high = value.astype(BF16)
    return high, (value - high.astype(F32)).astype(BF16)


def edge_segments(visits, rows, half, below):
    main = half // 8 * 8
    rest = half - main
    origin = half + rows if below else 0
    segments = []
    for v in range(visits):
        first = main + v * rest
        segments.append([(0, main, origin), (first, first + rest, origin + main - first)])
    return segments, main + visits * rest


def table_kernel(visits, rows, half, index_ref, table_ref, row_ref, col_ref, column_out, own_out, above_out, below_out):
    bases, taps = row_ref.shape
    window = 2 * LANES

    def spread(line, shift, count):
        line = jnp.broadcast_to(line, (8, LANES))
        block = pltpu.roll(line, 0, 1, stride=1, stride_axis=0)
        blocks = [pltpu.roll(block, (shift + i) % LANES, 1) for i in range(0, count, 8)]
        return jnp.concatenate(blocks, axis=0)

    tap = lax.broadcasted_iota(jnp.int32, (taps, LANES), 0)
    place = lane_index((taps, LANES))
    ahead = jnp.where(place == tap, 1.0, 0.0).astype(BF16)
    back = jnp.where(place == taps - 1 - tap, 1.0, 0.0).astype(BF16)
    row_lines = jnp.dot(row_ref[...], ahead, preferred_element_type=F32)
    col_lines = jnp.dot(col_ref[...], back, preferred_element_type=F32)
    k = lax.broadcasted_iota(jnp.int32, (window, LANES), 0)
    gap = k - lane_index((window, LANES))
    inside = (gap >= 0) & (gap < LANES)
    for b in range(bases):
        line = col_lines[b : b + 1, :]
        band = jnp.where(inside, spread(line, SHIFT - half, window), 0.0)
        column_out[:, b * LANES : (b + 1) * LANES] = band.astype(BF16)

    lane = lane_index((rows, LANES))

    def assemble(out_ref, high, segments):
        for b in range(bases):
            start = b * high % LANES
            group = b * high // LANES * LANES
            line = row_lines[b : b + 1, :]
            found = {}
            for v in range(visits):
                total = jnp.zeros((rows, LANES), F32)
                for first, last, offset in segments[v]:
                    if first == last:
                        continue
                    key = (first, last, offset)
                    if key not in found:
                        mask = (lane >= start + first) & (lane < start + last)
                        found[key] = jnp.where(mask, spread(line, start - offset, rows), 0.0)
                    total = total + found[key]
                top, low = split(total * table_ref[b, index_ref[v]])
                at = 2 * v * rows
                lanes = slice(group, group + LANES)
                if start == 0:
                    out_ref[at : at + rows, lanes] = top
                    out_ref[at + rows : at + 2 * rows, lanes] = low
                else:
                    out_ref[at : at + rows, lanes] += top
                    out_ref[at + rows : at + 2 * rows, lanes] += low

    assemble(own_out, rows, [[(0, rows, half)]] * visits)
    for below, out in enumerate((above_out, below_out)):
        segments, high = edge_segments(visits, rows, half, below)
        assemble(out, high, segments)


def tables(psf_index, psf_table, row_basis, col_basis, visits, rows):
    bases, taps = row_basis.shape
    half = taps // 2
    rim = (2 * visits * rows, bases * edge_segments(visits, rows, half, 0)[1])
    return pl.pallas_call(
        functools.partial(table_kernel, visits, rows, half),
        out_shape=(
            held((2 * LANES, bases * LANES), BF16),
            held((2 * visits * rows, bases * rows), BF16),
            held(rim, BF16),
            held(rim, BF16),
        ),
        in_specs=[whole(pltpu.SMEM)] * 2 + [whole()] * 2,
        out_specs=(whole(),) * 4,
        compiler_params=LIMIT,
        name="tables",
    )(psf_index, psf_table.T, row_basis, col_basis)


BLOCKS = 4


def column_pass(windows, column_ref):
    return jnp.dot(
        jnp.concatenate(windows, axis=0), column_ref[...], preferred_element_type=F32
    )


def row_pass(layers, count, row_ref, pieces, bases):
    high = row_ref.shape[0] // (2 * len(pieces))
    for first in range(0, layers.shape[0] // count, 2):
        totals = []
        for v, parts in enumerate(pieces):
            sides = []
            for n in (first, first + 1):
                taken = [
                    layers[n * count + top : n * count + last, b * LANES : (b + 1) * LANES]
                    for b in range(bases)
                    for top, last in parts
                    if last > top
                ]
                sides.append(jnp.concatenate(taken, axis=0).astype(BF16))
            total = jnp.dot(
                row_ref[2 * v * high : 2 * (v + 1) * high, :],
                jnp.concatenate(sides, axis=1),
                preferred_element_type=F32,
            )
            totals.append(total[:high] + total[high:])
        yield first, totals


def convolve(make_group, shifted, column_ref, row_ref, pieces, put):
    count = shifted.shape[0]
    groups = shifted.shape[1] // LANES - 1
    bases = column_ref.shape[1] // LANES
    blocks = min(BLOCKS, groups)
    made = [0]

    def columns_of(step):
        while made[0] <= blocks * (step + 1):
            g = made[0]
            shifted[:, g * LANES : (g + 1) * LANES] = make_group(g)
            made[0] += 1
        starts = [(blocks * step + n) * LANES for n in range(blocks)]
        return column_pass([shifted[:, at : at + 2 * LANES] for at in starts], column_ref)

    ahead = columns_of(0)
    for step in range(groups // blocks):
        layers = ahead
        if step + 1 < groups // blocks:
            ahead = columns_of(step + 1)
        for first, totals in row_pass(layers, count, row_ref, pieces, bases):
            put((blocks * step + first) * LANES, totals)


def own_kernel(visits, upper_ref, lower_ref, column_ref, row_ref, out_ref, shifted):
    half_count, columns = upper_ref.shape
    depth = half_count // visits
    rows = 2 * depth
    groups = columns // LANES
    low = lane_index((2 * half_count, LANES)) < SHIFT
    nothing = jnp.zeros((2 * half_count, LANES), F32)
    turned = {-1: nothing, groups: nothing}

    def turn(g):
        if g not in turned:
            lanes = slice(g * LANES, (g + 1) * LANES)
            value = jnp.concatenate([upper_ref[:, lanes], lower_ref[:, lanes]], axis=0)
            turned[g] = pltpu.roll(value.astype(F32), SHIFT, 1)
        return turned[g]

    def make_group(g):
        return jnp.where(low, turn(g - 1), turn(g)).astype(BF16)

    pieces = [
        [(place * half_count + v * depth, place * half_count + (v + 1) * depth) for place in (0, 1)]
        for v in range(visits)
    ]

    def put(start, totals):
        for v, total in enumerate(totals):
            out_ref[v * rows : (v + 1) * rows, start : start + 2 * LANES] = total

    convolve(make_group, shifted, column_ref, row_ref, pieces, put)


def own_part(upper, lower, column, own, visits):
    half_count, columns = upper.shape
    return pl.pallas_call(
        functools.partial(own_kernel, visits),
        out_shape=held((2 * half_count, columns), F32),
        in_specs=[whole()] * 4,
        out_specs=whole(),
        scratch_shapes=[pltpu.VMEM((2 * half_count, columns + LANES), BF16)],
        compiler_params=LIMIT,
        cost_estimate=pl.CostEstimate(flops=10**9, bytes_accessed=10**7, transcendentals=0),
        name="own_rows",
    )(*kept(upper, lower, column, own))


def rim_kernel(visits, half, side_ref, edge_ref, column_ref, row_ref, part_ref, out_ref, shifted):
    edge, columns = edge_ref.shape
    rows = out_ref.shape[0] // visits
    width = out_ref.shape[1]
    groups = columns // LANES
    inner = width // LANES
    base = side_ref[0] * inner if width < columns else 0
    lane = lane_index((edge, LANES))

    def make_group(g):
        at = base + g
        lanes = pl.ds(pl.multiple_of(lax.rem(at, groups) * LANES, LANES), LANES)
        value = edge_ref[:, lanes]
        if g == 0:
            value = value.astype(F32)
            value = jnp.where(lane >= jnp.where(at == 0, SHIFT, 0), value, 0.0).astype(BF16)
        if g == inner:
            value = value.astype(F32)
            value = jnp.where(lane < jnp.where(at == groups, SHIFT, LANES), value, 0.0)
            value = value.astype(BF16)
        return value

    main = half // 8 * 8
    pieces = [[(v * main, (v + 1) * main), (visits * main, edge)] for v in range(visits)]

    def put(start, totals):
        source = pl.ds(pl.multiple_of(base * LANES + start, 2 * LANES), 2 * LANES)
        for v, total in enumerate(totals):
            lines = slice(v * rows, (v + 1) * rows)
            value = (total + part_ref[lines, source]).astype(out_ref.dtype)
            out_ref[lines, start : start + 2 * LANES] = value

    convolve(make_group, shifted, column_ref, row_ref, pieces, put)


def rim_part(side, edge, column, table, part, visits, half, width, dtype):
    count = part.shape[0]
    return pl.pallas_call(
        functools.partial(rim_kernel, visits, half),
        out_shape=held((count, width), dtype),
        in_specs=[whole(pltpu.SMEM)] + [whole()] * 4,
        out_specs=whole(),
        scratch_shapes=[pltpu.VMEM((edge.shape[0], width + LANES), BF16)],
        compiler_params=LIMIT,
    )(side, *kept(edge, column, table, part))


def residual_kernel(visits, bands, *refs):
    value_refs, weight_refs = refs[0:2], refs[2:4]
    factor_ref, sums_ref, chi_ref, count_ref = refs[4:]
    rows = value_refs[0].shape[0] // visits
    width = value_refs[0].shape[1]
    high = min(16, rows // bands)
    chi_ref[...] = jnp.zeros_like(chi_ref)
    count_ref[...] = jnp.zeros_like(count_ref)

    def folded(value):
        total = value[:8]
        for start in range(8, high, 8):
            total = total + value[start : start + 8]
        return total

    members = [(side, v) for side in range(2) for v in range(visits)]
    count = value_refs[0].shape[0]
    levels = {}
    for side in range(2):
        found = weight_refs[side][count:, :LANES].astype(F32)
        for v in range(visits):
            for b in range(bands):
                spots = [(k * bands + b) * visits + v for k in range(3)]
                parts = [found[spot : spot + 1] for spot in spots]
                level = (parts[0] + parts[1]) + parts[2]
                levels[side, v, b] = jnp.broadcast_to(level, (high, LANES))

    def body(step, carry):
        lanes = pl.ds(pl.multiple_of(step * LANES, LANES), LANES)
        for row in range(0, rows, high):
            band = row // (rows // bands)
            values, weights, flags = [], [], []
            numer = denom = None
            for side, v in members:
                at = slice(v * rows + row, v * rows + row + high)
                value = value_refs[side][at, lanes].astype(F32)
                flag = weight_refs[side][at, lanes].astype(F32)
                weight = flag * levels[side, v, band]
                flags.append(flag)
                values.append(value)
                weights.append(weight)
                numer = weight * value if numer is None else numer + weight * value
                denom = weight if denom is None else denom + weight
            first = numer / (denom + PRIOR_WEIGHT)
            for m, (side, v) in enumerate(members):
                residual = values[m] - first
                term = weights[m] * (residual * residual)
                at = slice(m * 8, (m + 1) * 8)
                chi_ref[at, :] += folded(term)
                count_ref[at, :] += folded(flags[m])
                target = slice(m * rows + row, m * rows + row + high)
                factor_ref[target, lanes] = weights[m] / (1.0 + term / CLIP_LEVEL)
        return carry

    lax.fori_loop(0, width // LANES, body, 0, unroll=4)
    for m in range(len(members)):
        at = slice(m * 8, (m + 1) * 8)
        sums_ref[0, m : m + 1, :] = jnp.sum(chi_ref[at, :], axis=0, keepdims=True)
        sums_ref[1, m : m + 1, :] = jnp.sum(count_ref[at, :], axis=0, keepdims=True)


def residual_pass(values, weights, visits, bands):
    count, width = values[0].shape
    members = 2 * visits
    return pl.pallas_call(
        functools.partial(residual_kernel, visits, bands),
        out_shape=(held((2 * count, width), F32), held((2, members, LANES), F32)),
        in_specs=[whole()] * 4,
        out_specs=(whole(), whole()),
        scratch_shapes=[pltpu.VMEM((members * 8, LANES), F32)] * 2,
        compiler_params=LIMIT,
        name="residual",
    )(*kept(*values, *weights))


def final_kernel(visits, sums_ref, own_ref, other_ref, factor_ref, out_ref, chi_ref, done, sent):
    rows, width = done.shape
    chunks = sent.shape[0]
    high = min(16, rows)
    chi = jnp.sum(sums_ref[0], axis=1, keepdims=True) / jnp.sum(
        sums_ref[1], axis=1, keepdims=True
    )
    scale = 1.0 / (CHI_OFFSET + chi)
    for v in range(visits):
        chi_ref[v] = chi[v, 0]
    scales = [jnp.broadcast_to(scale[m : m + 1], (high, LANES)) for m in range(2 * visits)]
    copies = []
    for c in range(chunks):
        for lane in range(c * width // chunks, (c + 1) * width // chunks, LANES):
            lanes = slice(lane, lane + LANES)
            for row in range(0, rows, high):
                numer = denom = None
                for m in range(2 * visits):
                    source = own_ref if m < visits else other_ref
                    at = (m % visits) * rows + row
                    value = source[at : at + high, lanes].astype(F32)
                    at = m * rows + row
                    revised = factor_ref[at : at + high, lanes] * scales[m]
                    numer = revised * value if numer is None else numer + revised * value
                    denom = revised if denom is None else denom + revised
                done[row : row + high, lanes] = numer / (denom + PRIOR_WEIGHT)
        lanes = slice(c * width // chunks, (c + 1) * width // chunks)
        copies.append(
            pltpu.make_async_copy(done.at[:, lanes], out_ref.at[:, lanes], sent.at[c])
        )
        copies[c].start()
    for copy in copies:
        copy.wait()


def final_pass(sums, values, factors, visits):
    count, width = values[0].shape
    rows = count // visits
    chunks = 1
    return pl.pallas_call(
        functools.partial(final_kernel, visits),
        out_shape=(
            jax.ShapeDtypeStruct((rows, width), F32),
            jax.ShapeDtypeStruct((visits,), F32),
        ),
        in_specs=[whole()] * 4,
        out_specs=(pl.BlockSpec(memory_space=pl.ANY), whole(pltpu.SMEM)),
        scratch_shapes=[pltpu.VMEM((rows, width), F32), pltpu.SemaphoreType.DMA((chunks,))],
        compiler_params=LIMIT,
        name="final",
    )(*kept(sums, *values, factors))


def per_device(warps, badbits, coverage, variance, psf_index, psf_table, row_basis, col_basis):
    visits, rows, columns = warps.shape
    half = row_basis.shape[1] // 2
    strips = lax.axis_size("sky")
    up = [(i, i + 1) for i in range(strips - 1)]
    down = [(j, i) for i, j in up]
    swap = [(0, 1), (1, 0)]
    side = lax.axis_index("visit").astype(jnp.int32).reshape(1)

    last, lower = pack_rows(warps, half, False)
    before = lax.ppermute(last, "sky", up)
    send_weight, own_weight = pixel_weights(badbits, coverage, variance, side)
    other_weight = lax.ppermute(send_weight, "visit", swap)
    column, own, above, below = tables(psf_index, psf_table, row_basis, col_basis, visits, rows)
    leading, upper = pack_rows(warps, half, True, send_weight)
    after = lax.ppermute(leading, "sky", down)
    part = own_part(upper.reshape(-1, columns), lower.reshape(-1, columns), column, own, visits)
    part = rim_part(side, before, column, above, part, visits, half, columns, F32)
    send_value = rim_part(1 - side, after, column, below, part, visits, half, columns // 2, BF16)
    other_value = lax.ppermute(send_value, "visit", swap)
    own_value = rim_part(side, after, column, below, part, visits, half, columns // 2, BF16)
    values = (own_value, other_value)
    factors, sums = residual_pass(values, (own_weight, other_weight), visits, coverage.shape[1])
    theirs = lax.ppermute(sums, "visit", swap)
    sums = sums + jnp.concatenate([theirs[:, visits:], theirs[:, :visits]], axis=1)
    step = 1
    while step < strips:
        sums = sums + lax.ppermute(sums, "sky", [(i, i ^ step) for i in range(strips)])
        step *= 2
    return final_pass(sums, values, factors, visits)


def solution(mesh):
    placed = (
        P(("tract", "visit"), "sky", None),
        P(("tract", "visit"), "sky", None),
        P(("tract", "visit"), "sky"),
        P(("tract", "visit"), "sky"),
        P(("tract", "visit")),
        P(),
        P(),
        P(),
    )
    return jax.shard_map(
        per_device,
        mesh=mesh,
        in_specs=placed,
        out_specs=(P(("tract", "sky"), "visit"), P(("tract", "visit"))),
        check_vma=False,
    )
```

```python
import functools

import jax
import jax.numpy as jnp
from jax import lax
from jax.experimental import pallas as pl
from jax.experimental.pallas import tpu as pltpu
from jax.sharding import PartitionSpec as P

PRIOR_WEIGHT = 1.0
CLIP_LEVEL = 9.0
CHI_OFFSET = 0.5
LANES = 128
SHIFT = LANES // 2
F32 = jnp.float32
BF16 = jnp.bfloat16


def whole(space=pltpu.VMEM):
    return pl.BlockSpec(memory_space=space)


def kept(*arrays):
    return [pltpu.with_memory_space_constraint(array, pltpu.VMEM) for array in arrays]


def away(*arrays):
    return [pltpu.with_memory_space_constraint(array, pltpu.HBM) for array in arrays]


def held(shape, dtype):
    return pltpu.VMEM(shape, dtype)


LIMIT = pltpu.CompilerParams(vmem_limit_bytes=20 * 1024 * 1024)


def lane_index(shape):
    return lax.broadcasted_iota(jnp.int32, shape, len(shape) - 1)


def pack_kernel(half, first, skip, x_ref, *refs):
    edge_ref, rows_ref, arrived = refs[-3:]
    visits, depth, columns = rows_ref.shape
    chunks = arrived.shape[0]
    width = columns // chunks
    copies = []
    for c in range(chunks):
        lanes = slice(c * width, (c + 1) * width)
        copies.append(
            pltpu.make_async_copy(
                x_ref.at[:, first : first + depth, lanes], rows_ref.at[:, :, lanes], arrived.at[c]
            )
        )
        copies[c].start()
    main = half // 8 * 8
    rest = half - main
    shape = (visits * half, visits * depth)
    target = lax.broadcasted_iota(jnp.int32, shape, 0)
    source_row = lane_index(shape)
    line = jnp.where(
        target < visits * main,
        lax.div(target, max(main, 1)) * depth + lax.rem(target, max(main, 1)),
        lax.div(target - visits * main, max(rest, 1)) * depth
        + main
        + lax.rem(target - visits * main, max(rest, 1)),
    )
    select = jnp.where(source_row == line + skip, 1.0, 0.0).astype(BF16)
    low = lane_index((edge_ref.shape[0], LANES)) < SHIFT
    step = 2 * LANES

    def put(g, value):
        edge_ref[:, g * LANES : (g + 1) * LANES] = value.astype(BF16)

    before = opening = None
    for start in range(0, columns, step):
        if start % width == 0:
            copies[start // width].wait()
        source = rows_ref[:, :, start : start + step].reshape(visits * depth, step)
        found = jnp.dot(select, source, preferred_element_type=F32)
        for part in range(2):
            here = pltpu.roll(found[:, part * LANES : (part + 1) * LANES], SHIFT, 1)
            if before is None:
                opening = here
            else:
                put(start // LANES + part, jnp.where(low, before, here))
            before = here
    put(0, jnp.where(low, before, opening))


def pack_rows(warps, half, upper, *after):
    visits, rows, columns = warps.shape
    depth = rows // 2
    assert depth >= half and rows % 2 == 0
    first = 0 if upper else depth
    skip = 0 if upper else depth - half
    chunks = 1
    return pl.pallas_call(
        functools.partial(pack_kernel, half, first, skip),
        out_shape=(held((visits * half, columns), BF16), held((visits, depth, columns), BF16)),
        in_specs=[pl.BlockSpec(memory_space=pl.ANY)] * (1 + len(after)),
        out_specs=(whole(),) * 2,
        scratch_shapes=[pltpu.SemaphoreType.DMA((chunks,))],
        compiler_params=LIMIT,
        name="pack_upper" if upper else "pack_lower",
    )(*away(warps), *after)


def level_rows(visits, bands):
    return -(-3 * visits * bands // 16) * 16


def weight_kernel(visits, bands, side_ref, cover_ref, var_ref, bits_ref, send_ref, keep_ref):
    count = bits_ref.shape[0]
    rows = count // visits
    high = rows // bands
    width = bits_ref.shape[1]
    steps = send_ref.shape[1] // width
    step = pl.program_id(0)
    half = lax.div(step, steps)
    lanes = pl.ds(pl.multiple_of(lax.rem(step, steps) * width, width), width)
    extra = level_rows(visits, bands)

    def fill(out_ref):
        line = lax.broadcasted_iota(jnp.int32, (extra, LANES), 0)
        levels = jnp.zeros((extra, LANES), F32)
        for v in range(visits):
            for b in range(bands):
                at = slice(v * rows + b * high, v * rows + (b + 1) * high)
                covers = jnp.where(cover_ref[b, v] != 0, 7, 0)
                usable = jnp.bitwise_and(bits_ref[at, :], 7) < covers
                out_ref[at, lanes] = jnp.where(usable, 1.0, 0.0).astype(BF16)
                left = 1.0 / jnp.full((8, LANES), var_ref[b, v], F32)
                for k in range(3):
                    part = left.astype(BF16).astype(F32)
                    left = left - part
                    spot = (k * bands + b) * visits + v
                    levels = jnp.where(line == spot, part[:1], levels)
        wide = jnp.concatenate([levels.astype(BF16)] * (width // LANES), axis=1)
        out_ref[count:, lanes] = wide

    pl.when(half == 0)(lambda: fill(send_ref))
    pl.when(half == 1)(lambda: fill(keep_ref))


def pixel_weights(badbits, coverage, variance, side):
    visits, rows, columns = badbits.shape
    bands = coverage.shape[1]
    (bits,) = away(badbits.reshape(visits * rows, columns))
    width = columns // 2
    tile = width
    count = width // tile
    shape = held((visits * rows + level_rows(visits, bands), width), BF16)

    def block(i, s):
        first = i < count
        return 0, jnp.where(first, (1 - s[0]) * count + i, s[0] * count + i - count)

    return pl.pallas_call(
        functools.partial(weight_kernel, visits, bands),
        out_shape=(shape, shape),
        grid_spec=pltpu.PrefetchScalarGridSpec(
            num_scalar_prefetch=1,
            grid=(2 * count,),
            in_specs=[
                whole(pltpu.SMEM),
                whole(pltpu.SMEM),
                pl.BlockSpec((visits * rows, tile), block),
            ],
            out_specs=(whole(), whole()),
        ),
        compiler_params=LIMIT,
        name="weights",
    )(side, *away(coverage.T, variance.T), bits)


def split(value):
    high = value.astype(BF16)
    return high, (value - high.astype(F32)).astype(BF16)


def edge_segments(visits, rows, half, below):
    main = half // 8 * 8
    rest = half - main
    origin = half + rows if below else 0
    segments = []
    for v in range(visits):
        first = main + v * rest
        segments.append([(0, main, origin), (first, first + rest, origin + main - first)])
    return segments, main + visits * rest


def table_kernel(visits, rows, half, index_ref, table_ref, row_ref, col_ref, after_ref, column_out, own_out, above_out, below_out):
    bases, taps = row_ref.shape
    window = 2 * LANES

    def spread(line, shift, count):
        line = jnp.broadcast_to(line, (8, LANES))
        block = pltpu.roll(line, 0, 1, stride=1, stride_axis=0)
        blocks = [pltpu.roll(block, (shift + i) % LANES, 1) for i in range(0, count, 8)]
        return jnp.concatenate(blocks, axis=0)

    tap = lax.broadcasted_iota(jnp.int32, (taps, LANES), 0)
    place = lane_index((taps, LANES))
    ahead = jnp.where(place == tap, 1.0, 0.0).astype(BF16)
    back = jnp.where(place == taps - 1 - tap, 1.0, 0.0).astype(BF16)
    row_lines = jnp.dot(row_ref[...], ahead, preferred_element_type=F32)
    col_lines = jnp.dot(col_ref[...], back, preferred_element_type=F32)
    k = lax.broadcasted_iota(jnp.int32, (window, LANES), 0)
    gap = k - lane_index((window, LANES))
    inside = (gap >= 0) & (gap < LANES)
    for b in range(bases):
        line = col_lines[b : b + 1, :]
        band = jnp.where(inside, spread(line, SHIFT - half, window), 0.0)
        column_out[:, b * LANES : (b + 1) * LANES] = band.astype(BF16)

    lane = lane_index((rows, LANES))

    def assemble(out_ref, high, segments):
        for b in range(bases):
            start = b * high % LANES
            group = b * high // LANES * LANES
            line = row_lines[b : b + 1, :]
            found = {}
            for v in range(visits):
                total = jnp.zeros((rows, LANES), F32)
                for first, last, offset in segments[v]:
                    if first == last:
                        continue
                    key = (first, last, offset)
                    if key not in found:
                        mask = (lane >= start + first) & (lane < start + last)
                        found[key] = jnp.where(mask, spread(line, start - offset, rows), 0.0)
                    total = total + found[key]
                top, low = split(total * table_ref[b, index_ref[v]])
                at = 2 * v * rows
                lanes = slice(group, group + LANES)
                if start == 0:
                    out_ref[at : at + rows, lanes] = top
                    out_ref[at + rows : at + 2 * rows, lanes] = low
                else:
                    out_ref[at : at + rows, lanes] += top
                    out_ref[at + rows : at + 2 * rows, lanes] += low

    assemble(own_out, rows, [[(0, rows, half)]] * visits)
    for below, out in enumerate((above_out, below_out)):
        segments, high = edge_segments(visits, rows, half, below)
        assemble(out, high, segments)


def tables(psf_index, psf_table, row_basis, col_basis, visits, rows, after):
    bases, taps = row_basis.shape
    half = taps // 2
    rim = (2 * visits * rows, bases * edge_segments(visits, rows, half, 0)[1])
    return pl.pallas_call(
        functools.partial(table_kernel, visits, rows, half),
        out_shape=(
            held((2 * LANES, bases * LANES), BF16),
            held((2 * visits * rows, bases * rows), BF16),
            held(rim, BF16),
            held(rim, BF16),
        ),
        in_specs=[whole(pltpu.SMEM)] * 2 + [whole()] * 2 + [pl.BlockSpec(memory_space=pl.ANY)],
        out_specs=(whole(),) * 4,
        compiler_params=LIMIT,
        name="tables",
    )(psf_index, psf_table.T, row_basis, col_basis, after)


BLOCKS = 4


def column_pass(windows, column_ref):
    return jnp.dot(
        jnp.concatenate(windows, axis=0), column_ref[...], preferred_element_type=F32
    )


def row_pass(layers, count, row_ref, pieces, bases):
    high = row_ref.shape[0] // (2 * len(pieces))
    for first in range(0, layers.shape[0] // count, 2):
        totals = []
        for v, parts in enumerate(pieces):
            sides = []
            for n in (first, first + 1):
                taken = [
                    layers[n * count + top : n * count + last, b * LANES : (b + 1) * LANES]
                    for b in range(bases)
                    for top, last in parts
                    if last > top
                ]
                sides.append(jnp.concatenate(taken, axis=0).astype(BF16))
            total = jnp.dot(
                row_ref[2 * v * high : 2 * (v + 1) * high, :],
                jnp.concatenate(sides, axis=1),
                preferred_element_type=F32,
            )
            totals.append(total[:high] + total[high:])
        yield first, totals


def convolve(make_group, shifted, column_ref, row_ref, pieces, put):
    count = shifted.shape[0]
    groups = shifted.shape[1] // LANES - 1
    bases = column_ref.shape[1] // LANES
    blocks = min(BLOCKS, groups)
    made = [0]

    def columns_of(step):
        while made[0] <= blocks * (step + 1):
            g = made[0]
            shifted[:, g * LANES : (g + 1) * LANES] = make_group(g)
            made[0] += 1
        starts = [(blocks * step + n) * LANES for n in range(blocks)]
        return column_pass([shifted[:, at : at + 2 * LANES] for at in starts], column_ref)

    ahead = columns_of(0)
    for step in range(groups // blocks):
        layers = ahead
        if step + 1 < groups // blocks:
            ahead = columns_of(step + 1)
        for first, totals in row_pass(layers, count, row_ref, pieces, bases):
            put((blocks * step + first) * LANES, totals)


def own_kernel(visits, upper_ref, lower_ref, column_ref, row_ref, out_ref, shifted):
    half_count, columns = upper_ref.shape
    depth = half_count // visits
    rows = 2 * depth
    groups = columns // LANES
    low = lane_index((2 * half_count, LANES)) < SHIFT
    nothing = jnp.zeros((2 * half_count, LANES), F32)
    turned = {-1: nothing, groups: nothing}

    def turn(g):
        if g not in turned:
            lanes = slice(g * LANES, (g + 1) * LANES)
            value = jnp.concatenate([upper_ref[:, lanes], lower_ref[:, lanes]], axis=0)
            turned[g] = pltpu.roll(value.astype(F32), SHIFT, 1)
        return turned[g]

    def make_group(g):
        return jnp.where(low, turn(g - 1), turn(g)).astype(BF16)

    pieces = [
        [(place * half_count + v * depth, place * half_count + (v + 1) * depth) for place in (0, 1)]
        for v in range(visits)
    ]

    def put(start, totals):
        for v, total in enumerate(totals):
            out_ref[v * rows : (v + 1) * rows, start : start + 2 * LANES] = total

    convolve(make_group, shifted, column_ref, row_ref, pieces, put)


def own_part(upper, lower, column, own, visits):
    half_count, columns = upper.shape
    return pl.pallas_call(
        functools.partial(own_kernel, visits),
        out_shape=held((2 * half_count, columns), F32),
        in_specs=[whole()] * 4,
        out_specs=whole(),
        scratch_shapes=[pltpu.VMEM((2 * half_count, columns + LANES), BF16)],
        compiler_params=LIMIT,
        cost_estimate=pl.CostEstimate(flops=10**9, bytes_accessed=10**7, transcendentals=0),
        name="own_rows",
    )(*kept(upper, lower, column, own))


def rim_kernel(visits, half, side_ref, edge_ref, column_ref, row_ref, part_ref, out_ref, shifted):
    edge, columns = edge_ref.shape
    rows = out_ref.shape[0] // visits
    width = out_ref.shape[1]
    groups = columns // LANES
    inner = width // LANES
    base = side_ref[0] * inner if width < columns else 0
    lane = lane_index((edge, LANES))

    def make_group(g):
        at = base + g
        lanes = pl.ds(pl.multiple_of(lax.rem(at, groups) * LANES, LANES), LANES)
        value = edge_ref[:, lanes]
        if g == 0:
            value = value.astype(F32)
            value = jnp.where(lane >= jnp.where(at == 0, SHIFT, 0), value, 0.0).astype(BF16)
        if g == inner:
            value = value.astype(F32)
            value = jnp.where(lane < jnp.where(at == groups, SHIFT, LANES), value, 0.0)
            value = value.astype(BF16)
        return value

    main = half // 8 * 8
    pieces = [[(v * main, (v + 1) * main), (visits * main, edge)] for v in range(visits)]

    def put(start, totals):
        source = pl.ds(pl.multiple_of(base * LANES + start, 2 * LANES), 2 * LANES)
        for v, total in enumerate(totals):
            lines = slice(v * rows, (v + 1) * rows)
            value = (total + part_ref[lines, source]).astype(out_ref.dtype)
            out_ref[lines, start : start + 2 * LANES] = value

    convolve(make_group, shifted, column_ref, row_ref, pieces, put)


def rim_part(side, edge, column, table, part, visits, half, width, dtype):
    count = part.shape[0]
    return pl.pallas_call(
        functools.partial(rim_kernel, visits, half),
        out_shape=held((count, width), dtype),
        in_specs=[whole(pltpu.SMEM)] + [whole()] * 4,
        out_specs=whole(),
        scratch_shapes=[pltpu.VMEM((edge.shape[0], width + LANES), BF16)],
        compiler_params=LIMIT,
    )(side, *kept(edge, column, table, part))


def norm_kernel(visits, bands, *refs):
    flag_refs = refs[:2]
    weight_ref, inverse_ref, count_ref = refs[2:]
    rows, width = inverse_ref.shape
    count = visits * rows
    high = min(16, rows // bands)
    members = [(side, v) for side in range(2) for v in range(visits)]
    levels = {}
    for side in range(2):
        found = flag_refs[side][count:, :LANES].astype(F32)
        for v in range(visits):
            for b in range(bands):
                spots = [(k * bands + b) * visits + v for k in range(3)]
                parts = [found[spot : spot + 1] for spot in spots]
                level = (parts[0] + parts[1]) + parts[2]
                levels[side, v, b] = jnp.broadcast_to(level, (high, LANES))
    count_ref[...] = jnp.zeros_like(count_ref)

    def body(step, carry):
        lanes = pl.ds(pl.multiple_of(step * LANES, LANES), LANES)
        for row in range(0, rows, high):
            denom = PRIOR_WEIGHT
            for m, (side, v) in enumerate(members):
                flag = flag_refs[side][v * rows + row : v * rows + row + high, lanes].astype(F32)
                weight = flag * levels[side, v, row // (rows // bands)]
                weight_ref[m * rows + row : m * rows + row + high, lanes] = weight
                count_ref[m * 8 : (m + 1) * 8, :] += folded(flag)
                denom = denom + weight
            inverse_ref[row : row + high, lanes] = 1.0 / denom
        return carry

    lax.fori_loop(0, width // LANES, body, 0, unroll=4)


def folded(value):
    total = value[:8]
    for start in range(8, value.shape[0], 8):
        total = total + value[start : start + 8]
    return total


def norms(own_flags, other_flags, visits, bands, rows):
    width = own_flags.shape[1]
    members = 2 * visits
    return pl.pallas_call(
        functools.partial(norm_kernel, visits, bands),
        out_shape=(
            held((members * rows, width), F32),
            held((rows, width), F32),
            held((members * 8, LANES), F32),
        ),
        in_specs=[whole()] * 2,
        out_specs=(whole(),) * 3,
        compiler_params=LIMIT,
        name="norms",
    )(*kept(own_flags, other_flags))


def residual_kernel(visits, side_ref, *refs):
    value_refs = refs[:2]
    weight_ref, inverse_ref, count_ref, factor_ref, sums_ref, chi_ref = refs[2:]
    rows, width = inverse_ref.shape
    high = min(16, rows)
    chi_ref[...] = jnp.zeros_like(chi_ref)
    members = [(side, v) for side in range(2) for v in range(visits)]

    def body(step, carry):
        lanes = pl.ds(pl.multiple_of(step * LANES, LANES), LANES)
        for row in range(0, rows, high):
            values, weights = [], []
            numer = None
            for m, (side, v) in enumerate(members):
                at = slice(v * rows + row, v * rows + row + high)
                value = value_refs[side][at, lanes].astype(F32)
                weight = weight_ref[m * rows + row : m * rows + row + high, lanes]
                values.append(value)
                weights.append(weight)
                numer = weight * value if numer is None else numer + weight * value
            first = numer * inverse_ref[row : row + high, lanes]
            for m in range(len(members)):
                residual = values[m] - first
                term = weights[m] * (residual * residual)
                chi_ref[m * 8 : (m + 1) * 8, :] += folded(term)
                target = slice(m * rows + row, m * rows + row + high)
                factor_ref[target, lanes] = weights[m] / (CLIP_LEVEL + term)
        return carry

    lax.fori_loop(0, width // LANES, body, 0, unroll=4)
    for k, ref in enumerate((chi_ref, count_ref)):
        lines = [
            jnp.sum(ref[m * 8 : (m + 1) * 8, :], axis=0, keepdims=True)
            for m in range(len(members))
        ]
        total = jnp.concatenate(lines, axis=0)
        sums_ref[k] = jnp.where(side_ref[0] == 0, total, pltpu.roll(total, visits, 0))


def residual_pass(side, values, weights, inverse, counts, visits):
    rows, width = inverse.shape
    members = 2 * visits
    return pl.pallas_call(
        functools.partial(residual_kernel, visits),
        out_shape=(held((members * rows, width), F32), held((2, members, LANES), F32)),
        in_specs=[whole(pltpu.SMEM)] + [whole()] * 5,
        out_specs=(whole(), whole()),
        scratch_shapes=[pltpu.VMEM((members * 8, LANES), F32)],
        compiler_params=LIMIT,
        name="residual",
    )(side, *kept(*values, weights, inverse, counts))


def final_kernel(visits, side_ref, sums_ref, own_ref, other_ref, factor_ref, out_ref, chi_ref, done, sent):
    rows, width = done.shape
    high = min(16, rows)
    sums = [
        jnp.where(side_ref[0] == 0, sums_ref[k], pltpu.roll(sums_ref[k], visits, 0))
        for k in range(2)
    ]
    chi = jnp.sum(sums[0], axis=1, keepdims=True) / jnp.sum(sums[1], axis=1, keepdims=True)
    scale = CLIP_LEVEL / (CHI_OFFSET + chi)
    for v in range(visits):
        chi_ref[v] = chi[v, 0]
    scales = [jnp.broadcast_to(scale[m : m + 1], (high, LANES)) for m in range(2 * visits)]
    for lane in range(0, width, LANES):
        lanes = slice(lane, lane + LANES)
        for row in range(0, rows, high):
            numer = denom = None
            for m in range(2 * visits):
                source = own_ref if m < visits else other_ref
                at = (m % visits) * rows + row
                value = source[at : at + high, lanes].astype(F32)
                at = m * rows + row
                revised = factor_ref[at : at + high, lanes] * scales[m]
                numer = revised * value if numer is None else numer + revised * value
                denom = revised if denom is None else denom + revised
            done[row : row + high, lanes] = numer / (denom + PRIOR_WEIGHT)
    copy = pltpu.make_async_copy(done, out_ref, sent)
    copy.start()
    copy.wait()


def final_pass(side, sums, values, factors, visits):
    count, width = values[0].shape
    rows = count // visits
    return pl.pallas_call(
        functools.partial(final_kernel, visits),
        out_shape=(
            jax.ShapeDtypeStruct((rows, width), F32),
            jax.ShapeDtypeStruct((visits,), F32),
        ),
        in_specs=[whole(pltpu.SMEM)] + [whole()] * 4,
        out_specs=(pl.BlockSpec(memory_space=pl.ANY), whole(pltpu.SMEM)),
        scratch_shapes=[pltpu.VMEM((rows, width), F32), pltpu.SemaphoreType.DMA(())],
        compiler_params=LIMIT,
        name="final",
    )(side, *kept(sums, *values, factors))


def per_device(warps, badbits, coverage, variance, psf_index, psf_table, row_basis, col_basis):
    visits, rows, columns = warps.shape
    half = row_basis.shape[1] // 2
    strips = lax.axis_size("sky")
    up = [(i, i + 1) for i in range(strips - 1)]
    down = [(j, i) for i, j in up]
    swap = [(0, 1), (1, 0)]
    side = lax.axis_index("visit").astype(jnp.int32).reshape(1)

    last, lower = pack_rows(warps, half, False)
    before = lax.ppermute(last, "sky", up)
    send_weight, own_weight = pixel_weights(badbits, coverage, variance, side)
    other_weight = lax.ppermute(send_weight, "visit", swap)
    column, own, above, below = tables(
        psf_index, psf_table, row_basis, col_basis, visits, rows, own_weight
    )
    leading, upper = pack_rows(warps, half, True, column)
    after = lax.ppermute(leading, "sky", down)
    part = own_part(upper.reshape(-1, columns), lower.reshape(-1, columns), column, own, visits)
    part = rim_part(side, before, column, above, part, visits, half, columns, F32)
    weights, inverse, counts = norms(own_weight, other_weight, visits, coverage.shape[1], rows)
    send_value = rim_part(1 - side, after, column, below, part, visits, half, columns // 2, BF16)
    other_value = lax.ppermute(send_value, "visit", swap)
    own_value = rim_part(side, after, column, below, part, visits, half, columns // 2, BF16)
    values = (own_value, other_value)
    factors, sums = residual_pass(side, values, weights, inverse, counts, visits)
    sums = sums + lax.ppermute(sums, "visit", swap)
    step = 1
    while step < strips:
        pairs = [(i, i ^ step) for i in range(strips)]
        if step == 1:
            pairs = [(2 * i + v, 2 * j + 1 - v) for i, j in pairs for v in (0, 1)]
            theirs = lax.ppermute(sums, ("sky", "visit"), pairs)
        else:
            theirs = lax.ppermute(sums, "sky", pairs)
        sums = sums + theirs
        step *= 2
    return final_pass(side, sums, values, factors, visits)


def solution(mesh):
    placed = (
        P(("tract", "visit"), "sky", None),
        P(("tract", "visit"), "sky", None),
        P(("tract", "visit"), "sky"),
        P(("tract", "visit"), "sky"),
        P(("tract", "visit")),
        P(),
        P(),
        P(),
    )
    return jax.shard_map(
        per_device,
        mesh=mesh,
        in_specs=placed,
        out_specs=(P(("tract", "sky"), "visit"), P(("tract", "visit"))),
        check_vma=False,
    )
```

```python
import functools

import jax
import jax.numpy as jnp
from jax import lax
from jax.experimental import pallas as pl
from jax.experimental.pallas import tpu as pltpu
from jax.sharding import PartitionSpec as P

PRIOR_WEIGHT = 1.0
CLIP_LEVEL = 9.0
CHI_OFFSET = 0.5
LANES = 128
SHIFT = LANES // 2
F32 = jnp.float32
BF16 = jnp.bfloat16


def whole(space=pltpu.VMEM):
    return pl.BlockSpec(memory_space=space)


def kept(*arrays):
    return [pltpu.with_memory_space_constraint(array, pltpu.VMEM) for array in arrays]


def away(*arrays):
    return [pltpu.with_memory_space_constraint(array, pltpu.HBM) for array in arrays]


def held(shape, dtype):
    return pltpu.VMEM(shape, dtype)


LIMIT = pltpu.CompilerParams(vmem_limit_bytes=20 * 1024 * 1024)


def lane_index(shape):
    return lax.broadcasted_iota(jnp.int32, shape, len(shape) - 1)


def pack_kernel(half, first, skip, x_ref, *refs):
    edge_ref, rows_ref, arrived = refs[-3:]
    visits, depth, columns = rows_ref.shape
    chunks = arrived.shape[0]
    width = columns // chunks
    copies = []
    for c in range(chunks):
        lanes = slice(c * width, (c + 1) * width)
        copies.append(
            pltpu.make_async_copy(
                x_ref.at[:, first : first + depth, lanes], rows_ref.at[:, :, lanes], arrived.at[c]
            )
        )
        copies[c].start()
    main = half // 8 * 8
    rest = half - main
    shape = (visits * half, visits * depth)
    target = lax.broadcasted_iota(jnp.int32, shape, 0)
    source_row = lane_index(shape)
    line = jnp.where(
        target < visits * main,
        lax.div(target, max(main, 1)) * depth + lax.rem(target, max(main, 1)),
        lax.div(target - visits * main, max(rest, 1)) * depth
        + main
        + lax.rem(target - visits * main, max(rest, 1)),
    )
    select = jnp.where(source_row == line + skip, 1.0, 0.0).astype(BF16)
    low = lane_index((edge_ref.shape[0], LANES)) < SHIFT
    step = 2 * LANES

    def put(g, value):
        edge_ref[:, g * LANES : (g + 1) * LANES] = value.astype(BF16)

    before = opening = None
    for start in range(0, columns, step):
        if start % width == 0:
            copies[start // width].wait()
        source = rows_ref[:, :, start : start + step].reshape(visits * depth, step)
        found = jnp.dot(select, source, preferred_element_type=F32)
        for part in range(2):
            here = pltpu.roll(found[:, part * LANES : (part + 1) * LANES], SHIFT, 1)
            if before is None:
                opening = here
            else:
                put(start // LANES + part, jnp.where(low, before, here))
            before = here
    put(0, jnp.where(low, before, opening))


def pack_rows(warps, half, upper, *after):
    visits, rows, columns = warps.shape
    depth = rows // 2
    assert depth >= half and rows % 2 == 0
    first = 0 if upper else depth
    skip = 0 if upper else depth - half
    chunks = 1
    return pl.pallas_call(
        functools.partial(pack_kernel, half, first, skip),
        out_shape=(held((visits * half, columns), BF16), held((visits, depth, columns), BF16)),
        in_specs=[pl.BlockSpec(memory_space=pl.ANY)] * (1 + len(after)),
        out_specs=(whole(),) * 2,
        scratch_shapes=[pltpu.SemaphoreType.DMA((chunks,))],
        compiler_params=LIMIT,
        name="pack_upper" if upper else "pack_lower",
    )(*away(warps), *after)


def level_rows(visits, bands):
    return -(-3 * visits * bands // 16) * 16


def weight_kernel(visits, bands, side_ref, cover_ref, var_ref, bits_ref, send_ref, keep_ref):
    count = bits_ref.shape[0]
    rows = count // visits
    high = rows // bands
    width = bits_ref.shape[1]
    steps = send_ref.shape[1] // width
    step = pl.program_id(0)
    half = lax.div(step, steps)
    lanes = pl.ds(pl.multiple_of(lax.rem(step, steps) * width, width), width)
    extra = level_rows(visits, bands)

    def fill(out_ref):
        line = lax.broadcasted_iota(jnp.int32, (extra, LANES), 0)
        levels = jnp.zeros((extra, LANES), F32)
        for v in range(visits):
            for b in range(bands):
                at = slice(v * rows + b * high, v * rows + (b + 1) * high)
                covers = jnp.where(cover_ref[b, v] != 0, 7, 0)
                usable = jnp.bitwise_and(bits_ref[at, :], 7) < covers
                out_ref[at, lanes] = jnp.where(usable, 1.0, 0.0).astype(BF16)
                left = 1.0 / jnp.full((8, LANES), var_ref[b, v], F32)
                for k in range(3):
                    part = left.astype(BF16).astype(F32)
                    left = left - part
                    spot = (k * bands + b) * visits + v
                    levels = jnp.where(line == spot, part[:1], levels)
        wide = jnp.concatenate([levels.astype(BF16)] * (width // LANES), axis=1)
        out_ref[count:, lanes] = wide

    pl.when(half == 0)(lambda: fill(send_ref))
    pl.when(half == 1)(lambda: fill(keep_ref))


def pixel_weights(badbits, coverage, variance, side):
    visits, rows, columns = badbits.shape
    bands = coverage.shape[1]
    (bits,) = away(badbits.reshape(visits * rows, columns))
    width = columns // 2
    tile = width
    count = width // tile
    shape = held((visits * rows + level_rows(visits, bands), width), BF16)

    def block(i, s):
        first = i < count
        return 0, jnp.where(first, (1 - s[0]) * count + i, s[0] * count + i - count)

    return pl.pallas_call(
        functools.partial(weight_kernel, visits, bands),
        out_shape=(shape, shape),
        grid_spec=pltpu.PrefetchScalarGridSpec(
            num_scalar_prefetch=1,
            grid=(2 * count,),
            in_specs=[
                whole(pltpu.SMEM),
                whole(pltpu.SMEM),
                pl.BlockSpec((visits * rows, tile), block),
            ],
            out_specs=(whole(), whole()),
        ),
        compiler_params=LIMIT,
        name="weights",
    )(side, *away(coverage.T, variance.T), bits)


def split(value):
    high = value.astype(BF16)
    return high, (value - high.astype(F32)).astype(BF16)


def edge_segments(visits, rows, half, below):
    main = half // 8 * 8
    rest = half - main
    origin = half + rows if below else 0
    segments = []
    for v in range(visits):
        first = main + v * rest
        segments.append([(0, main, origin), (first, first + rest, origin + main - first)])
    return segments, main + visits * rest


def table_kernel(visits, rows, half, index_ref, table_ref, row_ref, col_ref, column_out, own_out, above_out, below_out):
    bases, taps = row_ref.shape
    window = 2 * LANES

    def spread(line, shift, count):
        line = jnp.broadcast_to(line, (8, LANES))
        block = pltpu.roll(line, 0, 1, stride=1, stride_axis=0)
        blocks = [pltpu.roll(block, (shift + i) % LANES, 1) for i in range(0, count, 8)]
        return jnp.concatenate(blocks, axis=0)

    tap = lax.broadcasted_iota(jnp.int32, (taps, LANES), 0)
    place = lane_index((taps, LANES))
    ahead = jnp.where(place == tap, 1.0, 0.0).astype(BF16)
    back = jnp.where(place == taps - 1 - tap, 1.0, 0.0).astype(BF16)
    row_lines = jnp.dot(row_ref[...], ahead, preferred_element_type=F32)
    col_lines = jnp.dot(col_ref[...], back, preferred_element_type=F32)
    k = lax.broadcasted_iota(jnp.int32, (window, LANES), 0)
    gap = k - lane_index((window, LANES))
    inside = (gap >= 0) & (gap < LANES)
    for b in range(bases):
        line = col_lines[b : b + 1, :]
        band = jnp.where(inside, spread(line, SHIFT - half, window), 0.0)
        column_out[:, b * LANES : (b + 1) * LANES] = band.astype(BF16)

    lane = lane_index((rows, LANES))

    def assemble(out_ref, high, segments):
        for b in range(bases):
            start = b * high % LANES
            group = b * high // LANES * LANES
            line = row_lines[b : b + 1, :]
            found = {}
            for v in range(visits):
                total = jnp.zeros((rows, LANES), F32)
                for first, last, offset in segments[v]:
                    if first == last:
                        continue
                    key = (first, last, offset)
                    if key not in found:
                        mask = (lane >= start + first) & (lane < start + last)
                        found[key] = jnp.where(mask, spread(line, start - offset, rows), 0.0)
                    total = total + found[key]
                top, low = split(total * table_ref[b, index_ref[v]])
                at = 2 * v * rows
                lanes = slice(group, group + LANES)
                if start == 0:
                    out_ref[at : at + rows, lanes] = top
                    out_ref[at + rows : at + 2 * rows, lanes] = low
                else:
                    out_ref[at : at + rows, lanes] += top
                    out_ref[at + rows : at + 2 * rows, lanes] += low

    assemble(own_out, rows, [[(0, rows, half)]] * visits)
    for below, out in enumerate((above_out, below_out)):
        segments, high = edge_segments(visits, rows, half, below)
        assemble(out, high, segments)


def tables(psf_index, psf_table, row_basis, col_basis, visits, rows):
    bases, taps = row_basis.shape
    half = taps // 2
    rim = (2 * visits * rows, bases * edge_segments(visits, rows, half, 0)[1])
    return pl.pallas_call(
        functools.partial(table_kernel, visits, rows, half),
        out_shape=(
            held((2 * LANES, bases * LANES), BF16),
            held((2 * visits * rows, bases * rows), BF16),
            held(rim, BF16),
            held(rim, BF16),
        ),
        in_specs=[whole(pltpu.SMEM)] * 2 + [whole()] * 2,
        out_specs=(whole(),) * 4,
        compiler_params=LIMIT,
        name="tables",
    )(psf_index, psf_table.T, row_basis, col_basis)


BLOCKS = 4


def column_pass(windows, column_ref):
    return jnp.dot(
        jnp.concatenate(windows, axis=0), column_ref[...], preferred_element_type=F32
    )


def row_pass(layers, count, row_ref, pieces, bases):
    high = row_ref.shape[0] // (2 * len(pieces))
    for first in range(0, layers.shape[0] // count, 2):
        totals = []
        for v, parts in enumerate(pieces):
            sides = []
            for n in (first, first + 1):
                taken = [
                    layers[n * count + top : n * count + last, b * LANES : (b + 1) * LANES]
                    for b in range(bases)
                    for top, last in parts
                    if last > top
                ]
                sides.append(jnp.concatenate(taken, axis=0).astype(BF16))
            total = jnp.dot(
                row_ref[2 * v * high : 2 * (v + 1) * high, :],
                jnp.concatenate(sides, axis=1),
                preferred_element_type=F32,
            )
            totals.append(total[:high] + total[high:])
        yield first, totals


def convolve(make_group, shifted, column_ref, row_ref, pieces, put):
    count = shifted.shape[0]
    groups = shifted.shape[1] // LANES - 1
    bases = column_ref.shape[1] // LANES
    blocks = min(BLOCKS, groups)
    made = [0]

    def columns_of(step):
        while made[0] <= blocks * (step + 1):
            g = made[0]
            shifted[:, g * LANES : (g + 1) * LANES] = make_group(g)
            made[0] += 1
        starts = [(blocks * step + n) * LANES for n in range(blocks)]
        return column_pass([shifted[:, at : at + 2 * LANES] for at in starts], column_ref)

    ahead = columns_of(0)
    for step in range(groups // blocks):
        layers = ahead
        if step + 1 < groups // blocks:
            ahead = columns_of(step + 1)
        for first, totals in row_pass(layers, count, row_ref, pieces, bases):
            put((blocks * step + first) * LANES, totals)


def own_kernel(visits, upper_ref, lower_ref, column_ref, row_ref, out_ref, shifted):
    half_count, columns = upper_ref.shape
    depth = half_count // visits
    rows = 2 * depth
    groups = columns // LANES
    low = lane_index((2 * half_count, LANES)) < SHIFT
    nothing = jnp.zeros((2 * half_count, LANES), F32)
    turned = {-1: nothing, groups: nothing}

    def turn(g):
        if g not in turned:
            lanes = slice(g * LANES, (g + 1) * LANES)
            value = jnp.concatenate([upper_ref[:, lanes], lower_ref[:, lanes]], axis=0)
            turned[g] = pltpu.roll(value.astype(F32), SHIFT, 1)
        return turned[g]

    def make_group(g):
        return jnp.where(low, turn(g - 1), turn(g)).astype(BF16)

    pieces = [
        [(place * half_count + v * depth, place * half_count + (v + 1) * depth) for place in (0, 1)]
        for v in range(visits)
    ]

    def put(start, totals):
        for v, total in enumerate(totals):
            out_ref[v * rows : (v + 1) * rows, start : start + 2 * LANES] = total

    convolve(make_group, shifted, column_ref, row_ref, pieces, put)


def own_part(upper, lower, column, own, visits):
    half_count, columns = upper.shape
    return pl.pallas_call(
        functools.partial(own_kernel, visits),
        out_shape=held((2 * half_count, columns), F32),
        in_specs=[whole()] * 4,
        out_specs=whole(),
        scratch_shapes=[pltpu.VMEM((2 * half_count, columns + LANES), BF16)],
        compiler_params=LIMIT,
        cost_estimate=pl.CostEstimate(flops=10**9, bytes_accessed=10**7, transcendentals=0),
        name="own_rows",
    )(*kept(upper, lower, column, own))


def rim_kernel(visits, half, side_ref, edge_ref, column_ref, row_ref, part_ref, out_ref, shifted):
    edge, columns = edge_ref.shape
    rows = out_ref.shape[0] // visits
    width = out_ref.shape[1]
    groups = columns // LANES
    inner = width // LANES
    base = side_ref[0] * inner if width < columns else 0
    lane = lane_index((edge, LANES))

    def make_group(g):
        at = base + g
        lanes = pl.ds(pl.multiple_of(lax.rem(at, groups) * LANES, LANES), LANES)
        value = edge_ref[:, lanes]
        if g == 0:
            value = value.astype(F32)
            value = jnp.where(lane >= jnp.where(at == 0, SHIFT, 0), value, 0.0).astype(BF16)
        if g == inner:
            value = value.astype(F32)
            value = jnp.where(lane < jnp.where(at == groups, SHIFT, LANES), value, 0.0)
            value = value.astype(BF16)
        return value

    main = half // 8 * 8
    pieces = [[(v * main, (v + 1) * main), (visits * main, edge)] for v in range(visits)]

    def put(start, totals):
        source = pl.ds(pl.multiple_of(base * LANES + start, 2 * LANES), 2 * LANES)
        for v, total in enumerate(totals):
            lines = slice(v * rows, (v + 1) * rows)
            value = (total + part_ref[lines, source]).astype(out_ref.dtype)
            out_ref[lines, start : start + 2 * LANES] = value

    convolve(make_group, shifted, column_ref, row_ref, pieces, put)


def rim_part(side, edge, column, table, part, visits, half, width, dtype):
    count = part.shape[0]
    return pl.pallas_call(
        functools.partial(rim_kernel, visits, half),
        out_shape=held((count, width), dtype),
        in_specs=[whole(pltpu.SMEM)] + [whole()] * 4,
        out_specs=whole(),
        scratch_shapes=[pltpu.VMEM((edge.shape[0], width + LANES), BF16)],
        compiler_params=LIMIT,
    )(side, *kept(edge, column, table, part))


def norm_kernel(visits, bands, *refs):
    flag_refs = refs[:2]
    weight_ref, inverse_ref, count_ref = refs[2:]
    rows, width = inverse_ref.shape
    count = visits * rows
    high = min(16, rows // bands)
    members = [(side, v) for side in range(2) for v in range(visits)]
    levels = {}
    for side in range(2):
        found = flag_refs[side][count:, :LANES].astype(F32)
        for v in range(visits):
            for b in range(bands):
                spots = [(k * bands + b) * visits + v for k in range(3)]
                parts = [found[spot : spot + 1] for spot in spots]
                level = (parts[0] + parts[1]) + parts[2]
                levels[side, v, b] = jnp.broadcast_to(level, (high, LANES))
    count_ref[...] = jnp.zeros_like(count_ref)

    def body(step, carry):
        lanes = pl.ds(pl.multiple_of(step * LANES, LANES), LANES)
        for row in range(0, rows, high):
            denom = PRIOR_WEIGHT
            for m, (side, v) in enumerate(members):
                flag = flag_refs[side][v * rows + row : v * rows + row + high, lanes].astype(F32)
                weight = flag * levels[side, v, row // (rows // bands)]
                weight_ref[m * rows + row : m * rows + row + high, lanes] = weight
                count_ref[m * 8 : (m + 1) * 8, :] += folded(flag)
                denom = denom + weight
            inverse_ref[row : row + high, lanes] = 1.0 / denom
        return carry

    lax.fori_loop(0, width // LANES, body, 0, unroll=4)


def folded(value):
    total = value[:8]
    for start in range(8, value.shape[0], 8):
        total = total + value[start : start + 8]
    return total


def norms(own_flags, other_flags, visits, bands, rows):
    width = own_flags.shape[1]
    members = 2 * visits
    return pl.pallas_call(
        functools.partial(norm_kernel, visits, bands),
        out_shape=(
            held((members * rows, width), F32),
            held((rows, width), F32),
            held((members * 8, LANES), F32),
        ),
        in_specs=[whole()] * 2,
        out_specs=(whole(),) * 3,
        compiler_params=LIMIT,
        name="norms",
    )(*kept(own_flags, other_flags))


def residual_kernel(visits, side_ref, *refs):
    value_refs = refs[:2]
    weight_ref, inverse_ref, count_ref, factor_ref, sums_ref, chi_ref = refs[2:]
    rows, width = inverse_ref.shape
    high = min(16, rows)
    chi_ref[...] = jnp.zeros_like(chi_ref)
    members = [(side, v) for side in range(2) for v in range(visits)]

    def body(step, carry):
        lanes = pl.ds(pl.multiple_of(step * LANES, LANES), LANES)
        for row in range(0, rows, high):
            values, weights = [], []
            numer = None
            for m, (side, v) in enumerate(members):
                at = slice(v * rows + row, v * rows + row + high)
                value = value_refs[side][at, lanes].astype(F32)
                weight = weight_ref[m * rows + row : m * rows + row + high, lanes]
                values.append(value)
                weights.append(weight)
                numer = weight * value if numer is None else numer + weight * value
            first = numer * inverse_ref[row : row + high, lanes]
            for m in range(len(members)):
                residual = values[m] - first
                term = weights[m] * (residual * residual)
                chi_ref[m * 8 : (m + 1) * 8, :] += folded(term)
                target = slice(m * rows + row, m * rows + row + high)
                factor_ref[target, lanes] = weights[m] / (CLIP_LEVEL + term)
        return carry

    lax.fori_loop(0, width // LANES, body, 0, unroll=4)
    for k, ref in enumerate((chi_ref, count_ref)):
        lines = [
            jnp.sum(ref[m * 8 : (m + 1) * 8, :], axis=0, keepdims=True)
            for m in range(len(members))
        ]
        total = jnp.concatenate(lines, axis=0)
        sums_ref[k] = jnp.where(side_ref[0] == 0, total, pltpu.roll(total, visits, 0))


def residual_pass(side, values, weights, inverse, counts, visits):
    rows, width = inverse.shape
    members = 2 * visits
    return pl.pallas_call(
        functools.partial(residual_kernel, visits),
        out_shape=(held((members * rows, width), F32), held((2, members, LANES), F32)),
        in_specs=[whole(pltpu.SMEM)] + [whole()] * 5,
        out_specs=(whole(), whole()),
        scratch_shapes=[pltpu.VMEM((members * 8, LANES), F32)],
        compiler_params=LIMIT,
        name="residual",
    )(side, *kept(*values, weights, inverse, counts))


def final_kernel(visits, side_ref, sums_ref, own_ref, other_ref, factor_ref, out_ref, chi_ref, done, mean, sent):
    rows, width = done.shape
    high = min(16, rows)
    sums = [
        jnp.where(side_ref[0] == 0, sums_ref[k], pltpu.roll(sums_ref[k], visits, 0))
        for k in range(2)
    ]
    chi = jnp.sum(sums[0], axis=1, keepdims=True) / jnp.sum(sums[1], axis=1, keepdims=True)
    scale = CLIP_LEVEL / (CHI_OFFSET + chi)
    for v in range(visits):
        mean[v] = chi[v, 0]
    chi_copy = pltpu.make_async_copy(mean, chi_ref, sent.at[1])
    chi_copy.start()
    scales = [jnp.broadcast_to(scale[m : m + 1], (high, LANES)) for m in range(2 * visits)]
    for lane in range(0, width, LANES):
        lanes = slice(lane, lane + LANES)
        for row in range(0, rows, high):
            numer = denom = None
            for m in range(2 * visits):
                source = own_ref if m < visits else other_ref
                at = (m % visits) * rows + row
                value = source[at : at + high, lanes].astype(F32)
                at = m * rows + row
                revised = factor_ref[at : at + high, lanes] * scales[m]
                numer = revised * value if numer is None else numer + revised * value
                denom = revised if denom is None else denom + revised
            done[row : row + high, lanes] = numer / (denom + PRIOR_WEIGHT)
    copy = pltpu.make_async_copy(done, out_ref, sent.at[0])
    copy.start()
    chi_copy.wait()
    copy.wait()


def final_pass(side, sums, values, factors, visits):
    count, width = values[0].shape
    rows = count // visits
    return pl.pallas_call(
        functools.partial(final_kernel, visits),
        out_shape=(
            jax.ShapeDtypeStruct((rows, width), F32),
            jax.ShapeDtypeStruct((visits,), F32),
        ),
        in_specs=[whole(pltpu.SMEM)] + [whole()] * 4,
        out_specs=(pl.BlockSpec(memory_space=pl.ANY),) * 2,
        scratch_shapes=[
            pltpu.VMEM((rows, width), F32),
            pltpu.SMEM((visits,), F32),
            pltpu.SemaphoreType.DMA((2,)),
        ],
        compiler_params=LIMIT,
        name="final",
    )(side, *kept(sums, *values, factors))


def per_device(warps, badbits, coverage, variance, psf_index, psf_table, row_basis, col_basis):
    visits, rows, columns = warps.shape
    half = row_basis.shape[1] // 2
    strips = lax.axis_size("sky")
    up = [(i, i + 1) for i in range(strips - 1)]
    down = [(j, i) for i, j in up]
    swap = [(0, 1), (1, 0)]
    side = lax.axis_index("visit").astype(jnp.int32).reshape(1)

    last, lower = pack_rows(warps, half, False)
    before = lax.ppermute(last, "sky", up)
    send_weight, own_weight = pixel_weights(badbits, coverage, variance, side)
    other_weight = lax.ppermute(send_weight, "visit", swap)
    column, own, above, below = tables(psf_index, psf_table, row_basis, col_basis, visits, rows)
    leading, upper = pack_rows(warps, half, True, send_weight)
    after = lax.ppermute(leading, "sky", down)
    part = own_part(upper.reshape(-1, columns), lower.reshape(-1, columns), column, own, visits)
    part = rim_part(side, before, column, above, part, visits, half, columns, F32)
    weights, inverse, counts = norms(own_weight, other_weight, visits, coverage.shape[1], rows)
    send_value = rim_part(1 - side, after, column, below, part, visits, half, columns // 2, BF16)
    other_value = lax.ppermute(send_value, "visit", swap)
    own_value = rim_part(side, after, column, below, part, visits, half, columns // 2, BF16)
    values = (own_value, other_value)
    factors, sums = residual_pass(side, values, weights, inverse, counts, visits)
    sums = sums + lax.ppermute(sums, "visit", swap)
    step = 1
    while step < strips:
        pairs = [(2 * i + v, 2 * (i ^ step) + 1 - v) for i in range(strips) for v in (0, 1)]
        sums = sums + lax.ppermute(sums, ("sky", "visit"), pairs)
        step *= 2
    return final_pass(side, sums, values, factors, visits)


def solution(mesh):
    placed = (
        P(("tract", "visit"), "sky", None),
        P(("tract", "visit"), "sky", None),
        P(("tract", "visit"), "sky"),
        P(("tract", "visit"), "sky"),
        P(("tract", "visit")),
        P(),
        P(),
        P(),
    )
    return jax.shard_map(
        per_device,
        mesh=mesh,
        in_specs=placed,
        out_specs=(P(("tract", "sky"), "visit"), P(("tract", "visit"))),
        check_vma=False,
    )
```

```python
import functools

import jax
import jax.numpy as jnp
from jax import lax
from jax.experimental import pallas as pl
from jax.experimental.pallas import tpu as pltpu
from jax.sharding import PartitionSpec as P

PRIOR_WEIGHT = 1.0
CLIP_LEVEL = 9.0
CHI_OFFSET = 0.5
LANES = 128
SHIFT = LANES // 2
F32 = jnp.float32
BF16 = jnp.bfloat16


def whole(space=pltpu.VMEM):
    return pl.BlockSpec(memory_space=space)


def kept(*arrays):
    return [pltpu.with_memory_space_constraint(array, pltpu.VMEM) for array in arrays]


def away(*arrays):
    return [pltpu.with_memory_space_constraint(array, pltpu.HBM) for array in arrays]


def held(shape, dtype):
    return pltpu.VMEM(shape, dtype)


LIMIT = pltpu.CompilerParams(vmem_limit_bytes=20 * 1024 * 1024)


def lane_index(shape):
    return lax.broadcasted_iota(jnp.int32, shape, len(shape) - 1)


def pack_kernel(half, first, skip, x_ref, *refs):
    edge_ref, rows_ref, arrived = refs[-3:]
    visits, depth, columns = rows_ref.shape
    chunks = arrived.shape[0]
    width = columns // chunks
    copies = []
    for c in range(chunks):
        lanes = slice(c * width, (c + 1) * width)
        copies.append(
            pltpu.make_async_copy(
                x_ref.at[:, first : first + depth, lanes], rows_ref.at[:, :, lanes], arrived.at[c]
            )
        )
        copies[c].start()
    main = half // 8 * 8
    rest = half - main
    shape = (visits * half, visits * depth)
    target = lax.broadcasted_iota(jnp.int32, shape, 0)
    source_row = lane_index(shape)
    line = jnp.where(
        target < visits * main,
        lax.div(target, max(main, 1)) * depth + lax.rem(target, max(main, 1)),
        lax.div(target - visits * main, max(rest, 1)) * depth
        + main
        + lax.rem(target - visits * main, max(rest, 1)),
    )
    select = jnp.where(source_row == line + skip, 1.0, 0.0).astype(BF16)
    low = lane_index((edge_ref.shape[0], LANES)) < SHIFT
    step = 2 * LANES

    def put(g, value):
        edge_ref[:, g * LANES : (g + 1) * LANES] = value.astype(BF16)

    before = opening = None
    for start in range(0, columns, step):
        if start % width == 0:
            copies[start // width].wait()
        source = rows_ref[:, :, start : start + step].reshape(visits * depth, step)
        found = jnp.dot(select, source, preferred_element_type=F32)
        for part in range(2):
            here = pltpu.roll(found[:, part * LANES : (part + 1) * LANES], SHIFT, 1)
            if before is None:
                opening = here
            else:
                put(start // LANES + part, jnp.where(low, before, here))
            before = here
    put(0, jnp.where(low, before, opening))


def pack_rows(warps, half, upper, *after):
    visits, rows, columns = warps.shape
    depth = rows // 2
    assert depth >= half and rows % 2 == 0
    first = 0 if upper else depth
    skip = 0 if upper else depth - half
    chunks = 1
    return pl.pallas_call(
        functools.partial(pack_kernel, half, first, skip),
        out_shape=(held((visits * half, columns), BF16), held((visits, depth, columns), BF16)),
        in_specs=[pl.BlockSpec(memory_space=pl.ANY)] * (1 + len(after)),
        out_specs=(whole(),) * 2,
        scratch_shapes=[pltpu.SemaphoreType.DMA((chunks,))],
        compiler_params=LIMIT,
        name="pack_upper" if upper else "pack_lower",
    )(*away(warps), *after)


def level_rows(visits, bands):
    return -(-3 * visits * bands // 16) * 16


def weight_kernel(visits, bands, side_ref, cover_ref, var_ref, bits_ref, send_ref, keep_ref):
    count = bits_ref.shape[0]
    rows = count // visits
    high = rows // bands
    width = bits_ref.shape[1]
    steps = send_ref.shape[1] // width
    step = pl.program_id(0)
    half = lax.div(step, steps)
    lanes = pl.ds(pl.multiple_of(lax.rem(step, steps) * width, width), width)
    extra = level_rows(visits, bands)

    def fill(out_ref):
        line = lax.broadcasted_iota(jnp.int32, (extra, LANES), 0)
        levels = jnp.zeros((extra, LANES), F32)
        for v in range(visits):
            for b in range(bands):
                at = slice(v * rows + b * high, v * rows + (b + 1) * high)
                covers = jnp.where(cover_ref[b, v] != 0, 7, 0)
                usable = jnp.bitwise_and(bits_ref[at, :], 7) < covers
                out_ref[at, lanes] = jnp.where(usable, 1.0, 0.0).astype(BF16)
                left = 1.0 / jnp.full((8, LANES), var_ref[b, v], F32)
                for k in range(3):
                    part = left.astype(BF16).astype(F32)
                    left = left - part
                    spot = (k * bands + b) * visits + v
                    levels = jnp.where(line == spot, part[:1], levels)
        wide = jnp.concatenate([levels.astype(BF16)] * (width // LANES), axis=1)
        out_ref[count:, lanes] = wide

    pl.when(half == 0)(lambda: fill(send_ref))
    pl.when(half == 1)(lambda: fill(keep_ref))


def pixel_weights(badbits, coverage, variance, side):
    visits, rows, columns = badbits.shape
    bands = coverage.shape[1]
    (bits,) = away(badbits.reshape(visits * rows, columns))
    width = columns // 2
    tile = width
    count = width // tile
    shape = held((visits * rows + level_rows(visits, bands), width), BF16)

    def block(i, s):
        first = i < count
        return 0, jnp.where(first, (1 - s[0]) * count + i, s[0] * count + i - count)

    return pl.pallas_call(
        functools.partial(weight_kernel, visits, bands),
        out_shape=(shape, shape),
        grid_spec=pltpu.PrefetchScalarGridSpec(
            num_scalar_prefetch=1,
            grid=(2 * count,),
            in_specs=[
                whole(pltpu.SMEM),
                whole(pltpu.SMEM),
                pl.BlockSpec((visits * rows, tile), block),
            ],
            out_specs=(whole(), whole()),
        ),
        compiler_params=LIMIT,
        name="weights",
    )(side, *away(coverage.T, variance.T), bits)


def split(value):
    high = value.astype(BF16)
    return high, (value - high.astype(F32)).astype(BF16)


def edge_segments(visits, rows, half, below):
    main = half // 8 * 8
    rest = half - main
    origin = half + rows if below else 0
    segments = []
    for v in range(visits):
        first = main + v * rest
        segments.append([(0, main, origin), (first, first + rest, origin + main - first)])
    return segments, main + visits * rest


def table_kernel(visits, rows, half, index_ref, table_ref, row_ref, col_ref, column_out, own_out, above_out, below_out):
    bases, taps = row_ref.shape
    window = 2 * LANES

    def spread(line, shift, count):
        line = jnp.broadcast_to(line, (8, LANES))
        block = pltpu.roll(line, 0, 1, stride=1, stride_axis=0)
        blocks = [pltpu.roll(block, (shift + i) % LANES, 1) for i in range(0, count, 8)]
        return jnp.concatenate(blocks, axis=0)

    tap = lax.broadcasted_iota(jnp.int32, (taps, LANES), 0)
    place = lane_index((taps, LANES))
    ahead = jnp.where(place == tap, 1.0, 0.0).astype(BF16)
    back = jnp.where(place == taps - 1 - tap, 1.0, 0.0).astype(BF16)
    row_lines = jnp.dot(row_ref[...], ahead, preferred_element_type=F32)
    col_lines = jnp.dot(col_ref[...], back, preferred_element_type=F32)
    k = lax.broadcasted_iota(jnp.int32, (window, LANES), 0)
    gap = k - lane_index((window, LANES))
    inside = (gap >= 0) & (gap < LANES)
    for b in range(bases):
        line = col_lines[b : b + 1, :]
        band = jnp.where(inside, spread(line, SHIFT - half, window), 0.0)
        column_out[:, b * LANES : (b + 1) * LANES] = band.astype(BF16)

    depth = rows // 2

    def assemble(out_ref, high, segments, top, lines):
        lane = lane_index((lines, LANES))
        for b in range(bases):
            start = b * high % LANES
            group = b * high // LANES * LANES
            line = row_lines[b : b + 1, :]
            found = {}
            for v in range(visits):
                total = jnp.zeros((lines, LANES), F32)
                for first, last, offset in segments[v]:
                    if first == last:
                        continue
                    key = (first, last, offset)
                    if key not in found:
                        mask = (lane >= start + first) & (lane < start + last)
                        turned = spread(line, start - offset + top, lines)
                        found[key] = jnp.where(mask, turned, 0.0)
                    total = total + found[key]
                high_part, low_part = split(total * table_ref[b, index_ref[v]])
                at = 2 * v * lines
                lanes = slice(group, group + LANES)
                if start == 0:
                    out_ref[at : at + lines, lanes] = high_part
                    out_ref[at + lines : at + 2 * lines, lanes] = low_part
                else:
                    out_ref[at : at + lines, lanes] += high_part
                    out_ref[at + lines : at + 2 * lines, lanes] += low_part

    assemble(own_out, rows, [[(0, rows, half)]] * visits, 0, rows)
    for below, out in enumerate((above_out, below_out)):
        segments, high = edge_segments(visits, rows, half, below)
        assemble(out, high, segments, below * depth, depth)


def tables(psf_index, psf_table, row_basis, col_basis, visits, rows):
    bases, taps = row_basis.shape
    half = taps // 2
    rim = (visits * rows, bases * edge_segments(visits, rows, half, 0)[1])
    return pl.pallas_call(
        functools.partial(table_kernel, visits, rows, half),
        out_shape=(
            held((2 * LANES, bases * LANES), BF16),
            held((2 * visits * rows, bases * rows), BF16),
            held(rim, BF16),
            held(rim, BF16),
        ),
        in_specs=[whole(pltpu.SMEM)] * 2 + [whole()] * 2,
        out_specs=(whole(),) * 4,
        compiler_params=LIMIT,
        name="tables",
    )(psf_index, psf_table.T, row_basis, col_basis)


BLOCKS = 4


def column_pass(windows, column_ref):
    return jnp.dot(
        jnp.concatenate(windows, axis=0), column_ref[...], preferred_element_type=F32
    )


def row_pass(layers, count, row_ref, pieces, bases):
    high = row_ref.shape[0] // (2 * len(pieces))
    for first in range(0, layers.shape[0] // count, 2):
        totals = []
        for v, parts in enumerate(pieces):
            sides = []
            for n in (first, first + 1):
                taken = [
                    layers[n * count + top : n * count + last, b * LANES : (b + 1) * LANES]
                    for b in range(bases)
                    for top, last in parts
                    if last > top
                ]
                sides.append(jnp.concatenate(taken, axis=0).astype(BF16))
            total = jnp.dot(
                row_ref[2 * v * high : 2 * (v + 1) * high, :],
                jnp.concatenate(sides, axis=1),
                preferred_element_type=F32,
            )
            totals.append(total[:high] + total[high:])
        yield first, totals


def convolve(make_group, shifted, column_ref, row_ref, pieces, put):
    count = shifted.shape[0]
    groups = shifted.shape[1] // LANES - 1
    bases = column_ref.shape[1] // LANES
    blocks = min(BLOCKS, groups)
    made = [0]

    def columns_of(step):
        while made[0] <= blocks * (step + 1):
            g = made[0]
            shifted[:, g * LANES : (g + 1) * LANES] = make_group(g)
            made[0] += 1
        starts = [(blocks * step + n) * LANES for n in range(blocks)]
        return column_pass([shifted[:, at : at + 2 * LANES] for at in starts], column_ref)

    ahead = columns_of(0)
    for step in range(groups // blocks):
        layers = ahead
        if step + 1 < groups // blocks:
            ahead = columns_of(step + 1)
        for first, totals in row_pass(layers, count, row_ref, pieces, bases):
            put((blocks * step + first) * LANES, totals)


def own_kernel(visits, upper_ref, lower_ref, column_ref, row_ref, top_ref, bottom_ref, shifted):
    half_count, columns = upper_ref.shape
    depth = half_count // visits
    groups = columns // LANES
    low = lane_index((2 * half_count, LANES)) < SHIFT
    nothing = jnp.zeros((2 * half_count, LANES), F32)
    turned = {-1: nothing, groups: nothing}

    def turn(g):
        if g not in turned:
            lanes = slice(g * LANES, (g + 1) * LANES)
            value = jnp.concatenate([upper_ref[:, lanes], lower_ref[:, lanes]], axis=0)
            turned[g] = pltpu.roll(value.astype(F32), SHIFT, 1)
        return turned[g]

    def make_group(g):
        return jnp.where(low, turn(g - 1), turn(g)).astype(BF16)

    pieces = [
        [(place * half_count + v * depth, place * half_count + (v + 1) * depth) for place in (0, 1)]
        for v in range(visits)
    ]

    def put(start, totals):
        for v, total in enumerate(totals):
            lines = slice(v * depth, (v + 1) * depth)
            top_ref[lines, start : start + 2 * LANES] = total[:depth]
            bottom_ref[lines, start : start + 2 * LANES] = total[depth:]

    convolve(make_group, shifted, column_ref, row_ref, pieces, put)


def own_part(upper, lower, column, own, visits):
    half_count, columns = upper.shape
    return pl.pallas_call(
        functools.partial(own_kernel, visits),
        out_shape=(held((half_count, columns), F32),) * 2,
        in_specs=[whole()] * 4,
        out_specs=(whole(),) * 2,
        scratch_shapes=[pltpu.VMEM((2 * half_count, columns + LANES), BF16)],
        compiler_params=LIMIT,
        cost_estimate=pl.CostEstimate(flops=10**9, bytes_accessed=10**7, transcendentals=0),
        name="own_rows",
    )(*kept(upper, lower, column, own))


def rim_kernel(visits, half, side_ref, edge_ref, column_ref, row_ref, part_ref, out_ref, shifted):
    edge, columns = edge_ref.shape
    rows = out_ref.shape[0] // visits
    width = out_ref.shape[1]
    groups = columns // LANES
    inner = width // LANES
    base = side_ref[0] * inner
    lane = lane_index((edge, LANES))

    def make_group(g):
        at = base + g
        lanes = pl.ds(pl.multiple_of(lax.rem(at, groups) * LANES, LANES), LANES)
        value = edge_ref[:, lanes]
        if g == 0:
            value = value.astype(F32)
            value = jnp.where(lane >= jnp.where(at == 0, SHIFT, 0), value, 0.0).astype(BF16)
        if g == inner:
            value = value.astype(F32)
            value = jnp.where(lane < jnp.where(at == groups, SHIFT, LANES), value, 0.0)
            value = value.astype(BF16)
        return value

    main = half // 8 * 8
    pieces = [[(v * main, (v + 1) * main), (visits * main, edge)] for v in range(visits)]

    def put(start, totals):
        source = pl.ds(pl.multiple_of(base * LANES + start, 2 * LANES), 2 * LANES)
        for v, total in enumerate(totals):
            lines = slice(v * rows, (v + 1) * rows)
            value = (total + part_ref[lines, source]).astype(out_ref.dtype)
            out_ref[lines, start : start + 2 * LANES] = value

    convolve(make_group, shifted, column_ref, row_ref, pieces, put)


def rim_part(side, edge, column, table, part, visits, half):
    count, columns = part.shape
    width = columns // 2
    return pl.pallas_call(
        functools.partial(rim_kernel, visits, half),
        out_shape=held((count, width), BF16),
        in_specs=[whole(pltpu.SMEM)] + [whole()] * 4,
        out_specs=whole(),
        scratch_shapes=[pltpu.VMEM((edge.shape[0], width + LANES), BF16)],
        compiler_params=LIMIT,
    )(side, *kept(edge, column, table, part))


def norm_kernel(visits, bands, *refs):
    flag_refs = refs[:2]
    weight_ref, inverse_ref, count_ref = refs[2:]
    rows, width = inverse_ref.shape
    count = visits * rows
    high = min(16, rows // bands)
    members = [(side, v) for side in range(2) for v in range(visits)]
    levels = {}
    for side in range(2):
        found = flag_refs[side][count:, :LANES].astype(F32)
        for v in range(visits):
            for b in range(bands):
                spots = [(k * bands + b) * visits + v for k in range(3)]
                parts = [found[spot : spot + 1] for spot in spots]
                level = (parts[0] + parts[1]) + parts[2]
                levels[side, v, b] = jnp.broadcast_to(level, (high, LANES))
    count_ref[...] = jnp.zeros_like(count_ref)

    def body(step, carry):
        lanes = pl.ds(pl.multiple_of(step * LANES, LANES), LANES)
        for row in range(0, rows, high):
            denom = PRIOR_WEIGHT
            for m, (side, v) in enumerate(members):
                flag = flag_refs[side][v * rows + row : v * rows + row + high, lanes].astype(F32)
                weight = flag * levels[side, v, row // (rows // bands)]
                weight_ref[m * rows + row : m * rows + row + high, lanes] = weight
                count_ref[m * 8 : (m + 1) * 8, :] += folded(flag)
                denom = denom + weight
            inverse_ref[row : row + high, lanes] = 1.0 / denom
        return carry

    lax.fori_loop(0, width // LANES, body, 0, unroll=4)


def folded(value):
    total = value[:8]
    for start in range(8, value.shape[0], 8):
        total = total + value[start : start + 8]
    return total


def norms(own_flags, other_flags, visits, bands, rows):
    width = own_flags.shape[1]
    members = 2 * visits
    return pl.pallas_call(
        functools.partial(norm_kernel, visits, bands),
        out_shape=(
            held((members * rows, width), F32),
            held((rows, width), F32),
            held((members * 8, LANES), F32),
        ),
        in_specs=[whole()] * 2,
        out_specs=(whole(),) * 3,
        compiler_params=LIMIT,
        name="norms",
    )(*kept(own_flags, other_flags))


def residual_kernel(visits, first, last, side_ref, *refs):
    value_refs = refs[:2]
    weight_ref, inverse_ref = refs[2:4]
    if last:
        so_far_ref, count_ref, factor_ref, sums_ref, chi_ref = refs[4:]
        chi_ref[...] = so_far_ref[...]
    else:
        factor_ref, chi_ref = refs[4:]
        chi_ref[...] = jnp.zeros_like(chi_ref)
    depth = value_refs[0].shape[0] // visits
    rows, width = inverse_ref.shape
    high = min(16, depth)
    members = [(side, v) for side in range(2) for v in range(visits)]

    def body(step, carry):
        lanes = pl.ds(pl.multiple_of(step * LANES, LANES), LANES)
        for row in range(0, depth, high):
            values, weights = [], []
            numer = None
            for m, (side, v) in enumerate(members):
                at = slice(v * depth + row, v * depth + row + high)
                value = value_refs[side][at, lanes].astype(F32)
                at = m * rows + first + row
                weight = weight_ref[at : at + high, lanes]
                values.append(value)
                weights.append(weight)
                numer = weight * value if numer is None else numer + weight * value
            mean = numer * inverse_ref[first + row : first + row + high, lanes]
            for m in range(len(members)):
                residual = values[m] - mean
                term = weights[m] * (residual * residual)
                chi_ref[m * 8 : (m + 1) * 8, :] += folded(term)
                target = slice(m * depth + row, m * depth + row + high)
                factor_ref[target, lanes] = weights[m] / (CLIP_LEVEL + term)
        return carry

    lax.fori_loop(0, width // LANES, body, 0, unroll=4)
    if not last:
        return
    for k, ref in enumerate((chi_ref, count_ref)):
        lines = [
            jnp.sum(ref[m * 8 : (m + 1) * 8, :], axis=0, keepdims=True)
            for m in range(len(members))
        ]
        total = jnp.concatenate(lines, axis=0)
        sums_ref[k] = jnp.where(side_ref[0] == 0, total, pltpu.roll(total, visits, 0))


def residual_pass(side, values, weights, inverse, visits, first, *ending):
    count, width = values[0].shape
    members = 2 * visits
    last = len(ending) > 0
    chi = (members * 8, LANES)
    return pl.pallas_call(
        functools.partial(residual_kernel, visits, first, last),
        out_shape=(
            held((2 * count, width), F32),
            held((2, members, LANES) if last else chi, F32),
        ),
        in_specs=[whole(pltpu.SMEM)] + [whole()] * (4 + len(ending)),
        out_specs=(whole(), whole()),
        scratch_shapes=[pltpu.VMEM(chi, F32)] * last,
        compiler_params=LIMIT,
        name="residual_last" if last else "residual",
    )(side, *kept(*values, weights, inverse, *ending))


def final_kernel(visits, side_ref, sums_ref, *refs):
    parts = [refs[:3], refs[3:6]]
    out_ref, chi_ref, done, mean, sent = refs[6:]
    rows, width = done.shape
    high = min(16, rows // 2)
    sums = [
        jnp.where(side_ref[0] == 0, sums_ref[k], pltpu.roll(sums_ref[k], visits, 0))
        for k in range(2)
    ]
    chi = jnp.sum(sums[0], axis=1, keepdims=True) / jnp.sum(sums[1], axis=1, keepdims=True)
    scale = CLIP_LEVEL / (CHI_OFFSET + chi)
    for v in range(visits):
        mean[v] = chi[v, 0]
    chi_copy = pltpu.make_async_copy(mean, chi_ref, sent.at[1])
    chi_copy.start()
    scales = [jnp.broadcast_to(scale[m : m + 1], (high, LANES)) for m in range(2 * visits)]
    depth = rows // 2
    for lane in range(0, width, LANES):
        lanes = slice(lane, lane + LANES)
        for top, part in zip((0, depth), parts):
            for row in range(0, depth, high):
                numer = denom = None
                for m in range(2 * visits):
                    at = (m % visits) * depth + row
                    value = part[m // visits][at : at + high, lanes].astype(F32)
                    at = m * depth + row
                    revised = part[2][at : at + high, lanes] * scales[m]
                    numer = revised * value if numer is None else numer + revised * value
                    denom = revised if denom is None else denom + revised
                done[top + row : top + row + high, lanes] = numer / (denom + PRIOR_WEIGHT)
    copy = pltpu.make_async_copy(done, out_ref, sent.at[0])
    copy.start()
    chi_copy.wait()
    copy.wait()


def final_pass(side, sums, upper, lower, visits):
    count, width = upper[0].shape
    rows = 2 * count // visits
    return pl.pallas_call(
        functools.partial(final_kernel, visits),
        out_shape=(
            jax.ShapeDtypeStruct((rows, width), F32),
            jax.ShapeDtypeStruct((visits,), F32),
        ),
        in_specs=[whole(pltpu.SMEM)] + [whole()] * 7,
        out_specs=(pl.BlockSpec(memory_space=pl.ANY),) * 2,
        scratch_shapes=[
            pltpu.VMEM((rows, width), F32),
            pltpu.SMEM((visits,), F32),
            pltpu.SemaphoreType.DMA((2,)),
        ],
        compiler_params=LIMIT,
        name="final",
    )(side, *kept(sums, *upper, *lower))


def per_device(warps, badbits, coverage, variance, psf_index, psf_table, row_basis, col_basis):
    visits, rows, columns = warps.shape
    half = row_basis.shape[1] // 2
    strips = lax.axis_size("sky")
    up = [(i, i + 1) for i in range(strips - 1)]
    down = [(j, i) for i, j in up]
    swap = [(0, 1), (1, 0)]
    side = lax.axis_index("visit").astype(jnp.int32).reshape(1)

    last, lower = pack_rows(warps, half, False)
    before = lax.ppermute(last, "sky", up)
    send_weight, own_weight = pixel_weights(badbits, coverage, variance, side)
    other_weight = lax.ppermute(send_weight, "visit", swap)
    column, own, above, below = tables(psf_index, psf_table, row_basis, col_basis, visits, rows)
    leading, upper = pack_rows(warps, half, True, send_weight)
    after = lax.ppermute(leading, "sky", down)
    top, bottom = own_part(
        upper.reshape(-1, columns), lower.reshape(-1, columns), column, own, visits
    )
    send_top = rim_part(1 - side, before, column, above, top, visits, half)
    other_top = lax.ppermute(send_top, "visit", swap)
    own_top = rim_part(side, before, column, above, top, visits, half)
    weights, inverse, counts = norms(own_weight, other_weight, visits, coverage.shape[1], rows)
    top_factors, chi = residual_pass(side, (own_top, other_top), weights, inverse, visits, 0)
    send_value = rim_part(1 - side, after, column, below, bottom, visits, half)
    other_value = lax.ppermute(send_value, "visit", swap)
    own_value = rim_part(side, after, column, below, bottom, visits, half)
    factors, sums = residual_pass(
        side, (own_value, other_value), weights, inverse, visits, rows // 2, chi, counts
    )
    sums = sums + lax.ppermute(sums, "visit", swap)
    step = 1
    while step < strips:
        pairs = [(2 * i + v, 2 * (i ^ step) + 1 - v) for i in range(strips) for v in (0, 1)]
        sums = sums + lax.ppermute(sums, ("sky", "visit"), pairs)
        step *= 2
    upper = (own_top, other_top, top_factors)
    return final_pass(side, sums, upper, (own_value, other_value, factors), visits)


def solution(mesh):
    placed = (
        P(("tract", "visit"), "sky", None),
        P(("tract", "visit"), "sky", None),
        P(("tract", "visit"), "sky"),
        P(("tract", "visit"), "sky"),
        P(("tract", "visit")),
        P(),
        P(),
        P(),
    )
    return jax.shard_map(
        per_device,
        mesh=mesh,
        in_specs=placed,
        out_specs=(P(("tract", "sky"), "visit"), P(("tract", "visit"))),
        check_vma=False,
    )
```

```python
import functools

import jax
import jax.numpy as jnp
from jax import lax
from jax.experimental import pallas as pl
from jax.experimental.pallas import tpu as pltpu
from jax.sharding import PartitionSpec as P

PRIOR_WEIGHT = 1.0
CLIP_LEVEL = 9.0
CHI_OFFSET = 0.5
LANES = 128
SHIFT = LANES // 2
F32 = jnp.float32
BF16 = jnp.bfloat16


def whole(space=pltpu.VMEM):
    return pl.BlockSpec(memory_space=space)


def kept(*arrays):
    return [pltpu.with_memory_space_constraint(array, pltpu.VMEM) for array in arrays]


def away(*arrays):
    return [pltpu.with_memory_space_constraint(array, pltpu.HBM) for array in arrays]


def held(shape, dtype):
    return pltpu.VMEM(shape, dtype)


LIMIT = pltpu.CompilerParams(vmem_limit_bytes=20 * 1024 * 1024)


def lane_index(shape):
    return lax.broadcasted_iota(jnp.int32, shape, len(shape) - 1)


def pack_kernel(half, first, skip, x_ref, *refs):
    edge_ref, rows_ref, arrived = refs[-3:]
    visits, depth, columns = rows_ref.shape
    chunks = arrived.shape[0]
    width = columns // chunks
    copies = []
    for c in range(chunks):
        lanes = slice(c * width, (c + 1) * width)
        copies.append(
            pltpu.make_async_copy(
                x_ref.at[:, first : first + depth, lanes], rows_ref.at[:, :, lanes], arrived.at[c]
            )
        )
        copies[c].start()
    main = half // 8 * 8
    rest = half - main
    shape = (visits * half, visits * depth)
    target = lax.broadcasted_iota(jnp.int32, shape, 0)
    source_row = lane_index(shape)
    line = jnp.where(
        target < visits * main,
        lax.div(target, max(main, 1)) * depth + lax.rem(target, max(main, 1)),
        lax.div(target - visits * main, max(rest, 1)) * depth
        + main
        + lax.rem(target - visits * main, max(rest, 1)),
    )
    select = jnp.where(source_row == line + skip, 1.0, 0.0).astype(BF16)
    low = lane_index((edge_ref.shape[0], LANES)) < SHIFT
    step = 2 * LANES

    def put(g, value):
        edge_ref[:, g * LANES : (g + 1) * LANES] = value.astype(BF16)

    before = opening = None
    for start in range(0, columns, step):
        if start % width == 0:
            copies[start // width].wait()
        source = rows_ref[:, :, start : start + step].reshape(visits * depth, step)
        found = jnp.dot(select, source, preferred_element_type=F32)
        for part in range(2):
            here = pltpu.roll(found[:, part * LANES : (part + 1) * LANES], SHIFT, 1)
            if before is None:
                opening = here
            else:
                put(start // LANES + part, jnp.where(low, before, here))
            before = here
    put(0, jnp.where(low, before, opening))


def pack_rows(warps, half, upper, *after):
    visits, rows, columns = warps.shape
    depth = rows // 2
    assert depth >= half and rows % 2 == 0
    first = 0 if upper else depth
    skip = 0 if upper else depth - half
    chunks = 1
    return pl.pallas_call(
        functools.partial(pack_kernel, half, first, skip),
        out_shape=(held((visits * half, columns), BF16), held((visits, depth, columns), BF16)),
        in_specs=[pl.BlockSpec(memory_space=pl.ANY)] * (1 + len(after)),
        out_specs=(whole(),) * 2,
        scratch_shapes=[pltpu.SemaphoreType.DMA((chunks,))],
        compiler_params=LIMIT,
        name="pack_upper" if upper else "pack_lower",
    )(*away(warps), *after)


def level_rows(visits, bands):
    return -(-3 * visits * bands // 16) * 16


def weight_kernel(visits, bands, side_ref, cover_ref, var_ref, bits_ref, send_ref, keep_ref):
    count = bits_ref.shape[0]
    rows = count // visits
    high = rows // bands
    width = bits_ref.shape[1]
    steps = send_ref.shape[1] // width
    step = pl.program_id(0)
    half = lax.div(step, steps)
    lanes = pl.ds(pl.multiple_of(lax.rem(step, steps) * width, width), width)
    extra = level_rows(visits, bands)

    def fill(out_ref):
        line = lax.broadcasted_iota(jnp.int32, (extra, LANES), 0)
        levels = jnp.zeros((extra, LANES), F32)
        for v in range(visits):
            for b in range(bands):
                at = slice(v * rows + b * high, v * rows + (b + 1) * high)
                covers = jnp.where(cover_ref[b, v] != 0, 7, 0)
                usable = jnp.bitwise_and(bits_ref[at, :], 7) < covers
                out_ref[at, lanes] = jnp.where(usable, 1.0, 0.0).astype(BF16)
                left = 1.0 / jnp.full((8, LANES), var_ref[b, v], F32)
                for k in range(3):
                    part = left.astype(BF16).astype(F32)
                    left = left - part
                    spot = (k * bands + b) * visits + v
                    levels = jnp.where(line == spot, part[:1], levels)
        wide = jnp.concatenate([levels.astype(BF16)] * (width // LANES), axis=1)
        out_ref[count:, lanes] = wide

    pl.when(half == 0)(lambda: fill(send_ref))
    pl.when(half == 1)(lambda: fill(keep_ref))


def pixel_weights(badbits, coverage, variance, side):
    visits, rows, columns = badbits.shape
    bands = coverage.shape[1]
    (bits,) = away(badbits.reshape(visits * rows, columns))
    width = columns // 2
    tile = width
    count = width // tile
    shape = held((visits * rows + level_rows(visits, bands), width), BF16)

    def block(i, s):
        first = i < count
        return 0, jnp.where(first, (1 - s[0]) * count + i, s[0] * count + i - count)

    return pl.pallas_call(
        functools.partial(weight_kernel, visits, bands),
        out_shape=(shape, shape),
        grid_spec=pltpu.PrefetchScalarGridSpec(
            num_scalar_prefetch=1,
            grid=(2 * count,),
            in_specs=[
                whole(pltpu.SMEM),
                whole(pltpu.SMEM),
                pl.BlockSpec((visits * rows, tile), block),
            ],
            out_specs=(whole(), whole()),
        ),
        compiler_params=LIMIT,
        name="weights",
    )(side, *away(coverage.T, variance.T), bits)


def split(value):
    high = value.astype(BF16)
    return high, (value - high.astype(F32)).astype(BF16)


def edge_segments(visits, rows, half, below):
    main = half // 8 * 8
    rest = half - main
    origin = half + rows if below else 0
    segments = []
    for v in range(visits):
        first = main + v * rest
        segments.append([(0, main, origin), (first, first + rest, origin + main - first)])
    return segments, main + visits * rest


def table_kernel(visits, rows, half, index_ref, table_ref, row_ref, col_ref, column_out, own_out, above_out, below_out):
    bases, taps = row_ref.shape
    window = 2 * LANES

    def spread(line, shift, count):
        line = jnp.broadcast_to(line, (8, LANES))
        block = pltpu.roll(line, 0, 1, stride=1, stride_axis=0)
        blocks = [pltpu.roll(block, (shift + i) % LANES, 1) for i in range(0, count, 8)]
        return jnp.concatenate(blocks, axis=0)

    tap = lax.broadcasted_iota(jnp.int32, (taps, LANES), 0)
    place = lane_index((taps, LANES))
    ahead = jnp.where(place == tap, 1.0, 0.0).astype(BF16)
    back = jnp.where(place == taps - 1 - tap, 1.0, 0.0).astype(BF16)
    row_lines = jnp.dot(row_ref[...], ahead, preferred_element_type=F32)
    col_lines = jnp.dot(col_ref[...], back, preferred_element_type=F32)
    k = lax.broadcasted_iota(jnp.int32, (window, LANES), 0)
    gap = k - lane_index((window, LANES))
    inside = (gap >= 0) & (gap < LANES)
    for b in range(bases):
        line = col_lines[b : b + 1, :]
        band = jnp.where(inside, spread(line, SHIFT - half, window), 0.0)
        column_out[:, b * LANES : (b + 1) * LANES] = band.astype(BF16)

    depth = rows // 2

    def assemble(out_ref, high, segments, top, lines):
        lane = lane_index((lines, LANES))
        for b in range(bases):
            start = b * high % LANES
            group = b * high // LANES * LANES
            line = row_lines[b : b + 1, :]
            found = {}
            for v in range(visits):
                total = jnp.zeros((lines, LANES), F32)
                for first, last, offset in segments[v]:
                    if first == last:
                        continue
                    key = (first, last, offset)
                    if key not in found:
                        mask = (lane >= start + first) & (lane < start + last)
                        turned = spread(line, start - offset + top, lines)
                        found[key] = jnp.where(mask, turned, 0.0)
                    total = total + found[key]
                high_part, low_part = split(total * table_ref[b, index_ref[v]])
                at = 2 * v * lines
                lanes = slice(group, group + LANES)
                if start == 0:
                    out_ref[at : at + lines, lanes] = high_part
                    out_ref[at + lines : at + 2 * lines, lanes] = low_part
                else:
                    out_ref[at : at + lines, lanes] += high_part
                    out_ref[at + lines : at + 2 * lines, lanes] += low_part

    assemble(own_out, rows, [[(0, rows, half)]] * visits, 0, rows)
    for below, out in enumerate((above_out, below_out)):
        segments, high = edge_segments(visits, rows, half, below)
        assemble(out, high, segments, below * depth, depth)


def tables(psf_index, psf_table, row_basis, col_basis, visits, rows):
    bases, taps = row_basis.shape
    half = taps // 2
    rim = (visits * rows, bases * edge_segments(visits, rows, half, 0)[1])
    return pl.pallas_call(
        functools.partial(table_kernel, visits, rows, half),
        out_shape=(
            held((2 * LANES, bases * LANES), BF16),
            held((2 * visits * rows, bases * rows), BF16),
            held(rim, BF16),
            held(rim, BF16),
        ),
        in_specs=[whole(pltpu.SMEM)] * 2 + [whole()] * 2,
        out_specs=(whole(),) * 4,
        compiler_params=LIMIT,
        name="tables",
    )(psf_index, psf_table.T, row_basis, col_basis)


def column_pass(windows, column_ref):
    return jnp.dot(
        jnp.concatenate(windows, axis=0), column_ref[...], preferred_element_type=F32
    )


def row_pass(layers, count, row_ref, pieces, bases):
    high = row_ref.shape[0] // (2 * len(pieces))
    for first in range(0, layers.shape[0] // count, 2):
        totals = []
        for v, parts in enumerate(pieces):
            sides = []
            for n in (first, first + 1):
                taken = [
                    layers[n * count + top : n * count + last, b * LANES : (b + 1) * LANES]
                    for b in range(bases)
                    for top, last in parts
                    if last > top
                ]
                sides.append(jnp.concatenate(taken, axis=0).astype(BF16))
            total = jnp.dot(
                row_ref[2 * v * high : 2 * (v + 1) * high, :],
                jnp.concatenate(sides, axis=1),
                preferred_element_type=F32,
            )
            totals.append(total[:high] + total[high:])
        yield first, totals


def convolve(make_group, shifted, column_ref, row_ref, pieces, put, blocks):
    count = shifted.shape[0]
    groups = shifted.shape[1] // LANES - 1
    bases = column_ref.shape[1] // LANES
    blocks = min(blocks, groups)
    made = [0]

    def columns_of(step):
        while made[0] <= blocks * (step + 1):
            g = made[0]
            shifted[:, g * LANES : (g + 1) * LANES] = make_group(g)
            made[0] += 1
        starts = [(blocks * step + n) * LANES for n in range(blocks)]
        return column_pass([shifted[:, at : at + 2 * LANES] for at in starts], column_ref)

    ahead = columns_of(0)
    for step in range(groups // blocks):
        layers = ahead
        if step + 1 < groups // blocks:
            ahead = columns_of(step + 1)
        for first, totals in row_pass(layers, count, row_ref, pieces, bases):
            put((blocks * step + first) * LANES, totals)


def own_kernel(visits, upper_ref, lower_ref, column_ref, row_ref, top_ref, bottom_ref, shifted):
    half_count, columns = upper_ref.shape
    depth = half_count // visits
    groups = columns // LANES
    low = lane_index((2 * half_count, LANES)) < SHIFT
    nothing = jnp.zeros((2 * half_count, LANES), F32)
    turned = {-1: nothing, groups: nothing}

    def turn(g):
        if g not in turned:
            lanes = slice(g * LANES, (g + 1) * LANES)
            value = jnp.concatenate([upper_ref[:, lanes], lower_ref[:, lanes]], axis=0)
            turned[g] = pltpu.roll(value.astype(F32), SHIFT, 1)
        return turned[g]

    def make_group(g):
        return jnp.where(low, turn(g - 1), turn(g)).astype(BF16)

    pieces = [
        [(place * half_count + v * depth, place * half_count + (v + 1) * depth) for place in (0, 1)]
        for v in range(visits)
    ]

    def put(start, totals):
        for v, total in enumerate(totals):
            lines = slice(v * depth, (v + 1) * depth)
            top_ref[lines, start : start + 2 * LANES] = total[:depth]
            bottom_ref[lines, start : start + 2 * LANES] = total[depth:]

    convolve(make_group, shifted, column_ref, row_ref, pieces, put, 4)


def own_part(upper, lower, column, own, visits):
    half_count, columns = upper.shape
    return pl.pallas_call(
        functools.partial(own_kernel, visits),
        out_shape=(held((half_count, columns), F32),) * 2,
        in_specs=[whole()] * 4,
        out_specs=(whole(),) * 2,
        scratch_shapes=[pltpu.VMEM((2 * half_count, columns + LANES), BF16)],
        compiler_params=LIMIT,
        cost_estimate=pl.CostEstimate(flops=10**9, bytes_accessed=10**7, transcendentals=0),
        name="own_rows",
    )(*kept(upper, lower, column, own))


def rim_kernel(visits, half, side_ref, edge_ref, column_ref, row_ref, part_ref, out_ref, shifted):
    edge, columns = edge_ref.shape
    rows = out_ref.shape[0] // visits
    width = out_ref.shape[1]
    groups = columns // LANES
    inner = width // LANES
    base = side_ref[0] * inner
    lane = lane_index((edge, LANES))

    def make_group(g):
        at = base + g
        lanes = pl.ds(pl.multiple_of(lax.rem(at, groups) * LANES, LANES), LANES)
        value = edge_ref[:, lanes]
        if g == 0:
            value = value.astype(F32)
            value = jnp.where(lane >= jnp.where(at == 0, SHIFT, 0), value, 0.0).astype(BF16)
        if g == inner:
            value = value.astype(F32)
            value = jnp.where(lane < jnp.where(at == groups, SHIFT, LANES), value, 0.0)
            value = value.astype(BF16)
        return value

    main = half // 8 * 8
    pieces = [[(v * main, (v + 1) * main), (visits * main, edge)] for v in range(visits)]

    def put(start, totals):
        source = pl.ds(pl.multiple_of(base * LANES + start, 2 * LANES), 2 * LANES)
        for v, total in enumerate(totals):
            lines = slice(v * rows, (v + 1) * rows)
            value = (total + part_ref[lines, source]).astype(out_ref.dtype)
            out_ref[lines, start : start + 2 * LANES] = value

    convolve(make_group, shifted, column_ref, row_ref, pieces, put, 8)


def rim_part(side, edge, column, table, part, visits, half):
    count, columns = part.shape
    width = columns // 2
    return pl.pallas_call(
        functools.partial(rim_kernel, visits, half),
        out_shape=held((count, width), BF16),
        in_specs=[whole(pltpu.SMEM)] + [whole()] * 4,
        out_specs=whole(),
        scratch_shapes=[pltpu.VMEM((edge.shape[0], width + LANES), BF16)],
        compiler_params=LIMIT,
    )(side, *kept(edge, column, table, part))


def norm_kernel(visits, bands, *refs):
    flag_refs = refs[:2]
    weight_ref, inverse_ref, count_ref = refs[2:]
    rows, width = inverse_ref.shape
    count = visits * rows
    high = min(16, rows // bands)
    members = [(side, v) for side in range(2) for v in range(visits)]
    levels = {}
    for side in range(2):
        found = flag_refs[side][count:, :LANES].astype(F32)
        for v in range(visits):
            for b in range(bands):
                spots = [(k * bands + b) * visits + v for k in range(3)]
                parts = [found[spot : spot + 1] for spot in spots]
                level = (parts[0] + parts[1]) + parts[2]
                levels[side, v, b] = jnp.broadcast_to(level, (high, LANES))
    count_ref[...] = jnp.zeros_like(count_ref)

    def body(step, carry):
        lanes = pl.ds(pl.multiple_of(step * LANES, LANES), LANES)
        for row in range(0, rows, high):
            denom = PRIOR_WEIGHT
            for m, (side, v) in enumerate(members):
                flag = flag_refs[side][v * rows + row : v * rows + row + high, lanes].astype(F32)
                weight = flag * levels[side, v, row // (rows // bands)]
                weight_ref[m * rows + row : m * rows + row + high, lanes] = weight
                count_ref[m * 8 : (m + 1) * 8, :] += folded(flag)
                denom = denom + weight
            inverse_ref[row : row + high, lanes] = 1.0 / denom
        return carry

    lax.fori_loop(0, width // LANES, body, 0, unroll=4)


def folded(value):
    total = value[:8]
    for start in range(8, value.shape[0], 8):
        total = total + value[start : start + 8]
    return total


def norms(own_flags, other_flags, visits, bands, rows):
    width = own_flags.shape[1]
    members = 2 * visits
    return pl.pallas_call(
        functools.partial(norm_kernel, visits, bands),
        out_shape=(
            held((members * rows, width), F32),
            held((rows, width), F32),
            held((members * 8, LANES), F32),
        ),
        in_specs=[whole()] * 2,
        out_specs=(whole(),) * 3,
        compiler_params=LIMIT,
        name="norms",
    )(*kept(own_flags, other_flags))


def residual_kernel(visits, first, last, side_ref, *refs):
    value_refs = refs[:2]
    weight_ref, inverse_ref = refs[2:4]
    if last:
        so_far_ref, count_ref, factor_ref, sums_ref, chi_ref = refs[4:]
        chi_ref[...] = so_far_ref[...]
    else:
        factor_ref, chi_ref = refs[4:]
        chi_ref[...] = jnp.zeros_like(chi_ref)
    depth = value_refs[0].shape[0] // visits
    rows, width = inverse_ref.shape
    high = min(16, depth)
    members = [(side, v) for side in range(2) for v in range(visits)]

    def body(step, carry):
        lanes = pl.ds(pl.multiple_of(step * LANES, LANES), LANES)
        for row in range(0, depth, high):
            values, weights = [], []
            numer = None
            for m, (side, v) in enumerate(members):
                at = slice(v * depth + row, v * depth + row + high)
                value = value_refs[side][at, lanes].astype(F32)
                at = m * rows + first + row
                weight = weight_ref[at : at + high, lanes]
                values.append(value)
                weights.append(weight)
                numer = weight * value if numer is None else numer + weight * value
            mean = numer * inverse_ref[first + row : first + row + high, lanes]
            for m in range(len(members)):
                residual = values[m] - mean
                term = weights[m] * (residual * residual)
                chi_ref[m * 8 : (m + 1) * 8, :] += folded(term)
                target = slice(m * depth + row, m * depth + row + high)
                factor_ref[target, lanes] = weights[m] / (CLIP_LEVEL + term)
        return carry

    lax.fori_loop(0, width // LANES, body, 0, unroll=4)
    if not last:
        return
    for k, ref in enumerate((chi_ref, count_ref)):
        lines = [
            jnp.sum(ref[m * 8 : (m + 1) * 8, :], axis=0, keepdims=True)
            for m in range(len(members))
        ]
        total = jnp.concatenate(lines, axis=0)
        sums_ref[k] = jnp.where(side_ref[0] == 0, total, pltpu.roll(total, visits, 0))


def residual_pass(side, values, weights, inverse, visits, first, *ending):
    count, width = values[0].shape
    members = 2 * visits
    last = len(ending) > 0
    chi = (members * 8, LANES)
    return pl.pallas_call(
        functools.partial(residual_kernel, visits, first, last),
        out_shape=(
            held((2 * count, width), F32),
            held((2, members, LANES) if last else chi, F32),
        ),
        in_specs=[whole(pltpu.SMEM)] + [whole()] * (4 + len(ending)),
        out_specs=(whole(), whole()),
        scratch_shapes=[pltpu.VMEM(chi, F32)] * last,
        compiler_params=LIMIT,
        name="residual_last" if last else "residual",
    )(side, *kept(*values, weights, inverse, *ending))


def final_kernel(visits, side_ref, sums_ref, *refs):
    parts = [refs[:3], refs[3:6]]
    out_ref, chi_ref, done, mean, sent = refs[6:]
    rows, width = done.shape
    high = min(16, rows // 2)
    sums = [
        jnp.where(side_ref[0] == 0, sums_ref[k], pltpu.roll(sums_ref[k], visits, 0))
        for k in range(2)
    ]
    chi = jnp.sum(sums[0], axis=1, keepdims=True) / jnp.sum(sums[1], axis=1, keepdims=True)
    scale = CLIP_LEVEL / (CHI_OFFSET + chi)
    for v in range(visits):
        mean[v] = chi[v, 0]
    chi_copy = pltpu.make_async_copy(mean, chi_ref, sent.at[1])
    chi_copy.start()
    scales = [jnp.broadcast_to(scale[m : m + 1], (high, LANES)) for m in range(2 * visits)]
    depth = rows // 2
    for lane in range(0, width, LANES):
        lanes = slice(lane, lane + LANES)
        for top, part in zip((0, depth), parts):
            for row in range(0, depth, high):
                numer = denom = None
                for m in range(2 * visits):
                    at = (m % visits) * depth + row
                    value = part[m // visits][at : at + high, lanes].astype(F32)
                    at = m * depth + row
                    revised = part[2][at : at + high, lanes] * scales[m]
                    numer = revised * value if numer is None else numer + revised * value
                    denom = revised if denom is None else denom + revised
                done[top + row : top + row + high, lanes] = numer / (denom + PRIOR_WEIGHT)
    copy = pltpu.make_async_copy(done, out_ref, sent.at[0])
    copy.start()
    chi_copy.wait()
    copy.wait()


def final_pass(side, sums, upper, lower, visits):
    count, width = upper[0].shape
    rows = 2 * count // visits
    return pl.pallas_call(
        functools.partial(final_kernel, visits),
        out_shape=(
            jax.ShapeDtypeStruct((rows, width), F32),
            jax.ShapeDtypeStruct((visits,), F32),
        ),
        in_specs=[whole(pltpu.SMEM)] + [whole()] * 7,
        out_specs=(pl.BlockSpec(memory_space=pl.ANY),) * 2,
        scratch_shapes=[
            pltpu.VMEM((rows, width), F32),
            pltpu.SMEM((visits,), F32),
            pltpu.SemaphoreType.DMA((2,)),
        ],
        compiler_params=LIMIT,
        name="final",
    )(side, *kept(sums, *upper, *lower))


def per_device(warps, badbits, coverage, variance, psf_index, psf_table, row_basis, col_basis):
    visits, rows, columns = warps.shape
    half = row_basis.shape[1] // 2
    strips = lax.axis_size("sky")
    up = [(i, i + 1) for i in range(strips - 1)]
    down = [(j, i) for i, j in up]
    swap = [(0, 1), (1, 0)]
    side = lax.axis_index("visit").astype(jnp.int32).reshape(1)

    last, lower = pack_rows(warps, half, False)
    before = lax.ppermute(last, "sky", up)
    send_weight, own_weight = pixel_weights(badbits, coverage, variance, side)
    other_weight = lax.ppermute(send_weight, "visit", swap)
    column, own, above, below = tables(psf_index, psf_table, row_basis, col_basis, visits, rows)
    leading, upper = pack_rows(warps, half, True, send_weight)
    after = lax.ppermute(leading, "sky", down)
    top, bottom = own_part(
        upper.reshape(-1, columns), lower.reshape(-1, columns), column, own, visits
    )
    send_top = rim_part(1 - side, before, column, above, top, visits, half)
    other_top = lax.ppermute(send_top, "visit", swap)
    own_top = rim_part(side, before, column, above, top, visits, half)
    weights, inverse, counts = norms(own_weight, other_weight, visits, coverage.shape[1], rows)
    top_factors, chi = residual_pass(side, (own_top, other_top), weights, inverse, visits, 0)
    send_value = rim_part(1 - side, after, column, below, bottom, visits, half)
    other_value = lax.ppermute(send_value, "visit", swap)
    own_value = rim_part(side, after, column, below, bottom, visits, half)
    factors, sums = residual_pass(
        side, (own_value, other_value), weights, inverse, visits, rows // 2, chi, counts
    )
    sums = sums + lax.ppermute(sums, "visit", swap)
    step = 1
    while step < strips:
        pairs = [(2 * i + v, 2 * (i ^ step) + 1 - v) for i in range(strips) for v in (0, 1)]
        sums = sums + lax.ppermute(sums, ("sky", "visit"), pairs)
        step *= 2
    upper = (own_top, other_top, top_factors)
    return final_pass(side, sums, upper, (own_value, other_value, factors), visits)


def solution(mesh):
    placed = (
        P(("tract", "visit"), "sky", None),
        P(("tract", "visit"), "sky", None),
        P(("tract", "visit"), "sky"),
        P(("tract", "visit"), "sky"),
        P(("tract", "visit")),
        P(),
        P(),
        P(),
    )
    return jax.shard_map(
        per_device,
        mesh=mesh,
        in_specs=placed,
        out_specs=(P(("tract", "sky"), "visit"), P(("tract", "visit"))),
        check_vma=False,
    )
```

```python
import functools

import jax
import jax.numpy as jnp
from jax import lax
from jax.experimental import pallas as pl
from jax.experimental.pallas import tpu as pltpu
from jax.sharding import PartitionSpec as P

PRIOR_WEIGHT = 1.0
CLIP_LEVEL = 9.0
CHI_OFFSET = 0.5
LANES = 128
SHIFT = LANES // 2
F32 = jnp.float32
BF16 = jnp.bfloat16


def whole(space=pltpu.VMEM):
    return pl.BlockSpec(memory_space=space)


def kept(*arrays):
    return [pltpu.with_memory_space_constraint(array, pltpu.VMEM) for array in arrays]


def away(*arrays):
    return [pltpu.with_memory_space_constraint(array, pltpu.HBM) for array in arrays]


def held(shape, dtype):
    return pltpu.VMEM(shape, dtype)


LIMIT = pltpu.CompilerParams(vmem_limit_bytes=20 * 1024 * 1024)


def lane_index(shape):
    return lax.broadcasted_iota(jnp.int32, shape, len(shape) - 1)


def pack_kernel(half, first, skip, x_ref, *refs):
    edge_ref, rows_ref, arrived = refs[-3:]
    visits, depth, columns = rows_ref.shape
    chunks = arrived.shape[0]
    width = columns // chunks
    copies = []
    for c in range(chunks):
        lanes = slice(c * width, (c + 1) * width)
        copies.append(
            pltpu.make_async_copy(
                x_ref.at[:, first : first + depth, lanes], rows_ref.at[:, :, lanes], arrived.at[c]
            )
        )
        copies[c].start()
    main = half // 8 * 8
    rest = half - main
    shape = (visits * half, visits * depth)
    target = lax.broadcasted_iota(jnp.int32, shape, 0)
    source_row = lane_index(shape)
    line = jnp.where(
        target < visits * main,
        lax.div(target, max(main, 1)) * depth + lax.rem(target, max(main, 1)),
        lax.div(target - visits * main, max(rest, 1)) * depth
        + main
        + lax.rem(target - visits * main, max(rest, 1)),
    )
    select = jnp.where(source_row == line + skip, 1.0, 0.0).astype(BF16)
    low = lane_index((edge_ref.shape[0], LANES)) < SHIFT
    step = 2 * LANES

    def put(g, value):
        edge_ref[:, g * LANES : (g + 1) * LANES] = value.astype(BF16)

    before = opening = None
    for start in range(0, columns, step):
        if start % width == 0:
            copies[start // width].wait()
        source = rows_ref[:, :, start : start + step].reshape(visits * depth, step)
        found = jnp.dot(select, source, preferred_element_type=F32)
        for part in range(2):
            here = pltpu.roll(found[:, part * LANES : (part + 1) * LANES], SHIFT, 1)
            if before is None:
                opening = here
            else:
                put(start // LANES + part, jnp.where(low, before, here))
            before = here
    put(0, jnp.where(low, before, opening))


def pack_rows(warps, half, upper, *after):
    visits, rows, columns = warps.shape
    depth = rows // 2
    assert depth >= half and rows % 2 == 0
    first = 0 if upper else depth
    skip = 0 if upper else depth - half
    chunks = 1
    return pl.pallas_call(
        functools.partial(pack_kernel, half, first, skip),
        out_shape=(held((visits * half, columns), BF16), held((visits, depth, columns), BF16)),
        in_specs=[pl.BlockSpec(memory_space=pl.ANY)] * (1 + len(after)),
        out_specs=(whole(),) * 2,
        scratch_shapes=[pltpu.SemaphoreType.DMA((chunks,))],
        compiler_params=LIMIT,
        name="pack_upper" if upper else "pack_lower",
    )(*away(warps), *after)


def level_rows(visits, bands):
    return -(-3 * visits * bands // 16) * 16


def weight_kernel(visits, bands, side_ref, cover_ref, var_ref, bits_ref, send_ref, keep_ref):
    count = bits_ref.shape[0]
    rows = count // visits
    high = rows // bands
    width = bits_ref.shape[1]
    steps = send_ref.shape[1] // width
    step = pl.program_id(0)
    half = lax.div(step, steps)
    lanes = pl.ds(pl.multiple_of(lax.rem(step, steps) * width, width), width)
    extra = level_rows(visits, bands)

    def fill(out_ref):
        line = lax.broadcasted_iota(jnp.int32, (extra, LANES), 0)
        levels = jnp.zeros((extra, LANES), F32)
        for v in range(visits):
            for b in range(bands):
                at = slice(v * rows + b * high, v * rows + (b + 1) * high)
                covers = jnp.where(cover_ref[b, v] != 0, 7, 0)
                usable = jnp.bitwise_and(bits_ref[at, :], 7) < covers
                out_ref[at, lanes] = jnp.where(usable, 1.0, 0.0).astype(BF16)
                left = 1.0 / jnp.full((8, LANES), var_ref[b, v], F32)
                for k in range(3):
                    part = left.astype(BF16).astype(F32)
                    left = left - part
                    spot = (k * bands + b) * visits + v
                    levels = jnp.where(line == spot, part[:1], levels)
        wide = jnp.concatenate([levels.astype(BF16)] * (width // LANES), axis=1)
        out_ref[count:, lanes] = wide

    pl.when(half == 0)(lambda: fill(send_ref))
    pl.when(half == 1)(lambda: fill(keep_ref))


def pixel_weights(badbits, coverage, variance, side):
    visits, rows, columns = badbits.shape
    bands = coverage.shape[1]
    (bits,) = away(badbits.reshape(visits * rows, columns))
    width = columns // 2
    tile = width
    count = width // tile
    shape = held((visits * rows + level_rows(visits, bands), width), BF16)

    def block(i, s):
        first = i < count
        return 0, jnp.where(first, (1 - s[0]) * count + i, s[0] * count + i - count)

    return pl.pallas_call(
        functools.partial(weight_kernel, visits, bands),
        out_shape=(shape, shape),
        grid_spec=pltpu.PrefetchScalarGridSpec(
            num_scalar_prefetch=1,
            grid=(2 * count,),
            in_specs=[
                whole(pltpu.SMEM),
                whole(pltpu.SMEM),
                pl.BlockSpec((visits * rows, tile), block),
            ],
            out_specs=(whole(), whole()),
        ),
        compiler_params=LIMIT,
        name="weights",
    )(side, *away(coverage.T, variance.T), bits)


def split(value):
    high = value.astype(BF16)
    return high, (value - high.astype(F32)).astype(BF16)


def edge_segments(visits, rows, half, below):
    main = half // 8 * 8
    rest = half - main
    origin = half + rows if below else 0
    segments = []
    for v in range(visits):
        first = main + v * rest
        segments.append([(0, main, origin), (first, first + rest, origin + main - first)])
    return segments, main + visits * rest


def table_kernel(visits, rows, half, index_ref, table_ref, row_ref, col_ref, column_out, own_out, above_out, below_out):
    bases, taps = row_ref.shape
    window = 2 * LANES

    def spread(line, shift, count):
        line = jnp.broadcast_to(line, (8, LANES))
        block = pltpu.roll(line, 0, 1, stride=1, stride_axis=0)
        blocks = [pltpu.roll(block, (shift + i) % LANES, 1) for i in range(0, count, 8)]
        return jnp.concatenate(blocks, axis=0)

    tap = lax.broadcasted_iota(jnp.int32, (taps, LANES), 0)
    place = lane_index((taps, LANES))
    ahead = jnp.where(place == tap, 1.0, 0.0).astype(BF16)
    back = jnp.where(place == taps - 1 - tap, 1.0, 0.0).astype(BF16)
    row_lines = jnp.dot(row_ref[...], ahead, preferred_element_type=F32)
    col_lines = jnp.dot(col_ref[...], back, preferred_element_type=F32)
    k = lax.broadcasted_iota(jnp.int32, (window, LANES), 0)
    gap = k - lane_index((window, LANES))
    inside = (gap >= 0) & (gap < LANES)
    for b in range(bases):
        line = col_lines[b : b + 1, :]
        band = jnp.where(inside, spread(line, SHIFT - half, window), 0.0)
        column_out[:, b * LANES : (b + 1) * LANES] = band.astype(BF16)

    depth = rows // 2

    def assemble(out_ref, high, segments, top, lines):
        lane = lane_index((lines, LANES))
        for b in range(bases):
            start = b * high % LANES
            group = b * high // LANES * LANES
            line = row_lines[b : b + 1, :]
            found = {}
            for v in range(visits):
                total = jnp.zeros((lines, LANES), F32)
                for first, last, offset in segments[v]:
                    if first == last:
                        continue
                    key = (first, last, offset)
                    if key not in found:
                        mask = (lane >= start + first) & (lane < start + last)
                        turned = spread(line, start - offset + top, lines)
                        found[key] = jnp.where(mask, turned, 0.0)
                    total = total + found[key]
                high_part, low_part = split(total * table_ref[b, index_ref[v]])
                at = 2 * v * lines
                lanes = slice(group, group + LANES)
                if start == 0:
                    out_ref[at : at + lines, lanes] = high_part
                    out_ref[at + lines : at + 2 * lines, lanes] = low_part
                else:
                    out_ref[at : at + lines, lanes] += high_part
                    out_ref[at + lines : at + 2 * lines, lanes] += low_part

    assemble(own_out, rows, [[(0, rows, half)]] * visits, 0, rows)
    for below, out in enumerate((above_out, below_out)):
        segments, high = edge_segments(visits, rows, half, below)
        assemble(out, high, segments, below * depth, depth)


def tables(psf_index, psf_table, row_basis, col_basis, visits, rows):
    bases, taps = row_basis.shape
    half = taps // 2
    rim = (visits * rows, bases * edge_segments(visits, rows, half, 0)[1])
    return pl.pallas_call(
        functools.partial(table_kernel, visits, rows, half),
        out_shape=(
            held((2 * LANES, bases * LANES), BF16),
            held((2 * visits * rows, bases * rows), BF16),
            held(rim, BF16),
            held(rim, BF16),
        ),
        in_specs=[whole(pltpu.SMEM)] * 2 + [whole()] * 2,
        out_specs=(whole(),) * 4,
        compiler_params=LIMIT,
        name="tables",
    )(psf_index, psf_table.T, row_basis, col_basis)


def column_pass(windows, column_ref):
    return jnp.dot(
        jnp.concatenate(windows, axis=0), column_ref[...], preferred_element_type=F32
    )


def row_pass(layers, count, row_ref, pieces, bases):
    high = row_ref.shape[0] // (2 * len(pieces))
    for first in range(0, layers.shape[0] // count, 2):
        totals = []
        for v, parts in enumerate(pieces):
            sides = []
            for n in (first, first + 1):
                taken = [
                    layers[n * count + top : n * count + last, b * LANES : (b + 1) * LANES]
                    for b in range(bases)
                    for top, last in parts
                    if last > top
                ]
                sides.append(jnp.concatenate(taken, axis=0).astype(BF16))
            total = jnp.dot(
                row_ref[2 * v * high : 2 * (v + 1) * high, :],
                jnp.concatenate(sides, axis=1),
                preferred_element_type=F32,
            )
            totals.append(total[:high] + total[high:])
        yield first, totals


def convolve(make_group, shifted, column_ref, row_ref, pieces, put, blocks):
    count = shifted.shape[0]
    groups = shifted.shape[1] // LANES - 1
    bases = column_ref.shape[1] // LANES
    blocks = min(blocks, groups)
    made = [0]

    def columns_of(step):
        while made[0] <= blocks * (step + 1):
            g = made[0]
            shifted[:, g * LANES : (g + 1) * LANES] = make_group(g)
            made[0] += 1
        starts = [(blocks * step + n) * LANES for n in range(blocks)]
        return column_pass([shifted[:, at : at + 2 * LANES] for at in starts], column_ref)

    ahead = columns_of(0)
    for step in range(groups // blocks):
        layers = ahead
        if step + 1 < groups // blocks:
            ahead = columns_of(step + 1)
        for first, totals in row_pass(layers, count, row_ref, pieces, bases):
            put((blocks * step + first) * LANES, totals)


def own_kernel(visits, upper_ref, lower_ref, column_ref, row_ref, top_ref, bottom_ref, shifted):
    half_count, columns = upper_ref.shape
    depth = half_count // visits
    groups = columns // LANES
    low = lane_index((2 * half_count, LANES)) < SHIFT
    nothing = jnp.zeros((2 * half_count, LANES), F32)
    turned = {-1: nothing, groups: nothing}

    def turn(g):
        if g not in turned:
            lanes = slice(g * LANES, (g + 1) * LANES)
            value = jnp.concatenate([upper_ref[:, lanes], lower_ref[:, lanes]], axis=0)
            turned[g] = pltpu.roll(value.astype(F32), SHIFT, 1)
        return turned[g]

    def make_group(g):
        return jnp.where(low, turn(g - 1), turn(g)).astype(BF16)

    pieces = [
        [(place * half_count + v * depth, place * half_count + (v + 1) * depth) for place in (0, 1)]
        for v in range(visits)
    ]

    def put(start, totals):
        for v, total in enumerate(totals):
            lines = slice(v * depth, (v + 1) * depth)
            top_ref[lines, start : start + 2 * LANES] = total[:depth]
            bottom_ref[lines, start : start + 2 * LANES] = total[depth:]

    convolve(make_group, shifted, column_ref, row_ref, pieces, put, 4)


def own_part(upper, lower, column, own, visits):
    half_count, columns = upper.shape
    return pl.pallas_call(
        functools.partial(own_kernel, visits),
        out_shape=(held((half_count, columns), F32),) * 2,
        in_specs=[whole()] * 4,
        out_specs=(whole(),) * 2,
        scratch_shapes=[pltpu.VMEM((2 * half_count, columns + LANES), BF16)],
        compiler_params=LIMIT,
        cost_estimate=pl.CostEstimate(flops=10**9, bytes_accessed=10**7, transcendentals=0),
        name="own_rows",
    )(*kept(upper, lower, column, own))


def rim_kernel(visits, half, side_ref, edge_ref, column_ref, row_ref, part_ref, out_ref, shifted):
    edge, columns = edge_ref.shape
    rows = out_ref.shape[0] // visits
    width = out_ref.shape[1]
    groups = columns // LANES
    inner = width // LANES
    base = side_ref[0] * inner
    lane = lane_index((edge, LANES))

    def make_group(g):
        at = base + g
        lanes = pl.ds(pl.multiple_of(lax.rem(at, groups) * LANES, LANES), LANES)
        value = edge_ref[:, lanes]
        if g == 0:
            value = value.astype(F32)
            value = jnp.where(lane >= jnp.where(at == 0, SHIFT, 0), value, 0.0).astype(BF16)
        if g == inner:
            value = value.astype(F32)
            value = jnp.where(lane < jnp.where(at == groups, SHIFT, LANES), value, 0.0)
            value = value.astype(BF16)
        return value

    main = half // 8 * 8
    pieces = [[(v * main, (v + 1) * main), (visits * main, edge)] for v in range(visits)]

    def put(start, totals):
        source = pl.ds(pl.multiple_of(base * LANES + start, 2 * LANES), 2 * LANES)
        for v, total in enumerate(totals):
            lines = slice(v * rows, (v + 1) * rows)
            value = (total + part_ref[lines, source]).astype(out_ref.dtype)
            out_ref[lines, start : start + 2 * LANES] = value

    convolve(make_group, shifted, column_ref, row_ref, pieces, put, 8)


def rim_part(side, edge, column, table, part, visits, half):
    count, columns = part.shape
    width = columns // 2
    return pl.pallas_call(
        functools.partial(rim_kernel, visits, half),
        out_shape=held((count, width), BF16),
        in_specs=[whole(pltpu.SMEM)] + [whole()] * 4,
        out_specs=whole(),
        scratch_shapes=[pltpu.VMEM((edge.shape[0], width + LANES), BF16)],
        compiler_params=LIMIT,
    )(side, *kept(edge, column, table, part))


def norm_kernel(visits, bands, *refs):
    flag_refs = refs[:2]
    weight_ref, inverse_ref, count_ref = refs[2:]
    rows, width = inverse_ref.shape
    count = visits * rows
    high = min(16, rows // bands)
    members = [(side, v) for side in range(2) for v in range(visits)]
    levels = {}
    for side in range(2):
        found = flag_refs[side][count:, :LANES].astype(F32)
        for v in range(visits):
            for b in range(bands):
                spots = [(k * bands + b) * visits + v for k in range(3)]
                parts = [found[spot : spot + 1] for spot in spots]
                level = (parts[0] + parts[1]) + parts[2]
                levels[side, v, b] = jnp.broadcast_to(level, (high, LANES))
    count_ref[...] = jnp.zeros_like(count_ref)

    def body(step, carry):
        lanes = pl.ds(pl.multiple_of(step * LANES, LANES), LANES)
        for row in range(0, rows, high):
            denom = PRIOR_WEIGHT
            for m, (side, v) in enumerate(members):
                flag = flag_refs[side][v * rows + row : v * rows + row + high, lanes].astype(F32)
                weight = flag * levels[side, v, row // (rows // bands)]
                weight_ref[m * rows + row : m * rows + row + high, lanes] = weight
                count_ref[m * 8 : (m + 1) * 8, :] += folded(flag)
                denom = denom + weight
            inverse_ref[row : row + high, lanes] = 1.0 / denom
        return carry

    lax.fori_loop(0, width // LANES, body, 0, unroll=4)


def folded(value):
    total = value[:8]
    for start in range(8, value.shape[0], 8):
        total = total + value[start : start + 8]
    return total


def norms(own_flags, other_flags, visits, bands, rows):
    width = own_flags.shape[1]
    members = 2 * visits
    return pl.pallas_call(
        functools.partial(norm_kernel, visits, bands),
        out_shape=(
            held((members * rows, width), F32),
            held((rows, width), F32),
            held((members * 8, LANES), F32),
        ),
        in_specs=[whole()] * 2,
        out_specs=(whole(),) * 3,
        compiler_params=LIMIT,
        name="norms",
    )(*kept(own_flags, other_flags))


def residual_kernel(visits, first, last, side_ref, *refs):
    value_refs = refs[:2]
    weight_ref, inverse_ref = refs[2:4]
    if last:
        so_far_ref, count_ref, factor_ref, sums_ref, chi_ref = refs[4:]
        chi_ref[...] = so_far_ref[...]
    else:
        factor_ref, chi_ref = refs[4:]
        chi_ref[...] = jnp.zeros_like(chi_ref)
    depth = value_refs[0].shape[0] // visits
    rows, width = inverse_ref.shape
    high = min(16, depth)
    members = [(side, v) for side in range(2) for v in range(visits)]

    def body(step, carry):
        lanes = pl.ds(pl.multiple_of(step * LANES, LANES), LANES)
        for row in range(0, depth, high):
            values, weights = [], []
            numer = None
            for m, (side, v) in enumerate(members):
                at = slice(v * depth + row, v * depth + row + high)
                value = value_refs[side][at, lanes].astype(F32)
                at = m * rows + first + row
                weight = weight_ref[at : at + high, lanes]
                values.append(value)
                weights.append(weight)
                numer = weight * value if numer is None else numer + weight * value
            mean = numer * inverse_ref[first + row : first + row + high, lanes]
            for m in range(len(members)):
                residual = values[m] - mean
                term = weights[m] * (residual * residual)
                chi_ref[m * 8 : (m + 1) * 8, :] += folded(term)
                target = slice(m * depth + row, m * depth + row + high)
                factor_ref[target, lanes] = weights[m] / (CLIP_LEVEL + term)
        return carry

    lax.fori_loop(0, width // LANES, body, 0, unroll=4)
    if not last:
        return
    for k, ref in enumerate((chi_ref, count_ref)):
        lines = [
            jnp.sum(ref[m * 8 : (m + 1) * 8, :], axis=0, keepdims=True)
            for m in range(len(members))
        ]
        total = jnp.concatenate(lines, axis=0)
        sums_ref[k] = jnp.where(side_ref[0] == 0, total, pltpu.roll(total, visits, 0))


def residual_pass(side, values, weights, inverse, visits, first, *ending):
    count, width = values[0].shape
    members = 2 * visits
    last = len(ending) > 0
    chi = (members * 8, LANES)
    return pl.pallas_call(
        functools.partial(residual_kernel, visits, first, last),
        out_shape=(
            held((2 * count, width), F32),
            held((2, members, LANES) if last else chi, F32),
        ),
        in_specs=[whole(pltpu.SMEM)] + [whole()] * (4 + len(ending)),
        out_specs=(whole(), whole()),
        scratch_shapes=[pltpu.VMEM(chi, F32)] * last,
        compiler_params=LIMIT,
        name="residual_last" if last else "residual",
    )(side, *kept(*values, weights, inverse, *ending))


def final_kernel(visits, side_ref, sums_ref, *refs):
    parts = [refs[:3], refs[3:6]]
    out_ref, chi_ref, done, mean, sent = refs[6:]
    rows, width = done.shape
    high = min(16, rows // 2)
    sums = [
        jnp.where(side_ref[0] == 0, sums_ref[k], pltpu.roll(sums_ref[k], visits, 0))
        for k in range(2)
    ]
    chi = jnp.sum(sums[0], axis=1, keepdims=True) / jnp.sum(sums[1], axis=1, keepdims=True)
    scale = CLIP_LEVEL / (CHI_OFFSET + chi)
    for v in range(visits):
        mean[v] = chi[v, 0]
    chi_copy = pltpu.make_async_copy(mean, chi_ref, sent.at[1])
    chi_copy.start()
    scales = [jnp.broadcast_to(scale[m : m + 1], (high, LANES)) for m in range(2 * visits)]
    depth = rows // 2
    for lane in range(0, width, LANES):
        lanes = slice(lane, lane + LANES)
        for top, part in zip((0, depth), parts):
            for row in range(0, depth, high):
                numer = denom = None
                for m in range(2 * visits):
                    at = (m % visits) * depth + row
                    value = part[m // visits][at : at + high, lanes].astype(F32)
                    at = m * depth + row
                    revised = part[2][at : at + high, lanes] * scales[m]
                    numer = revised * value if numer is None else numer + revised * value
                    denom = revised if denom is None else denom + revised
                done[top + row : top + row + high, lanes] = numer / (denom + PRIOR_WEIGHT)
    copy = pltpu.make_async_copy(done, out_ref, sent.at[0])
    copy.start()
    chi_copy.wait()
    copy.wait()


def final_pass(side, sums, upper, lower, visits):
    count, width = upper[0].shape
    rows = 2 * count // visits
    return pl.pallas_call(
        functools.partial(final_kernel, visits),
        out_shape=(
            jax.ShapeDtypeStruct((rows, width), F32),
            jax.ShapeDtypeStruct((visits,), F32),
        ),
        in_specs=[whole(pltpu.SMEM)] + [whole()] * 7,
        out_specs=(pl.BlockSpec(memory_space=pl.ANY),) * 2,
        scratch_shapes=[
            pltpu.VMEM((rows, width), F32),
            pltpu.SMEM((visits,), F32),
            pltpu.SemaphoreType.DMA((2,)),
        ],
        compiler_params=LIMIT,
        name="final",
    )(side, *kept(sums, *upper, *lower))


def partners(strips, step, crossing):
    turn = 1 if crossing else 0
    return [(2 * i + v, 2 * (i ^ step) + (v ^ turn)) for i in range(strips) for v in (0, 1)]


def per_device(warps, badbits, coverage, variance, psf_index, psf_table, row_basis, col_basis):
    visits, rows, columns = warps.shape
    half = row_basis.shape[1] // 2
    strips = lax.axis_size("sky")
    up = [(i, i + 1) for i in range(strips - 1)]
    down = [(j, i) for i, j in up]
    swap = [(0, 1), (1, 0)]
    side = lax.axis_index("visit").astype(jnp.int32).reshape(1)

    last, lower = pack_rows(warps, half, False)
    before = lax.ppermute(last, "sky", up)
    send_weight, own_weight = pixel_weights(badbits, coverage, variance, side)
    other_weight = lax.ppermute(send_weight, "visit", swap)
    column, own, above, below = tables(psf_index, psf_table, row_basis, col_basis, visits, rows)
    leading, upper = pack_rows(warps, half, True, send_weight)
    after = lax.ppermute(leading, "sky", down)
    top, bottom = own_part(
        upper.reshape(-1, columns), lower.reshape(-1, columns), column, own, visits
    )
    send_top = rim_part(1 - side, before, column, above, top, visits, half)
    other_top = lax.ppermute(send_top, "visit", swap)
    own_top = rim_part(side, before, column, above, top, visits, half)
    weights, inverse, counts = norms(own_weight, other_weight, visits, coverage.shape[1], rows)
    top_factors, chi = residual_pass(side, (own_top, other_top), weights, inverse, visits, 0)
    send_value = rim_part(1 - side, after, column, below, bottom, visits, half)
    other_value = lax.ppermute(send_value, "visit", swap)
    own_value = rim_part(side, after, column, below, bottom, visits, half)
    factors, sums = residual_pass(
        side, (own_value, other_value), weights, inverse, visits, rows // 2, chi, counts
    )
    step = 1
    while step < strips:
        crossing = lax.ppermute(sums, ("sky", "visit"), partners(strips, step, True))
        if 4 * step <= strips:
            second = lax.ppermute(sums, ("sky", "visit"), partners(strips, 2 * step, True))
            third = lax.ppermute(sums, ("sky", "visit"), partners(strips, 3 * step, False))
            sums = (sums + crossing) + (second + third)
            step *= 4
        else:
            sums = sums + crossing
            step *= 2
    sums = sums + lax.ppermute(sums, "visit", swap)
    upper = (own_top, other_top, top_factors)
    return final_pass(side, sums, upper, (own_value, other_value, factors), visits)


def solution(mesh):
    placed = (
        P(("tract", "visit"), "sky", None),
        P(("tract", "visit"), "sky", None),
        P(("tract", "visit"), "sky"),
        P(("tract", "visit"), "sky"),
        P(("tract", "visit")),
        P(),
        P(),
        P(),
    )
    return jax.shard_map(
        per_device,
        mesh=mesh,
        in_specs=placed,
        out_specs=(P(("tract", "sky"), "visit"), P(("tract", "visit"))),
        check_vma=False,
    )
```

```python
import functools

import jax
import jax.numpy as jnp
from jax import lax
from jax.experimental import pallas as pl
from jax.experimental.pallas import tpu as pltpu
from jax.sharding import PartitionSpec as P

PRIOR_WEIGHT = 1.0
CLIP_LEVEL = 9.0
CHI_OFFSET = 0.5
LANES = 128
SHIFT = LANES // 2
F32 = jnp.float32
BF16 = jnp.bfloat16


def whole(space=pltpu.VMEM):
    return pl.BlockSpec(memory_space=space)


def kept(*arrays):
    return [pltpu.with_memory_space_constraint(array, pltpu.VMEM) for array in arrays]


def away(*arrays):
    return [pltpu.with_memory_space_constraint(array, pltpu.HBM) for array in arrays]


def held(shape, dtype):
    return pltpu.VMEM(shape, dtype)


LIMIT = pltpu.CompilerParams(vmem_limit_bytes=20 * 1024 * 1024)


def lane_index(shape):
    return lax.broadcasted_iota(jnp.int32, shape, len(shape) - 1)


def pack_kernel(half, first, skip, x_ref, *refs):
    edge_ref, rows_ref, arrived = refs[-3:]
    visits, depth, columns = rows_ref.shape
    chunks = arrived.shape[0]
    width = columns // chunks
    copies = []
    for c in range(chunks):
        lanes = slice(c * width, (c + 1) * width)
        copies.append(
            pltpu.make_async_copy(
                x_ref.at[:, first : first + depth, lanes], rows_ref.at[:, :, lanes], arrived.at[c]
            )
        )
        copies[c].start()
    main = half // 8 * 8
    rest = half - main
    shape = (visits * half, visits * depth)
    target = lax.broadcasted_iota(jnp.int32, shape, 0)
    source_row = lane_index(shape)
    line = jnp.where(
        target < visits * main,
        lax.div(target, max(main, 1)) * depth + lax.rem(target, max(main, 1)),
        lax.div(target - visits * main, max(rest, 1)) * depth
        + main
        + lax.rem(target - visits * main, max(rest, 1)),
    )
    select = jnp.where(source_row == line + skip, 1.0, 0.0).astype(BF16)
    low = lane_index((edge_ref.shape[0], LANES)) < SHIFT
    step = 2 * LANES

    def put(g, value):
        edge_ref[:, g * LANES : (g + 1) * LANES] = value.astype(BF16)

    before = opening = None
    for start in range(0, columns, step):
        if start % width == 0:
            copies[start // width].wait()
        source = rows_ref[:, :, start : start + step].reshape(visits * depth, step)
        found = jnp.dot(select, source, preferred_element_type=F32)
        for part in range(2):
            here = pltpu.roll(found[:, part * LANES : (part + 1) * LANES], SHIFT, 1)
            if before is None:
                opening = here
            else:
                put(start // LANES + part, jnp.where(low, before, here))
            before = here
    put(0, jnp.where(low, before, opening))


def pack_rows(warps, half, upper, *after):
    visits, rows, columns = warps.shape
    depth = rows // 2
    assert depth >= half and rows % 2 == 0
    first = 0 if upper else depth
    skip = 0 if upper else depth - half
    chunks = 1
    return pl.pallas_call(
        functools.partial(pack_kernel, half, first, skip),
        out_shape=(held((visits * half, columns), BF16), held((visits, depth, columns), BF16)),
        in_specs=[pl.BlockSpec(memory_space=pl.ANY)] * (1 + len(after)),
        out_specs=(whole(),) * 2,
        scratch_shapes=[pltpu.SemaphoreType.DMA((chunks,))],
        compiler_params=LIMIT,
        name="pack_upper" if upper else "pack_lower",
    )(*away(warps), *after)


def level_rows(visits, bands):
    return -(-3 * visits * bands // 16) * 16


def weight_kernel(visits, bands, side_ref, cover_ref, var_ref, bits_ref, send_ref, keep_ref):
    count = bits_ref.shape[0]
    rows = count // visits
    high = rows // bands
    width = bits_ref.shape[1]
    steps = send_ref.shape[1] // width
    step = pl.program_id(0)
    half = lax.div(step, steps)
    lanes = pl.ds(pl.multiple_of(lax.rem(step, steps) * width, width), width)
    extra = level_rows(visits, bands)

    def fill(out_ref):
        line = lax.broadcasted_iota(jnp.int32, (extra, LANES), 0)
        levels = jnp.zeros((extra, LANES), F32)
        for v in range(visits):
            for b in range(bands):
                at = slice(v * rows + b * high, v * rows + (b + 1) * high)
                covers = jnp.where(cover_ref[b, v] != 0, 7, 0)
                usable = jnp.bitwise_and(bits_ref[at, :], 7) < covers
                out_ref[at, lanes] = jnp.where(usable, 1.0, 0.0).astype(BF16)
                left = 1.0 / jnp.full((8, LANES), var_ref[b, v], F32)
                for k in range(3):
                    part = left.astype(BF16).astype(F32)
                    left = left - part
                    spot = (k * bands + b) * visits + v
                    levels = jnp.where(line == spot, part[:1], levels)
        wide = jnp.concatenate([levels.astype(BF16)] * (width // LANES), axis=1)
        out_ref[count:, lanes] = wide

    pl.when(half == 0)(lambda: fill(send_ref))
    pl.when(half == 1)(lambda: fill(keep_ref))


def pixel_weights(badbits, coverage, variance, side):
    visits, rows, columns = badbits.shape
    bands = coverage.shape[1]
    (bits,) = away(badbits.reshape(visits * rows, columns))
    width = columns // 2
    tile = width
    count = width // tile
    shape = held((visits * rows + level_rows(visits, bands), width), BF16)

    def block(i, s):
        first = i < count
        return 0, jnp.where(first, (1 - s[0]) * count + i, s[0] * count + i - count)

    return pl.pallas_call(
        functools.partial(weight_kernel, visits, bands),
        out_shape=(shape, shape),
        grid_spec=pltpu.PrefetchScalarGridSpec(
            num_scalar_prefetch=1,
            grid=(2 * count,),
            in_specs=[
                whole(pltpu.SMEM),
                whole(pltpu.SMEM),
                pl.BlockSpec((visits * rows, tile), block),
            ],
            out_specs=(whole(), whole()),
        ),
        compiler_params=LIMIT,
        name="weights",
    )(side, *away(coverage.T, variance.T), bits)


def split(value):
    high = value.astype(BF16)
    return high, (value - high.astype(F32)).astype(BF16)


def edge_segments(visits, rows, half, below):
    main = half // 8 * 8
    rest = half - main
    origin = half + rows if below else 0
    segments = []
    for v in range(visits):
        first = main + v * rest
        segments.append([(0, main, origin), (first, first + rest, origin + main - first)])
    return segments, main + visits * rest


def table_kernel(visits, rows, half, index_ref, table_ref, row_ref, col_ref, column_out, own_out, above_out, below_out):
    bases, taps = row_ref.shape
    window = 2 * LANES

    def spread(line, shift, count):
        line = jnp.broadcast_to(line, (8, LANES))
        block = pltpu.roll(line, 0, 1, stride=1, stride_axis=0)
        blocks = [pltpu.roll(block, (shift + i) % LANES, 1) for i in range(0, count, 8)]
        return jnp.concatenate(blocks, axis=0)

    tap = lax.broadcasted_iota(jnp.int32, (taps, LANES), 0)
    place = lane_index((taps, LANES))
    ahead = jnp.where(place == tap, 1.0, 0.0).astype(BF16)
    back = jnp.where(place == taps - 1 - tap, 1.0, 0.0).astype(BF16)
    row_lines = jnp.dot(row_ref[...], ahead, preferred_element_type=F32)
    col_lines = jnp.dot(col_ref[...], back, preferred_element_type=F32)
    k = lax.broadcasted_iota(jnp.int32, (window, LANES), 0)
    gap = k - lane_index((window, LANES))
    inside = (gap >= 0) & (gap < LANES)
    for b in range(bases):
        line = col_lines[b : b + 1, :]
        band = jnp.where(inside, spread(line, SHIFT - half, window), 0.0)
        column_out[:, b * LANES : (b + 1) * LANES] = band.astype(BF16)

    depth = rows // 2

    def assemble(out_ref, high, segments, top, lines):
        lane = lane_index((lines, LANES))
        for b in range(bases):
            start = b * high % LANES
            group = b * high // LANES * LANES
            line = row_lines[b : b + 1, :]
            found = {}
            for v in range(visits):
                total = jnp.zeros((lines, LANES), F32)
                for first, last, offset in segments[v]:
                    if first == last:
                        continue
                    key = (first, last, offset)
                    if key not in found:
                        mask = (lane >= start + first) & (lane < start + last)
                        turned = spread(line, start - offset + top, lines)
                        found[key] = jnp.where(mask, turned, 0.0)
                    total = total + found[key]
                high_part, low_part = split(total * table_ref[b, index_ref[v]])
                at = 2 * v * lines
                lanes = slice(group, group + LANES)
                if start == 0:
                    out_ref[at : at + lines, lanes] = high_part
                    out_ref[at + lines : at + 2 * lines, lanes] = low_part
                else:
                    out_ref[at : at + lines, lanes] += high_part
                    out_ref[at + lines : at + 2 * lines, lanes] += low_part

    assemble(own_out, rows, [[(0, rows, half)]] * visits, 0, rows)
    for below, out in enumerate((above_out, below_out)):
        segments, high = edge_segments(visits, rows, half, below)
        assemble(out, high, segments, below * depth, depth)


def tables(psf_index, psf_table, row_basis, col_basis, visits, rows):
    bases, taps = row_basis.shape
    half = taps // 2
    rim = (visits * rows, bases * edge_segments(visits, rows, half, 0)[1])
    return pl.pallas_call(
        functools.partial(table_kernel, visits, rows, half),
        out_shape=(
            held((2 * LANES, bases * LANES), BF16),
            held((2 * visits * rows, bases * rows), BF16),
            held(rim, BF16),
            held(rim, BF16),
        ),
        in_specs=[whole(pltpu.SMEM)] * 2 + [whole()] * 2,
        out_specs=(whole(),) * 4,
        compiler_params=LIMIT,
        name="tables",
    )(psf_index, psf_table.T, row_basis, col_basis)


def column_pass(windows, column_ref):
    return jnp.dot(
        jnp.concatenate(windows, axis=0), column_ref[...], preferred_element_type=F32
    )


def row_pass(layers, count, row_ref, pieces, bases):
    high = row_ref.shape[0] // (2 * len(pieces))
    for first in range(0, layers.shape[0] // count, 2):
        totals = []
        for v, parts in enumerate(pieces):
            sides = []
            for n in (first, first + 1):
                taken = [
                    layers[n * count + top : n * count + last, b * LANES : (b + 1) * LANES]
                    for b in range(bases)
                    for top, last in parts
                    if last > top
                ]
                sides.append(jnp.concatenate(taken, axis=0).astype(BF16))
            total = jnp.dot(
                row_ref[2 * v * high : 2 * (v + 1) * high, :],
                jnp.concatenate(sides, axis=1),
                preferred_element_type=F32,
            )
            totals.append(total[:high] + total[high:])
        yield first, totals


def convolve(make_group, shifted, column_ref, row_ref, pieces, put, blocks):
    count = shifted.shape[0]
    groups = shifted.shape[1] // LANES - 1
    bases = column_ref.shape[1] // LANES
    blocks = min(blocks, groups)
    made = [0]

    def columns_of(step):
        while made[0] <= blocks * (step + 1):
            g = made[0]
            shifted[:, g * LANES : (g + 1) * LANES] = make_group(g)
            made[0] += 1
        starts = [(blocks * step + n) * LANES for n in range(blocks)]
        return column_pass([shifted[:, at : at + 2 * LANES] for at in starts], column_ref)

    ahead = columns_of(0)
    for step in range(groups // blocks):
        layers = ahead
        if step + 1 < groups // blocks:
            ahead = columns_of(step + 1)
        for first, totals in row_pass(layers, count, row_ref, pieces, bases):
            put((blocks * step + first) * LANES, totals)


def own_kernel(visits, upper_ref, lower_ref, column_ref, row_ref, top_ref, bottom_ref, shifted):
    half_count, columns = upper_ref.shape
    depth = half_count // visits
    groups = columns // LANES
    low = lane_index((2 * half_count, LANES)) < SHIFT
    nothing = jnp.zeros((2 * half_count, LANES), F32)
    turned = {-1: nothing, groups: nothing}

    def turn(g):
        if g not in turned:
            lanes = slice(g * LANES, (g + 1) * LANES)
            value = jnp.concatenate([upper_ref[:, lanes], lower_ref[:, lanes]], axis=0)
            turned[g] = pltpu.roll(value.astype(F32), SHIFT, 1)
        return turned[g]

    def make_group(g):
        return jnp.where(low, turn(g - 1), turn(g)).astype(BF16)

    pieces = [
        [(place * half_count + v * depth, place * half_count + (v + 1) * depth) for place in (0, 1)]
        for v in range(visits)
    ]

    def put(start, totals):
        for v, total in enumerate(totals):
            lines = slice(v * depth, (v + 1) * depth)
            top_ref[lines, start : start + 2 * LANES] = total[:depth]
            bottom_ref[lines, start : start + 2 * LANES] = total[depth:]

    convolve(make_group, shifted, column_ref, row_ref, pieces, put, 4)


def own_part(upper, lower, column, own, visits):
    half_count, columns = upper.shape
    return pl.pallas_call(
        functools.partial(own_kernel, visits),
        out_shape=(held((half_count, columns), F32),) * 2,
        in_specs=[whole()] * 4,
        out_specs=(whole(),) * 2,
        scratch_shapes=[pltpu.VMEM((2 * half_count, columns + LANES), BF16)],
        compiler_params=LIMIT,
        cost_estimate=pl.CostEstimate(flops=10**9, bytes_accessed=10**7, transcendentals=0),
        name="own_rows",
    )(*kept(upper, lower, column, own))


def rim_kernel(visits, half, side_ref, edge_ref, column_ref, row_ref, part_ref, out_ref, shifted):
    edge, columns = edge_ref.shape
    rows = out_ref.shape[0] // visits
    width = out_ref.shape[1]
    groups = columns // LANES
    inner = width // LANES
    base = side_ref[0] * inner
    lane = lane_index((edge, LANES))

    def make_group(g):
        at = base + g
        lanes = pl.ds(pl.multiple_of(lax.rem(at, groups) * LANES, LANES), LANES)
        value = edge_ref[:, lanes]
        if g == 0:
            value = value.astype(F32)
            value = jnp.where(lane >= jnp.where(at == 0, SHIFT, 0), value, 0.0).astype(BF16)
        if g == inner:
            value = value.astype(F32)
            value = jnp.where(lane < jnp.where(at == groups, SHIFT, LANES), value, 0.0)
            value = value.astype(BF16)
        return value

    main = half // 8 * 8
    pieces = [[(v * main, (v + 1) * main), (visits * main, edge)] for v in range(visits)]

    def put(start, totals):
        source = pl.ds(pl.multiple_of(base * LANES + start, 2 * LANES), 2 * LANES)
        for v, total in enumerate(totals):
            lines = slice(v * rows, (v + 1) * rows)
            value = (total + part_ref[lines, source]).astype(out_ref.dtype)
            out_ref[lines, start : start + 2 * LANES] = value

    convolve(make_group, shifted, column_ref, row_ref, pieces, put, 8)


def rim_part(side, edge, column, table, part, visits, half):
    count, columns = part.shape
    width = columns // 2
    return pl.pallas_call(
        functools.partial(rim_kernel, visits, half),
        out_shape=held((count, width), BF16),
        in_specs=[whole(pltpu.SMEM)] + [whole()] * 4,
        out_specs=whole(),
        scratch_shapes=[pltpu.VMEM((edge.shape[0], width + LANES), BF16)],
        compiler_params=LIMIT,
    )(side, *kept(edge, column, table, part))


def norm_kernel(visits, bands, *refs):
    flag_refs = refs[:2]
    weight_ref, inverse_ref, count_ref = refs[2:]
    rows, width = inverse_ref.shape
    count = visits * rows
    high = min(16, rows // bands)
    members = [(side, v) for side in range(2) for v in range(visits)]
    levels = {}
    for side in range(2):
        found = flag_refs[side][count:, :LANES].astype(F32)
        for v in range(visits):
            for b in range(bands):
                spots = [(k * bands + b) * visits + v for k in range(3)]
                parts = [found[spot : spot + 1] for spot in spots]
                level = (parts[0] + parts[1]) + parts[2]
                levels[side, v, b] = jnp.broadcast_to(level, (high, LANES))
    count_ref[...] = jnp.zeros_like(count_ref)

    def body(step, carry):
        lanes = pl.ds(pl.multiple_of(step * LANES, LANES), LANES)
        for row in range(0, rows, high):
            denom = PRIOR_WEIGHT
            for m, (side, v) in enumerate(members):
                flag = flag_refs[side][v * rows + row : v * rows + row + high, lanes].astype(F32)
                weight = flag * levels[side, v, row // (rows // bands)]
                weight_ref[m * rows + row : m * rows + row + high, lanes] = weight
                count_ref[m * 8 : (m + 1) * 8, :] += folded(flag)
                denom = denom + weight
            inverse_ref[row : row + high, lanes] = 1.0 / denom
        return carry

    lax.fori_loop(0, width // LANES, body, 0, unroll=4)


def folded(value):
    total = value[:8]
    for start in range(8, value.shape[0], 8):
        total = total + value[start : start + 8]
    return total


def norms(own_flags, other_flags, visits, bands, rows):
    width = own_flags.shape[1]
    members = 2 * visits
    return pl.pallas_call(
        functools.partial(norm_kernel, visits, bands),
        out_shape=(
            held((members * rows, width), F32),
            held((rows, width), F32),
            held((members * 8, LANES), F32),
        ),
        in_specs=[whole()] * 2,
        out_specs=(whole(),) * 3,
        compiler_params=LIMIT,
        name="norms",
    )(*kept(own_flags, other_flags))


def residual_kernel(visits, first, last, side_ref, *refs):
    value_refs = refs[:2]
    weight_ref, inverse_ref = refs[2:4]
    if last:
        so_far_ref, count_ref, factor_ref, sums_ref, chi_ref = refs[4:]
        chi_ref[...] = so_far_ref[...]
    else:
        factor_ref, chi_ref = refs[4:]
        chi_ref[...] = jnp.zeros_like(chi_ref)
    depth = value_refs[0].shape[0] // visits
    rows, width = inverse_ref.shape
    high = min(16, depth)
    members = [(side, v) for side in range(2) for v in range(visits)]

    def body(step, carry):
        lanes = pl.ds(pl.multiple_of(step * LANES, LANES), LANES)
        for row in range(0, depth, high):
            values, weights = [], []
            numer = None
            for m, (side, v) in enumerate(members):
                at = slice(v * depth + row, v * depth + row + high)
                value = value_refs[side][at, lanes].astype(F32)
                at = m * rows + first + row
                weight = weight_ref[at : at + high, lanes]
                values.append(value)
                weights.append(weight)
                numer = weight * value if numer is None else numer + weight * value
            mean = numer * inverse_ref[first + row : first + row + high, lanes]
            for m in range(len(members)):
                residual = values[m] - mean
                term = weights[m] * (residual * residual)
                chi_ref[m * 8 : (m + 1) * 8, :] += folded(term)
                target = slice(m * depth + row, m * depth + row + high)
                factor_ref[target, lanes] = weights[m] / (CLIP_LEVEL + term)
        return carry

    lax.fori_loop(0, width // LANES, body, 0, unroll=4)
    if not last:
        return
    for k, ref in enumerate((chi_ref, count_ref)):
        lines = [
            jnp.sum(ref[m * 8 : (m + 1) * 8, :], axis=0, keepdims=True)
            for m in range(len(members))
        ]
        total = jnp.concatenate(lines, axis=0)
        sums_ref[k] = jnp.where(side_ref[0] == 0, total, pltpu.roll(total, visits, 0))


def residual_pass(side, values, weights, inverse, visits, first, *ending):
    count, width = values[0].shape
    members = 2 * visits
    last = len(ending) > 0
    chi = (members * 8, LANES)
    return pl.pallas_call(
        functools.partial(residual_kernel, visits, first, last),
        out_shape=(
            held((2 * count, width), F32),
            held((2, members, LANES) if last else chi, F32),
        ),
        in_specs=[whole(pltpu.SMEM)] + [whole()] * (4 + len(ending)),
        out_specs=(whole(), whole()),
        scratch_shapes=[pltpu.VMEM(chi, F32)] * last,
        compiler_params=LIMIT,
        name="residual_last" if last else "residual",
    )(side, *kept(*values, weights, inverse, *ending))


def final_kernel(visits, side_ref, sums_ref, *refs):
    parts = [refs[:3], refs[3:6]]
    out_ref, chi_ref, done, mean, sent = refs[6:]
    rows, width = done.shape
    high = min(16, rows // 2)
    sums = [
        jnp.where(side_ref[0] == 0, sums_ref[k], pltpu.roll(sums_ref[k], visits, 0))
        for k in range(2)
    ]
    chi = jnp.sum(sums[0], axis=1, keepdims=True) / jnp.sum(sums[1], axis=1, keepdims=True)
    scale = CLIP_LEVEL / (CHI_OFFSET + chi)
    for v in range(visits):
        mean[v] = chi[v, 0]
    chi_copy = pltpu.make_async_copy(mean, chi_ref, sent.at[1])
    chi_copy.start()
    scales = [jnp.broadcast_to(scale[m : m + 1], (high, LANES)) for m in range(2 * visits)]
    depth = rows // 2
    copies = []
    for k, part in enumerate(parts):
        for lane in range(0, width, LANES):
            lanes = slice(lane, lane + LANES)
            for row in range(0, depth, high):
                numer = denom = None
                for m in range(2 * visits):
                    at = (m % visits) * depth + row
                    value = part[m // visits][at : at + high, lanes].astype(F32)
                    at = m * depth + row
                    revised = part[2][at : at + high, lanes] * scales[m]
                    numer = revised * value if numer is None else numer + revised * value
                    denom = revised if denom is None else denom + revised
                at = k * depth + row
                done[at : at + high, lanes] = numer / (denom + PRIOR_WEIGHT)
        lines = slice(k * depth, (k + 1) * depth)
        copies.append(
            pltpu.make_async_copy(done.at[lines], out_ref.at[lines], sent.at[2 * k])
        )
        copies[k].start()
    chi_copy.wait()
    for copy in copies:
        copy.wait()


def final_pass(side, sums, upper, lower, visits):
    count, width = upper[0].shape
    rows = 2 * count // visits
    return pl.pallas_call(
        functools.partial(final_kernel, visits),
        out_shape=(
            jax.ShapeDtypeStruct((rows, width), F32),
            jax.ShapeDtypeStruct((visits,), F32),
        ),
        in_specs=[whole(pltpu.SMEM)] + [whole()] * 7,
        out_specs=(pl.BlockSpec(memory_space=pl.ANY),) * 2,
        scratch_shapes=[
            pltpu.VMEM((rows, width), F32),
            pltpu.SMEM((visits,), F32),
            pltpu.SemaphoreType.DMA((3,)),
        ],
        compiler_params=LIMIT,
        name="final",
    )(side, *kept(sums, *upper, *lower))


def partners(strips, step, crossing):
    turn = 1 if crossing else 0
    return [(2 * i + v, 2 * (i ^ step) + (v ^ turn)) for i in range(strips) for v in (0, 1)]


def per_device(warps, badbits, coverage, variance, psf_index, psf_table, row_basis, col_basis):
    visits, rows, columns = warps.shape
    half = row_basis.shape[1] // 2
    strips = lax.axis_size("sky")
    up = [(i, i + 1) for i in range(strips - 1)]
    down = [(j, i) for i, j in up]
    swap = [(0, 1), (1, 0)]
    side = lax.axis_index("visit").astype(jnp.int32).reshape(1)

    last, lower = pack_rows(warps, half, False)
    before = lax.ppermute(last, "sky", up)
    send_weight, own_weight = pixel_weights(badbits, coverage, variance, side)
    other_weight = lax.ppermute(send_weight, "visit", swap)
    column, own, above, below = tables(psf_index, psf_table, row_basis, col_basis, visits, rows)
    leading, upper = pack_rows(warps, half, True, send_weight)
    after = lax.ppermute(leading, "sky", down)
    top, bottom = own_part(
        upper.reshape(-1, columns), lower.reshape(-1, columns), column, own, visits
    )
    send_top = rim_part(1 - side, before, column, above, top, visits, half)
    other_top = lax.ppermute(send_top, "visit", swap)
    own_top = rim_part(side, before, column, above, top, visits, half)
    weights, inverse, counts = norms(own_weight, other_weight, visits, coverage.shape[1], rows)
    top_factors, chi = residual_pass(side, (own_top, other_top), weights, inverse, visits, 0)
    send_value = rim_part(1 - side, after, column, below, bottom, visits, half)
    other_value = lax.ppermute(send_value, "visit", swap)
    own_value = rim_part(side, after, column, below, bottom, visits, half)
    factors, sums = residual_pass(
        side, (own_value, other_value), weights, inverse, visits, rows // 2, chi, counts
    )
    step = 1
    while step < strips:
        crossing = lax.ppermute(sums, ("sky", "visit"), partners(strips, step, True))
        if 4 * step <= strips:
            second = lax.ppermute(sums, ("sky", "visit"), partners(strips, 2 * step, True))
            third = lax.ppermute(sums, ("sky", "visit"), partners(strips, 3 * step, False))
            sums = (sums + crossing) + (second + third)
            step *= 4
        else:
            sums = sums + crossing
            step *= 2
    sums = sums + lax.ppermute(sums, "visit", swap)
    upper = (own_top, other_top, top_factors)
    return final_pass(side, sums, upper, (own_value, other_value, factors), visits)


def solution(mesh):
    placed = (
        P(("tract", "visit"), "sky", None),
        P(("tract", "visit"), "sky", None),
        P(("tract", "visit"), "sky"),
        P(("tract", "visit"), "sky"),
        P(("tract", "visit")),
        P(),
        P(),
        P(),
    )
    return jax.shard_map(
        per_device,
        mesh=mesh,
        in_specs=placed,
        out_specs=(P(("tract", "sky"), "visit"), P(("tract", "visit"))),
        check_vma=False,
    )
```
